32 devices in a mesh: dp: 4 (over y, x), seq: 8 (over z, core).
Axes of the slice: x: 2, y: 2, z: 4, core: 2. Of those that a mesh axis runs over, the one named last changes fastest.
Arguments:
- hidden_in: bfloat16 [8, 8192, 768], P('dp', 'seq'), may hold values from -6 to 6
- lengths: int32 [8], P('dp'), may hold values from 2048 to 8192, as said below
- w_in: bfloat16 [768, 3352], P(('dp', 'seq')), may hold values from -0.21875 to 0.21875
- conv_w: bfloat16 [4, 1792], P(None, ('dp', 'seq')), may hold values from -3 to 3
- conv_b: bfloat16 [1792], P(('dp', 'seq')), may hold values from -3 to 3
- g_norm: bfloat16 [768], P(('dp', 'seq')), may hold values from 0.5 to 1.5
- g_gate: bfloat16 [1536], P(('dp', 'seq')), may hold values from 0.5 to 1.5
- w_out: bfloat16 [1536, 768], P(None, ('dp', 'seq')), may hold values from -0.15625 to 0.15625
- a_log: float32 [24], replicated, may hold values from -12 to 0
- dt_bias: float32 [24], replicated, may hold values from -12 to 0
- d_skip: float32 [24], replicated, may hold values from 0.5 to 1.5
- out_cotangent: bfloat16 [8, 8192, 768], P('dp', 'seq'), may hold values from -6 to 6
Outputs:
- block_out: bfloat16 [8, 8192, 768], P('dp', 'seq')
- input_grad: float32 [8, 8192, 768], P('dp', 'seq')
- w_in_grad: float32 [768, 3352], P(('dp', 'seq'))
- conv_w_grad: float32 [4, 1792], P(None, ('dp', 'seq'))
- conv_b_grad: float32 [1792], P(('dp', 'seq'))
- g_norm_grad: float32 [768], P(('dp', 'seq'))
- g_gate_grad: float32 [1536], P(('dp', 'seq'))
- w_out_grad: float32 [1536, 768], P(None, ('dp', 'seq'))
- a_log_grad: float32 [24], replicated
- dt_bias_grad: float32 [24], replicated
- d_skip_grad: float32 [24], replicated
The draws below stay inside these ranges and needn't reach their ends.
Inputs may be any that keep to these rules, and one draw needn't show every extreme that they name: Slot b holds its first lengths[b] tokens, the rest is padding; some slot is full.
All inputs are finite; a program needn't handle non-finite values.
Results may differ from the reference program's by a relative error of at most 0.0068.
Values may be sent and summed in bfloat16 or wider, within the bound.
No kernel may reach another device: no remote copies, remote signals or barrier semaphores. Data moves between devices by JAX's collectives and lax.ppermute only.
A program may use at most 512 MiB of HBM per device.

```python
import jax
import jax.numpy as jnp
from jax import lax

D = 768
HEADS = 24
HEADDIM = 64
STATE = 128
CONV = 4
GROUP = 256
DI = 1536
CONV_CH = 1792
PROJ = 3352
SLOTS = 8
LENGTH = 8192


def head_rates(key):
    pick, spread, jitter = jax.random.split(jax.random.fold_in(key, 11), 3)
    slow_part = 0.5
    slow = jax.random.uniform(pick, (HEADS,)) < slow_part
    fraction = jax.random.uniform(spread, (HEADS,))
    slow_low = 0.1 / LENGTH
    slow_high = 1.2 / LENGTH
    fast_high = 0.03
    decay_rate = jnp.where(slow, slow_low * (slow_high / slow_low) ** fraction, slow_high * (fast_high / slow_high) ** fraction)
    step_base = 0.5 * jnp.sqrt(decay_rate) * jnp.exp(jax.random.uniform(jitter, (HEADS,), minval=-0.3, maxval=0.3))
    return (decay_rate, step_base)


def draw_a_log(key, part):
    decay_rate, step_base = head_rates(key)
    return jnp.log(decay_rate / step_base).astype(jnp.float32)


def draw_dt_bias(key, part):
    decay_rate, step_base = head_rates(key)
    return jnp.log(jnp.expm1(step_base)).astype(jnp.float32)


def draw_lengths(key, part):
    first, second = jax.random.split(jax.random.fold_in(key, 5))
    drawn = jax.random.randint(first, (SLOTS,), LENGTH // 4, LENGTH + 1)
    longest = jax.random.randint(second, (), 0, SLOTS)
    return jnp.where(jnp.arange(SLOTS) == longest, LENGTH, drawn).astype(jnp.int32)


def shard_levels(own_key, extent, shards, smallest, high):
    gain, own = 1.0, jax.random.fold_in(own_key, 6)
    for axis_at, parts in shards:
        heights = jnp.exp(jax.random.uniform(jax.random.fold_in(own, axis_at), (parts,), jnp.float32, smallest / len(shards), high / len(shards)))
        gain = gain * jnp.repeat(heights, extent[axis_at] // parts).reshape([-1 if axis == axis_at else 1 for axis in range(len(extent))])
    return gain


def centred(rng, shape, deviation, bound, cuts=(), kind=jnp.bfloat16):
    values = deviation * jax.random.normal(rng, shape, jnp.float32)
    if cuts:
        values = values * shard_levels(rng, shape, cuts, -0.22, 0.18)
    return jnp.clip(values, -bound, bound).astype(kind)


def setup_inputs(seed: int = 0) -> dict:
    streams_of = jax.random.split(jax.random.key(seed), 13)
    return {
        "hidden_in": centred(streams_of[0], (SLOTS, LENGTH, D), 1.0, 6.0, ((0, 4), (1, 8))),
        "lengths": draw_lengths(jax.random.fold_in(streams_of[12], 71), 0),
        "w_in": centred(streams_of[2], (D, PROJ), D ** -0.5, 0.21875, ((0, 32),)),
        "conv_w": centred(streams_of[3], (CONV, CONV_CH), CONV ** -0.5, 3.0, ((1, 32),)),
        "conv_b": centred(streams_of[4], (CONV_CH,), 0.5, 3.0, ((0, 32),)),
        "g_norm": jnp.clip(1.0 + 0.1 * jax.random.normal(streams_of[5], (D,), jnp.float32), 0.5, 1.5).astype(jnp.bfloat16),
        "g_gate": jnp.clip(1.0 + 0.1 * jax.random.normal(streams_of[6], (DI,), jnp.float32), 0.5, 1.5).astype(jnp.bfloat16),
        "w_out": centred(streams_of[7], (DI, D), DI ** -0.5, 0.15625, ((1, 32),)),
        "a_log": draw_a_log(jax.random.fold_in(streams_of[12], 71), 0),
        "dt_bias": draw_dt_bias(jax.random.fold_in(streams_of[12], 71), 0),
        "d_skip": jnp.clip(jax.random.uniform(streams_of[10], (HEADS,), jnp.float32, 0.5, 1.5), 0.5, 1.5),
        "out_cotangent": centred(streams_of[11], (SLOTS, LENGTH, D), 1.0, 6.0, ((0, 4), (1, 8))),
    }


EPSILON = 1e-05
HIGHEST = lax.Precision.HIGHEST

@jax.custom_vjp
def low(v):
    return lax.optimization_barrier(v.astype(jnp.bfloat16)).astype(jnp.float32)

@jax.custom_vjp
def low_back(v):
    return v

def low_keep(v):
    return (low(v), None)

def low_pass(kept, grad):
    return (grad,)

def back_keep(v):
    return (v, None)

def back_low(kept, grad):
    return (low(grad),)
low.defvjp(low_keep, low_pass)
low_back.defvjp(back_keep, back_low)

def group_scan(carry, block):
    x_heads, b_proj, c_proj, step_size, arate = block
    log_decay = jnp.cumsum(arate, axis=0)
    index = jnp.arange(GROUP, dtype=jnp.int32)
    causal = (index[:, None] >= index[None, :])[:, :, None]
    spread = log_decay[:, None, :] - log_decay[None, :, :]
    decay_mat = jnp.exp(jnp.where(causal, spread, -jnp.inf))
    inner_cb = jnp.dot(c_proj, b_proj.T, precision=HIGHEST)
    mixing = inner_cb[:, :, None] * decay_mat * step_size[None, :, :]
    local_out = jnp.einsum('tkh,khp->thp', mixing, x_heads, precision=HIGHEST)
    cross_out = jnp.einsum('tn,hpn->thp', c_proj, carry, precision=HIGHEST) * jnp.exp(log_decay)[:, :, None]
    to_end = jnp.exp(log_decay[-1][None, :] - log_decay) * step_size
    state = jnp.exp(log_decay[-1])[:, None, None] * carry + jnp.einsum('kh,khp,kn->hpn', to_end, x_heads, b_proj, precision=HIGHEST)
    return (state, local_out + cross_out)

def layer(hidden, w_in, conv_w, conv_b, g_norm, g_gate, w_out, a_log, dt_bias, d_skip, keep):
    inv_rms = lax.rsqrt(lax.optimization_barrier(jnp.mean(hidden * hidden, axis=-1, keepdims=True)) + EPSILON)
    normed = low(hidden * inv_rms * g_norm)
    proj = low_back(jnp.dot(normed, w_in, precision=HIGHEST))
    gate_pre = proj[:, :DI]
    conv_in = low(proj[:, DI:DI + CONV_CH])
    step_raw = proj[:, DI + CONV_CH:]
    padded = jnp.concatenate([jnp.zeros((CONV - 1, CONV_CH), jnp.float32), conv_in], axis=0)
    conv_pre = conv_b + padded[0:LENGTH] * conv_w[0]
    for tap in range(1, CONV):
        conv_pre = conv_pre + padded[tap:tap + LENGTH] * conv_w[tap]
    act = jax.nn.silu(conv_pre)
    x_heads = act[:, :DI].reshape(LENGTH, HEADS, HEADDIM)
    b_proj = act[:, DI:DI + STATE]
    c_proj = act[:, DI + STATE:]
    step_size = jax.nn.softplus(step_raw + dt_bias)
    arate = -jnp.exp(a_log) * step_size
    count = LENGTH // GROUP
    blocks = (x_heads.reshape(count, GROUP, HEADS, HEADDIM), b_proj.reshape(count, GROUP, STATE), c_proj.reshape(count, GROUP, STATE), step_size.reshape(count, GROUP, HEADS), arate.reshape(count, GROUP, HEADS))
    start = jnp.zeros((HEADS, HEADDIM, STATE), jnp.float32)
    _, scan_out = lax.scan(jax.checkpoint(group_scan), start, blocks)
    mixed = scan_out.reshape(LENGTH, HEADS, HEADDIM) + d_skip[:, None] * x_heads
    gated = mixed.reshape(LENGTH, DI) * jax.nn.silu(gate_pre)
    inv_gate = lax.rsqrt(lax.optimization_barrier(jnp.mean(gated * gated, axis=-1, keepdims=True)) + EPSILON)
    gated_norm = low(gated * inv_gate * g_gate)
    branch = jnp.dot(gated_norm, w_out, precision=HIGHEST)
    return hidden + keep[:, None] * branch

def reference(hidden_in, lengths, w_in, conv_w, conv_b, g_norm, g_gate, w_out, a_log, dt_bias, d_skip, out_cotangent):
    params = tuple((p.astype(jnp.float32) for p in (w_in, conv_w, conv_b, g_norm, g_gate, w_out, a_log, dt_bias, d_skip)))
    place = jnp.arange(LENGTH, dtype=jnp.int32)

    def per_slot(total, item):
        hidden_row, length, cotangent_row = item
        keep = (place < length).astype(jnp.float32)

        def forward(hidden, *weights):
            return layer(hidden, *weights, keep)
        result, pull = jax.vjp(forward, hidden_row.astype(jnp.float32), *params)
        grads = pull(cotangent_row.astype(jnp.float32))
        total = tuple((a + b for a, b in zip(total, grads[1:])))
        return (total, (result.astype(jnp.bfloat16), grads[0]))
    zeros = tuple((jnp.zeros_like(p) for p in params))
    total, (block_out, input_grad) = lax.scan(per_slot, zeros, (hidden_in, lengths, out_cotangent))
    return (block_out, input_grad, total[0], total[1], total[2], total[3], total[4], total[5], total[6], total[7], total[8])
```

```python
import functools

import jax
import jax.numpy as jnp
from jax import lax
from jax.experimental import pallas as pl
from jax.experimental.pallas import tpu as pltpu
from jax.sharding import PartitionSpec as P

D = 768
HEADS = 24
HEADDIM = 64
STATE = 128
CONV = 4
DI = 1536
CONV_CH = 1792
PROJ = 3352
T = 128
PAIRS = HEADS // 2
LANES = 128
EPSILON = 1e-05
MASKED = -1e30
F32 = jnp.float32
BF16 = jnp.bfloat16
NN = (((1,), (0,)), ((), ()))
NT = (((1,), (1,)), ((), ()))


def mm(a, b, dims=NN):
    return lax.dot_general(a, b, dims, preferred_element_type=F32)


def split(v):
    high = v.astype(BF16)
    return high, (v - high.astype(F32)).astype(BF16)


def mm3(a, b, dims=NN):
    return mm(a[0], b[0], dims) + (mm(a[0], b[1], dims) + mm(a[1], b[0], dims))


def left_half(rows):
    return lax.broadcasted_iota(jnp.int32, (rows, LANES), 1) < HEADDIM


def spread(values, pair, left):
    return jnp.where(
        left, values[:, 2 * pair : 2 * pair + 1], values[:, 2 * pair + 1 : 2 * pair + 2]
    )


def cols(j):
    return slice(j * LANES, (j + 1) * LANES)


def running(v, reverse):
    row = lax.broadcasted_iota(jnp.int32, v.shape, 0)
    hop = 1
    while hop < T:
        moved = pltpu.roll(v, T - hop if reverse else hop, 0)
        inside = row < T - hop if reverse else row >= hop
        v = v + jnp.where(inside, moved, 0.0)
        hop *= 2
    return v


def fold(v):
    return jnp.sum(v.reshape(T // 8, 8, v.shape[-1]), axis=0)


def two_heads(high, low, left):
    zero = jnp.zeros_like(high)
    top = jnp.concatenate([jnp.where(left, high, zero), jnp.where(left, low, zero)], axis=1)
    bottom = jnp.concatenate([jnp.where(left, zero, high), jnp.where(left, zero, low)], axis=1)
    return jnp.concatenate([top, bottom], axis=0)


def sigmoid(v):
    return 1.0 / (1.0 + jnp.exp(-v))


def convolve(window, taps_ref, at, first):
    total = taps_ref[CONV : CONV + 1, at]
    for tap in range(CONV):
        total = total + window[first + tap : first + tap + T, at] * taps_ref[tap : tap + 1, at]
    return total


def states_kernel(
    conv_ref, halo_ref, dt_ref, taps_ref, heads_ref,
    act_ref, log_ref, step_ref, aux_ref, enter_ref, final_ref, total_ref,
    window, state, before,
):
    c = pl.program_id(1)

    @pl.when(c == 0)
    def _():
        window[0:8, :] = halo_ref[0].astype(F32)
        state[...] = jnp.zeros_like(state)
        before[...] = jnp.zeros_like(before)

    window[8 : 8 + T, :] = conv_ref[0].astype(F32)
    for j in range(CONV_CH // LANES):
        pre = convolve(window, taps_ref, cols(j), 8 - (CONV - 1))
        act_ref[0, :, cols(j)] = pre * sigmoid(pre)
    window[0:8, :] = window[T : T + 8, :]

    step = jax.nn.softplus(dt_ref[0] + heads_ref[0:1, :])
    log = running(step * heads_ref[1:2, :], False)
    end = log[T - 1 : T, :]
    step_ref[0] = step
    log_ref[0] = log
    weight = jnp.exp(end - log) * step
    decay = jnp.exp(end)
    left = left_half(T)
    aux_ref[0, 0] = jnp.concatenate([before[0:1, :], end, jnp.zeros((6, LANES), F32)], axis=0)
    before[0:1, :] = before[0:1, :] + end
    b_turned = split(act_ref[0, :, DI : DI + STATE].T)
    for j in range(PAIRS):
        prior = state[:, cols(j)]
        enter_ref[0, 0, :, cols(j)] = prior
        fed = split(act_ref[0, :, cols(j)] * spread(weight, j, left))
        state[:, cols(j)] = prior * spread(decay, j, left[0:1]) + mm3(b_turned, fed)

    @pl.when(c == pl.num_programs(1) - 1)
    def _():
        final_ref[0] = state[...]
        total_ref[0] = before[...]


def local_kernel(act_ref, log_ref, step_ref, enter_ref, out_ref):
    log = log_ref[0]
    log_turned = log.T
    step = step_ref[0]
    grown = jnp.exp(log)
    left = left_half(T)
    row = lax.broadcasted_iota(jnp.int32, (T, T), 0)
    col = lax.broadcasted_iota(jnp.int32, (T, T), 1)
    causal = row >= col
    b_pair = split(act_ref[0, :, DI : DI + STATE])
    c_pair = split(act_ref[0, :, DI + STATE :])
    inner = mm3(c_pair, b_pair, NT)
    for j in range(PAIRS):
        fed = split(act_ref[0, :, cols(j)] * spread(step, j, left))
        rhs = two_heads(fed[0], fed[1], left)
        mats = []
        for head in (2 * j, 2 * j + 1):
            gap = log[:, head : head + 1] - log_turned[head : head + 1, :]
            mats.append(inner * jnp.exp(jnp.where(causal, gap, MASKED)))
        mixing = split(jnp.concatenate(mats, axis=1))
        wide = mm(mixing[0], rhs)
        out = wide[:, :LANES] + (wide[:, LANES:] + mm(mixing[1], rhs[:, :LANES]))
        crossed = mm3(c_pair, split(enter_ref[0, 0, :, cols(j)]))
        out_ref[0, :, cols(j)] = out + spread(grown, j, left) * crossed


def gate_kernel(
    act_ref, log_ref, aux_ref, local_ref, gate_ref, ng_ref, start_ref, rows_ref, sel_ref,
    normed_ref, mixed_grad_ref, gate_grad_ref, lg_ref, enter_ref, final_ref, sums_ref,
    scan_s, gated_s, adj, q_high, q_low,
):
    s, c = pl.program_id(0), pl.program_id(1)

    @pl.when(c == 0)
    def _():
        adj[...] = jnp.zeros_like(adj)

    @pl.when((s == 0) & (c == 0))
    def _():
        sums_ref[...] = jnp.zeros_like(sums_ref)

    log = log_ref[0]
    before = aux_ref[0, 0, 0:1, :]
    end = aux_ref[0, 0, 1:2, :]
    left = left_half(T)
    since = jnp.exp(before + log)
    grown = jnp.exp(log)
    decay = jnp.exp(end)
    c_rows = act_ref[0, :, DI + STATE :]
    c_pair = split(c_rows)
    c_turned = split(c_rows.T)
    squares = jnp.zeros((T, LANES), F32)
    products = jnp.zeros((T, LANES), F32)
    for j in range(PAIRS):
        at = cols(j)
        crossed = mm3(c_pair, split(start_ref[0, :, at]))
        scan = local_ref[0, :, at] + spread(since, j, left) * crossed
        gate = gate_ref[0, :, at]
        mixed = scan + rows_ref[1:2, at] * act_ref[0, :, at]
        gated = mixed * (gate * sigmoid(gate))
        scan_s[:, at] = scan
        gated_s[:, at] = gated
        squares = squares + gated * gated
        products = products + ng_ref[0, :, at] * rows_ref[0:1, at] * gated
    inv = lax.rsqrt(jnp.sum(squares, axis=-1, keepdims=True) / DI + EPSILON)
    mean = jnp.sum(products, axis=-1, keepdims=True) / DI
    pull = inv * inv * mean
    for j in range(PAIRS):
        at = cols(j)
        scan = scan_s[:, at]
        gated = gated_s[:, at]
        gate = gate_ref[0, :, at]
        x = act_ref[0, :, at]
        gain = rows_ref[0:1, at]
        ng = ng_ref[0, :, at]
        sig = sigmoid(gate)
        unit = gated * inv
        normed_ref[0, :, at] = (unit * gain).astype(BF16)
        sums_ref[0:8, at] = sums_ref[0:8, at] + fold(ng * unit)
        gated_grad = inv * (ng * gain - gated * pull)
        mixed = scan + rows_ref[1:2, at] * x
        mixed_grad = gated_grad * (gate * sig)
        mixed_grad_ref[0, :, at] = mixed_grad
        gate_grad_ref[0, :, at] = (
            gated_grad * mixed * sig * (1.0 + gate * (1.0 - sig))
        ).astype(BF16)
        sums_ref[8:16, at] = sums_ref[8:16, at] + fold(x * mixed_grad)
        q = split(mixed_grad * scan)
        q_high[:, at] = q[0]
        q_low[:, at] = q[1]
        prior = adj[:, at]
        enter_ref[0, 0, :, at] = prior
        fed = split(mixed_grad * spread(grown, j, left))
        adj[:, at] = prior * spread(decay, j, left[0:1]) + mm3(c_turned, fed)
    lg_ref[0] = mm(q_high[...], sel_ref[...]) + mm(q_low[...], sel_ref[...])

    @pl.when(c == pl.num_programs(1) - 1)
    def _():
        final_ref[0] = adj[...]


def adjoint_kernel(
    act_ref, log_ref, step_ref, aux_ref, grad_ref, enter_ref, start_ref, adj_ref,
    xadj_ref, bc_ref,
):
    log = log_ref[0]
    log_turned = log.T
    step = step_ref[0]
    before = aux_ref[0, 0, 0:1, :]
    end = aux_ref[0, 0, 1:2, :]
    left = left_half(T)
    row = lax.broadcasted_iota(jnp.int32, (T, T), 0)
    col = lax.broadcasted_iota(jnp.int32, (T, T), 1)
    later = col >= row
    b_rows = act_ref[0, :, DI : DI + STATE]
    c_rows = act_ref[0, :, DI + STATE :]
    b_pair = split(b_rows)
    c_pair = split(c_rows)
    inner = mm3(b_pair, c_pair, NT)
    grown = jnp.exp(log)
    to_end = jnp.exp(end - log)
    reach = jnp.exp(before)
    weighted = jnp.zeros((T, T), F32)
    b_total = jnp.zeros((T, STATE), F32)
    c_total = jnp.zeros((T, STATE), F32)
    for j in range(PAIRS):
        at = cols(j)
        grad = grad_ref[0, :, at]
        fed = act_ref[0, :, at] * spread(step, j, left)
        high, low = split(grad)
        rhs = two_heads(high, low, left)
        decays = []
        for head in (2 * j, 2 * j + 1):
            gap = log_turned[head : head + 1, :] - log[:, head : head + 1]
            decays.append(jnp.exp(jnp.where(later, gap, MASKED)))
        mixing = split(jnp.concatenate([inner * decays[0], inner * decays[1]], axis=1))
        wide = mm(mixing[0], rhs)
        out = wide[:, :LANES] + (wide[:, LANES:] + mm(mixing[1], rhs[:, :LANES]))
        short = fed.astype(BF16)
        zero = jnp.zeros_like(short)
        stacked = jnp.concatenate(
            [jnp.where(left, short, zero), jnp.where(left, zero, short)], axis=0
        )
        dots = mm(stacked, high, NT)
        weighted = weighted + (decays[0] * dots[:T] + decays[1] * dots[T:])
        adj = split(adj_ref[0, 0, :, at])
        reached = spread(to_end, j, left)
        xadj_ref[0, :, at] = out + reached * mm3(b_pair, adj)
        b_total = b_total + mm((fed * reached).astype(BF16), adj[0], NT)
        entering = enter_ref[0, 0, :, at] + spread(reach, j, left[0:1]) * start_ref[0, :, at]
        c_total = c_total + mm3(split(grad * spread(grown, j, left)), split(entering), NT)
    bc_ref[0, :, 0:STATE] = b_total + mm(weighted.astype(BF16), c_pair[0])
    bc_ref[0, :, STATE:] = c_total + mm(weighted.T.astype(BF16), b_pair[0])


def finish_kernel(
    act_ref, log_ref, step_ref, aux_ref, total_ref, grad_ref, xadj_ref, bc_ref, lg_ref,
    end_ref, conv_ref, prev_ref, halo_ref, dt_ref, tail_ref, taps_ref, heads_ref, rows_ref,
    sel_ref,
    out_ref, head_ref, last_ref, sums_ref, head_sums_ref,
    window, pre_s, q_high, q_low, carry,
):
    s, c = pl.program_id(0), pl.program_id(1)
    first = c == pl.num_programs(1) - 1

    @pl.when(c == 0)
    def _():
        pre_s[T : T + 8, :] = jnp.zeros((8, CONV_CH), F32)
        carry[...] = tail_ref[0]

    @pl.when((s == 0) & (c == 0))
    def _():
        sums_ref[...] = jnp.zeros_like(sums_ref)
        head_sums_ref[...] = jnp.zeros_like(head_sums_ref)

    @pl.when(first)
    def _():
        window[8:16, :] = halo_ref[0].astype(F32)

    @pl.when(jnp.logical_not(first))
    def _():
        window[8:16, :] = prev_ref[0].astype(F32)[8:16, :]

    window[16 : 16 + T, :] = conv_ref[0].astype(F32)
    log = log_ref[0]
    step = step_ref[0]
    before = aux_ref[0, 0, 0:1, :]
    end = aux_ref[0, 0, 1:2, :]
    left = left_half(T)
    remain = jnp.exp((total_ref[0, 0:1, :] - before - end) + (end - log))
    b_pair = split(act_ref[0, :, DI : DI + STATE])
    b_total = bc_ref[0, :, 0:STATE]

    def through(at, act_grad):
        pre = convolve(window, taps_ref, at, 16 - (CONV - 1))
        sig = sigmoid(pre)
        pre_grad = act_grad * sig * (1.0 + pre * (1.0 - sig))
        pre_s[0:T, at] = pre_grad
        for tap in range(CONV):
            shifted = window[16 - (CONV - 1) + tap : 16 - (CONV - 1) + tap + T, at]
            rows = slice(8 * tap, 8 * tap + 8)
            sums_ref[rows, at] = sums_ref[rows, at] + fold(pre_grad * shifted)
        sums_ref[32:40, at] = sums_ref[32:40, at] + fold(pre_grad)
        into = pre_grad * taps_ref[CONV - 1 : CONV, at]
        for tap in range(CONV - 1):
            ahead = CONV - 1 - tap
            into = into + pre_s[ahead : ahead + T, at] * taps_ref[tap : tap + 1, at]
        out_ref[0, :, at] = into.astype(BF16)

        @pl.when(c == 0)
        def _():
            last_ref[0, :, at] = into[T - 8 :, :]

        pre_s[T : T + 8, at] = pre_grad[0:8, :]

        @pl.when(first)
        def _():
            head_ref[0, :, at] = pre_grad[0:8, :]

    for j in range(PAIRS):
        at = cols(j)
        x = act_ref[0, :, at]
        stepped = spread(step, j, left)
        left_over = spread(remain, j, left)
        end_pair = split(end_ref[0, :, at])
        xadj = xadj_ref[0, :, at] + left_over * mm3(b_pair, end_pair)
        b_total = b_total + mm((x * stepped * left_over).astype(BF16), end_pair[0], NT)
        q = split(x * xadj)
        q_high[:, at] = q[0]
        q_low[:, at] = q[1]
        through(at, stepped * xadj + rows_ref[1:2, at] * grad_ref[0, :, at])
    through(slice(DI, DI + STATE), b_total)
    through(slice(DI + STATE, DI + 2 * STATE), bc_ref[0, :, STATE:])

    direct = mm(q_high[...], sel_ref[...]) + mm(q_low[...], sel_ref[...])
    log_grad = running(lg_ref[0] - step * direct, True) + carry[0:1, :]
    carry[0:1, :] = log_grad[0:1, :]
    rate = heads_ref[1:2, :]
    step_grad = direct + log_grad * rate
    step_pre_grad = step_grad * sigmoid(dt_ref[0] + heads_ref[0:1, :])
    out_ref[0, :, CONV_CH:] = step_pre_grad.astype(BF16)
    head_sums_ref[0:8, :] = head_sums_ref[0:8, :] + fold(log_grad * step * rate)
    head_sums_ref[8:16, :] = head_sums_ref[8:16, :] + fold(step_pre_grad)


def call(kernel, grid, ins, outs, scratch, flops, moved):
    return pl.pallas_call(
        kernel,
        grid=grid,
        in_specs=ins,
        out_specs=[spec for spec, _ in outs],
        out_shape=[shape for _, shape in outs],
        scratch_shapes=scratch,
        compiler_params=pltpu.CompilerParams(
            dimension_semantics=("arbitrary", "arbitrary"), vmem_limit_bytes=56 * 2**20
        ),
        cost_estimate=pl.CostEstimate(flops=flops, bytes_accessed=moved, transcendentals=0),
    )


def flip(value, axis, bit):
    count = lax.axis_size(axis)
    return lax.ppermute(value, axis, [(i, i ^ bit) for i in range(count)])


def shifted(value, axis, steps):
    count = lax.axis_size(axis)
    initial, last = (max(0, -steps), min(count, count - steps))
    return lax.ppermute(value, axis, [(source, source + steps) for source in range(initial, last)])


def bits_of(mesh_axes):
    names = []
    for axis in mesh_axes:
        bit = lax.axis_size(axis) // 2
        while bit:
            names.append((axis, bit))
            bit //= 2
    return names


def orders(names):
    core = names[-1:]
    rest = names[:-1]
    dp = [n for n in rest if n[0] == names[0][0]]
    seq = [n for n in rest if n[0] != names[0][0]]
    return [
        core + dp[::-1] + seq[::-1],
        core + dp + seq[::-1],
        core + seq[::-1] + dp,
    ]


def my_bit(name):
    return (lax.axis_index(name[0]) // name[1]) % 2


def scatter_sum(value, axes, parts):
    names = bits_of(axes)
    rows = value.shape[0] >> len(names)
    pieces = []
    for order, (begin, stop) in zip(orders(names), parts):
        a = value[:, begin:stop].reshape((2,) * len(names) + (rows, stop - begin))
        live = list(names)
        for name in order:
            d = live.index(name)
            b = my_bit(name)
            mine = lax.dynamic_index_in_dim(a, b, d, False)
            other = lax.dynamic_index_in_dim(a, 1 - b, d, False)
            a = mine + flip(other, *name)
            live.pop(d)
        pieces.append(a)
    return jnp.concatenate(pieces, axis=-1) if len(pieces) > 1 else pieces[0]


def gather(value, axes, parts):
    names = bits_of(axes)
    rows = value.shape[0]
    pieces = []
    for order, (begin, stop) in zip(orders(names), parts):
        wide = stop - begin
        place = [my_bit(name) for name in names]
        a = jnp.zeros((2,) * len(names) + (rows, wide), value.dtype)
        share = value[:, begin:stop].reshape((1,) * len(names) + (rows, wide))
        a = lax.dynamic_update_slice(a, share, place + [0, 0])
        held = [1] * len(names)
        for name in order[::-1]:
            d = names.index(name)
            starts = [0 if held[i] == 2 else place[i] for i in range(len(names))]
            block = lax.dynamic_slice(a, starts + [0, 0], held + [rows, wide])
            arrived = flip(block, *name)
            starts[d] = 1 - place[d]
            a = lax.dynamic_update_slice(a, arrived, starts + [0, 0])
            held[d] = 2
        pieces.append(a.reshape(-1, wide))
    return pieces


def total_sum(value, axes):
    for name in bits_of(axes):
        value = value + flip(value, *name)
    return value


def lanes_of(log_decay):
    return jnp.repeat(jnp.exp(log_decay[:, :HEADS]), HEADDIM, axis=1)[:, None, :]


def entering(state, logs, axis, reverse):
    count = lax.axis_size(axis)
    sign = -1 if reverse else 1
    if count == 1:
        return jnp.zeros_like(state)
    half = DI // 2
    odd = lax.axis_index(axis) % 2
    here = 1 - odd if reverse else odd
    partner = flip(state, axis, 1)
    partner_logs = flip(logs, axis, 1)
    own_half = lax.dynamic_slice_in_dim(state, odd * half, half, 2)
    other_half = lax.dynamic_slice_in_dim(partner, odd * half, half, 2)
    decay_here = lax.dynamic_slice_in_dim(lanes_of(logs), odd * half, half, 2)
    decay_there = lax.dynamic_slice_in_dim(lanes_of(partner_logs), odd * half, half, 2)
    late = here == 1
    total = jnp.where(late, decay_here * other_half + own_half, decay_there * own_half + other_half)
    decay = decay_here * decay_there
    chips = count // 2
    if chips > 1:
        window, window_decay = (shifted(v, axis, 2 * sign) for v in (total, decay))
        length = 1
        if chips > 2:
            tail, tail_decay = decay * window + total, decay * window_decay
            hop = 2
            while hop < chips:
                got, got_decay = (shifted(v, axis, 2 * sign * hop) for v in (tail, tail_decay))
                window_new = window_decay * got + window
                window_decay_new = window_decay * got_decay
                if 2 * hop < chips:
                    tail = tail_decay * got + tail
                    tail_decay = tail_decay * got_decay
                window, window_decay = window_new, window_decay_new
                hop *= 2
                length = 2 * length + 1
    else:
        window = jnp.zeros_like(total)
    whole = flip(window, axis, 1)
    both = jnp.where(
        odd == 0,
        jnp.concatenate([window, whole], axis=2),
        jnp.concatenate([whole, window], axis=2),
    )
    return jnp.where(late, lanes_of(partner_logs) * both + partner, both)


def thirds(width):
    cut = width // LANES // 3 * LANES
    return [(0, cut), (cut, 2 * cut), (2 * cut, width)]


def on_device(
    hidden_in,
    lengths,
    w_in,
    conv_w,
    conv_b,
    g_norm,
    g_gate,
    w_out,
    a_log,
    dt_bias,
    d_skip,
    out_cotangent,
):
    axes = ("dp", "seq")
    devices = lax.axis_size("dp") * lax.axis_size("seq")
    slots, tokens, _ = hidden_in.shape
    blocks = tokens // T
    rows = slots * tokens
    grid = (slots, blocks)
    share = D // devices

    small = jnp.concatenate(
        [conv_w.reshape(-1), conv_b, g_norm, g_gate], axis=0
    )
    per_row = -(-small.shape[0] // share)
    small = jnp.pad(small, (0, per_row * share - small.shape[0])).reshape(share, per_row)
    front = jnp.concatenate([w_in[:, DI:], small], axis=1)
    got = gather(front, axes, thirds(front.shape[1]))
    front_full = jnp.concatenate(got, axis=1)
    w_conv = front_full[:, :CONV_CH]
    w_dt = jnp.pad(front_full[:, CONV_CH : CONV_CH + HEADS], ((0, 0), (0, LANES - HEADS)))
    extra = front_full[:, CONV_CH + HEADS :].reshape(devices, -1)
    lane = CONV_CH // devices
    taps_full = jnp.moveaxis(extra[:, : CONV * lane].reshape(devices, CONV, lane), 0, 1)
    taps_full = taps_full.reshape(CONV, CONV_CH).astype(F32)
    at = CONV * lane
    bias_full = extra[:, at : at + lane].reshape(1, CONV_CH).astype(F32)
    at += lane
    norm_gain = extra[:, at : at + share].reshape(D).astype(F32)
    at += share
    gate_gain = extra[:, at : at + DI // devices].reshape(1, DI).astype(F32)
    back = jnp.concatenate([w_in[:, :DI], w_out.T], axis=1)
    back, front_full = lax.optimization_barrier((back, front_full))
    w_gate, w_out_turned = gather(back, axes, [(0, DI), (DI, 2 * DI)])

    taps_rows = jnp.concatenate([taps_full, bias_full, jnp.zeros((3, CONV_CH), F32)], axis=0)
    rate = -jnp.exp(a_log)
    heads_rows = jnp.pad(jnp.stack([dt_bias, rate]), ((0, 6), (0, LANES - HEADS)))
    skip_row = jnp.repeat(d_skip, HEADDIM)[None]
    gain_rows = jnp.concatenate([gate_gain, skip_row, jnp.zeros((6, DI), F32)], axis=0)
    select = (
        jnp.arange(DI, dtype=jnp.int32)[:, None] // HEADDIM
        == jnp.arange(LANES, dtype=jnp.int32)[None]
    ).astype(BF16)

    place = lax.axis_index("seq") * tokens + jnp.arange(tokens, dtype=jnp.int32)
    keep = (place[None, :] < lengths[:, None]).astype(F32)
    residual = hidden_in.astype(F32)
    inv_rms = lax.rsqrt(jnp.mean(residual * residual, axis=-1, keepdims=True) + EPSILON)
    normed = (residual * inv_rms * norm_gain).astype(BF16).reshape(rows, D)
    conv_in = jnp.dot(normed, w_conv, preferred_element_type=F32).astype(BF16)
    conv_in = conv_in.reshape(slots, tokens, CONV_CH)
    step_raw = jnp.dot(normed, w_dt, preferred_element_type=F32).reshape(slots, tokens, LANES)
    halo = shifted(conv_in[:, tokens - 8 :, :], "seq", 1)

    def tile(width, dtype=F32, flip_order=False, height=T):
        if flip_order:
            spec = pl.BlockSpec((1, height, width), lambda s, c: (s, blocks - 1 - c, 0))
        else:
            spec = pl.BlockSpec((1, height, width), lambda s, c: (s, c, 0))
        return spec, jax.ShapeDtypeStruct((slots, tokens, width), dtype)

    def per_block(height, width, flip_order=False):
        if flip_order:
            spec = pl.BlockSpec((1, 1, height, width), lambda s, c: (s, blocks - 1 - c, 0, 0))
        else:
            spec = pl.BlockSpec((1, 1, height, width), lambda s, c: (s, c, 0, 0))
        return spec, jax.ShapeDtypeStruct((slots, blocks, height, width), F32)

    def per_slot(height, width):
        spec = pl.BlockSpec((1, height, width), lambda s, c: (s, 0, 0))
        return spec, jax.ShapeDtypeStruct((slots, height, width), F32)

    def fixed(height, width):
        spec = pl.BlockSpec((height, width), lambda s, c: (0, 0))
        return spec, jax.ShapeDtypeStruct((height, width), F32)

    def specs(*pairs):
        return [spec for spec, _ in pairs]

    act, log, step, aux, enter, final, total = call(
        states_kernel,
        grid,
        specs(tile(CONV_CH), per_slot(8, CONV_CH), tile(LANES), fixed(8, CONV_CH), fixed(8, LANES)),
        [
            tile(CONV_CH), tile(LANES), tile(LANES), per_block(8, LANES),
            per_block(STATE, DI), per_slot(STATE, DI), per_slot(8, LANES),
        ],
        [pltpu.VMEM((T + 8, CONV_CH), F32), pltpu.VMEM((STATE, DI), F32), pltpu.VMEM((8, LANES), F32)],
        6 * rows * STATE * DI,
        rows * (CONV_CH * 6 + DI * 4),
    )(conv_in, halo, step_raw, taps_rows, heads_rows)
    logs = total[:, 0, :]
    start = entering(final, logs, "seq", False)

    gate_pre = jnp.dot(normed, w_gate, preferred_element_type=F32).reshape(slots, tokens, DI)
    cotangent = out_cotangent.astype(F32)
    branch_grad = (cotangent * keep[..., None]).astype(BF16).reshape(rows, D)
    norm_grad = jnp.dot(branch_grad, w_out_turned, preferred_element_type=F32)
    norm_grad = norm_grad.reshape(slots, tokens, DI)
    (local,) = call(
        local_kernel,
        grid,
        specs(tile(CONV_CH), tile(LANES), tile(LANES), per_block(STATE, DI)),
        [tile(DI)],
        [],
        12 * rows * T * DI,
        rows * (CONV_CH + 2 * DI) * 4,
    )(act, log, step, enter)

    gated_norm, mixed_grad, gate_grad, lg, adj_enter, adj_final, gate_sums = call(
        gate_kernel,
        grid,
        specs(
            tile(CONV_CH, flip_order=True), tile(LANES, flip_order=True),
            per_block(8, LANES, True), tile(DI, flip_order=True), tile(DI, flip_order=True),
            tile(DI, flip_order=True), per_slot(STATE, DI), fixed(8, DI), fixed(DI, LANES),
        ),
        [
            tile(DI, BF16, True), tile(DI, F32, True), tile(DI, BF16, True),
            tile(LANES, F32, True), per_block(STATE, DI, True), per_slot(STATE, DI), fixed(16, DI),
        ],
        [
            pltpu.VMEM((T, DI), F32), pltpu.VMEM((T, DI), F32), pltpu.VMEM((STATE, DI), F32),
            pltpu.VMEM((T, DI), BF16), pltpu.VMEM((T, DI), BF16),
        ],
        12 * rows * STATE * DI,
        rows * (CONV_CH * 4 + DI * 24),
    )(act, log, aux, local, gate_pre, norm_grad, start, gain_rows, select)
    gated_norm = gated_norm.reshape(rows, DI)
    gate_grad = gate_grad.reshape(rows, DI)
    end_adj = entering(adj_final, logs, "seq", True)

    w_out_grad = lax.dot_general(
        branch_grad, gated_norm, (((0,), (0,)), ((), ())), preferred_element_type=F32
    )
    w_out_owned = scatter_sum(w_out_grad, axes, thirds(DI))
    w_gate_grad = lax.dot_general(
        normed, gate_grad, (((0,), (0,)), ((), ())), preferred_element_type=F32
    )
    w_gate_owned = scatter_sum(w_gate_grad, axes, thirds(DI))
    branch = lax.dot_general(gated_norm, w_out_turned, NT, preferred_element_type=F32)
    block_out = (residual + keep[..., None] * branch.reshape(slots, tokens, D)).astype(BF16)

    xadj, bc_grad = call(
        adjoint_kernel,
        grid,
        specs(
            tile(CONV_CH), tile(LANES), tile(LANES), per_block(8, LANES), tile(DI),
            per_block(STATE, DI), per_slot(STATE, DI), per_block(STATE, DI),
        ),
        [tile(DI), tile(2 * STATE)],
        [],
        30 * rows * T * DI,
        rows * (CONV_CH + 4 * DI) * 4,
    )(act, log, step, aux, mixed_grad, enter, start, adj_enter)

    end_state = lanes_of(logs) * start + final
    tail = jnp.sum(end_adj * end_state, axis=1).reshape(slots, HEADS, HEADDIM).sum(-1)
    tail = jnp.broadcast_to(jnp.pad(tail, ((0, 0), (0, LANES - HEADS)))[:, None], (slots, 8, LANES))
    wide = CONV_CH + LANES
    prev = pl.BlockSpec(
        (1, 16, CONV_CH), lambda s, c: (s, jnp.maximum((blocks - 1 - c) * (T // 16) - 1, 0), 0)
    )
    proj_grad, head_rows, last_rows, conv_sums, head_sums = call(
        finish_kernel,
        grid,
        specs(
            tile(CONV_CH, flip_order=True), tile(LANES, flip_order=True), tile(LANES, flip_order=True),
            per_block(8, LANES, True), per_slot(8, LANES), tile(DI, flip_order=True),
            tile(DI, flip_order=True), tile(2 * STATE, flip_order=True), tile(LANES, flip_order=True),
            per_slot(STATE, DI), tile(CONV_CH, flip_order=True), (prev, None), per_slot(8, CONV_CH),
            tile(LANES, flip_order=True), per_slot(8, LANES), fixed(8, CONV_CH), fixed(8, LANES),
            fixed(8, DI), fixed(DI, LANES),
        ),
        [
            tile(wide, BF16, True), per_slot(8, CONV_CH), per_slot(8, CONV_CH),
            fixed(40, CONV_CH), fixed(16, LANES),
        ],
        [
            pltpu.VMEM((T + 16, CONV_CH), F32), pltpu.VMEM((T + 8, CONV_CH), F32),
            pltpu.VMEM((T, DI), BF16), pltpu.VMEM((T, DI), BF16), pltpu.VMEM((8, LANES), F32),
        ],
        12 * rows * STATE * DI,
        rows * (CONV_CH * 8 + DI * 8),
    )(
        act, log, step, aux, total, mixed_grad, xadj, bc_grad, lg, end_adj, conv_in, conv_in, halo,
        step_raw, tail, taps_rows, heads_rows, gain_rows, select,
    )

    ahead = shifted(head_rows, "seq", -1)
    ahead = jnp.concatenate([jnp.zeros((slots, 8, CONV_CH), F32), ahead], axis=1)
    for tap in range(CONV):
        begin = CONV - 1 - tap
        last_rows = last_rows + ahead[:, begin : begin + 8] * taps_full[tap]
    proj_grad = lax.dynamic_update_slice(
        proj_grad, last_rows.astype(BF16), (0, tokens - 8, 0)
    ).reshape(rows, wide)

    w_front_grad = lax.dot_general(
        normed, proj_grad, (((0,), (0,)), ((), ())), preferred_element_type=F32
    )
    w_front_owned = scatter_sum(w_front_grad, axes, thirds(wide))
    w_front = jnp.concatenate([w_conv, w_dt], axis=1)
    normed_grad = lax.dot_general(proj_grad, w_front, NT, preferred_element_type=F32)
    normed_grad = normed_grad + lax.dot_general(gate_grad, w_gate, NT, preferred_element_type=F32)
    normed_grad = normed_grad.reshape(slots, tokens, D)
    g_norm_grad = jnp.sum(normed_grad * residual * inv_rms, axis=(0, 1))
    scaled_in = normed_grad * norm_gain
    input_grad = cotangent + inv_rms * (
        scaled_in
        - residual * inv_rms * inv_rms * jnp.mean(scaled_in * residual, axis=-1, keepdims=True)
    )

    sums = conv_sums.reshape(CONV + 1, 8, CONV_CH).sum(1)
    d_skip_grad = gate_sums[8:].sum(0).reshape(HEADS, HEADDIM).sum(-1)
    head_grads = head_sums.reshape(2, 8, LANES).sum(1)[:, :HEADS]
    vectors = jnp.concatenate(
        [
            sums.reshape(-1), g_norm_grad, gate_sums[:8].sum(0), head_grads.reshape(-1), d_skip_grad,
        ]
    )
    count = vectors.shape[0]
    vectors = jnp.pad(vectors, (0, -count % 1024)).reshape(-1, LANES)
    vectors = total_sum(vectors, axes).reshape(-1)
    me = lax.axis_index("dp") * lax.axis_size("seq") + lax.axis_index("seq")

    def owned(begin, length):
        per = length // devices
        return lax.dynamic_slice_in_dim(vectors, begin + me * per, per)

    conv_w_grad = jnp.stack([owned(k * CONV_CH, CONV_CH) for k in range(CONV)])
    conv_b_grad = owned(CONV * CONV_CH, CONV_CH)
    at = (CONV + 1) * CONV_CH
    w_front_owned = w_front_owned[:, : CONV_CH + HEADS]
    heads_at = at + D + DI
    return (
        block_out,
        input_grad,
        jnp.concatenate([w_gate_owned, w_front_owned], axis=1),
        conv_w_grad,
        conv_b_grad,
        owned(at, D),
        owned(at + D, DI),
        w_out_owned.T,
        vectors[heads_at : heads_at + HEADS],
        vectors[heads_at + HEADS : heads_at + 2 * HEADS],
        vectors[heads_at + 2 * HEADS : heads_at + 3 * HEADS],
    )


def solution(mesh):
    placed = (
        P("dp", "seq", None),
        P("dp"),
        P(("dp", "seq"), None),
        P(None, ("dp", "seq")),
        P(("dp", "seq")),
        P(("dp", "seq")),
        P(("dp", "seq")),
        P(None, ("dp", "seq")),
        P(),
        P(),
        P(),
        P("dp", "seq", None),
    )
    return jax.shard_map(
        on_device,
        mesh=mesh,
        in_specs=placed,
        out_specs=(
            P("dp", "seq", None),
            P("dp", "seq", None),
            P(("dp", "seq"), None),
            P(None, ("dp", "seq")),
            P(("dp", "seq")),
            P(("dp", "seq")),
            P(("dp", "seq")),
            P(None, ("dp", "seq")),
            P(),
            P(),
            P(),
        ),
        check_vma=False,
    )
```

```python
import functools

import jax
import jax.numpy as jnp
from jax import lax
from jax.experimental import pallas as pl
from jax.experimental.pallas import tpu as pltpu
from jax.sharding import PartitionSpec as P

D = 768
HEADS = 24
HEADDIM = 64
STATE = 128
CONV = 4
DI = 1536
CONV_CH = 1792
PROJ = 3352
T = 128
PAIRS = HEADS // 2
LANES = 128
EPSILON = 1e-05
MASKED = -1e30
F32 = jnp.float32
BF16 = jnp.bfloat16
NN = (((1,), (0,)), ((), ()))
NT = (((1,), (1,)), ((), ()))


def mm(a, b, dims=NN):
    return lax.dot_general(a, b, dims, preferred_element_type=F32)


def split(v):
    high = v.astype(BF16)
    return high, (v - high.astype(F32)).astype(BF16)


def mm3(a, b, dims=NN):
    return mm(a[0], b[0], dims) + (mm(a[0], b[1], dims) + mm(a[1], b[0], dims))


def left_half(rows):
    return lax.broadcasted_iota(jnp.int32, (rows, LANES), 1) < HEADDIM


def spread(values, pair, left):
    return jnp.where(
        left, values[:, 2 * pair : 2 * pair + 1], values[:, 2 * pair + 1 : 2 * pair + 2]
    )


def cols(j):
    return slice(j * LANES, (j + 1) * LANES)


def running(v, reverse):
    row = lax.broadcasted_iota(jnp.int32, v.shape, 0)
    hop = 1
    while hop < T:
        moved = pltpu.roll(v, T - hop if reverse else hop, 0)
        inside = row < T - hop if reverse else row >= hop
        v = v + jnp.where(inside, moved, 0.0)
        hop *= 2
    return v


def fold(v):
    return jnp.sum(v.reshape(T // 8, 8, v.shape[-1]), axis=0)


def two_heads(high, low, left):
    zero = jnp.zeros_like(high)
    top = jnp.concatenate([jnp.where(left, high, zero), jnp.where(left, low, zero)], axis=1)
    bottom = jnp.concatenate([jnp.where(left, zero, high), jnp.where(left, zero, low)], axis=1)
    return jnp.concatenate([top, bottom], axis=0)


def sigmoid(v):
    return 0.5 * jnp.tanh(0.5 * v) + 0.5


def convolve(window, taps_ref, at, first):
    total = taps_ref[CONV : CONV + 1, at]
    rows = [window[first + tap : first + tap + T, at] for tap in range(CONV)]
    for tap in range(CONV):
        total = total + rows[tap] * taps_ref[tap : tap + 1, at]
    return total, rows


def states_kernel(
    conv_ref, halo_ref, dt_ref, taps_ref, heads_ref,
    act_ref, log_ref, step_ref, aux_ref, enter_ref, final_ref, total_ref,
    window, state, before,
):
    c = pl.program_id(1)

    @pl.when(c == 0)
    def _():
        window[0:8, :] = halo_ref[0].astype(F32)
        state[...] = jnp.zeros_like(state)
        before[...] = jnp.zeros_like(before)

    window[8 : 8 + T, :] = conv_ref[0].astype(F32)
    for j in range(CONV_CH // LANES):
        pre, _ = convolve(window, taps_ref, cols(j), 8 - (CONV - 1))
        act_ref[0, :, cols(j)] = pre * sigmoid(pre)
    window[0:8, :] = window[T : T + 8, :]

    step = jax.nn.softplus(dt_ref[0] + heads_ref[0:1, :])
    log = running(step * heads_ref[1:2, :], False)
    end = log[T - 1 : T, :]
    step_ref[0] = step
    log_ref[0] = log
    weight = jnp.exp(end - log) * step
    decay = jnp.exp(end)
    left = left_half(T)
    aux_ref[0, 0] = jnp.concatenate([before[0:1, :], end, jnp.zeros((6, LANES), F32)], axis=0)
    before[0:1, :] = before[0:1, :] + end
    b_turned = split(act_ref[0, :, DI : DI + STATE].T)
    for j in range(PAIRS):
        prior = state[:, cols(j)]
        enter_ref[0, 0, :, cols(j)] = prior
        fed = split(act_ref[0, :, cols(j)] * spread(weight, j, left))
        state[:, cols(j)] = prior * spread(decay, j, left[0:1]) + mm3(b_turned, fed)

    @pl.when(c == pl.num_programs(1) - 1)
    def _():
        final_ref[0] = state[...]
        total_ref[0] = before[...]


def local_kernel(act_ref, log_ref, step_ref, enter_ref, out_ref):
    log = log_ref[0]
    log_turned = log.T
    step = step_ref[0]
    grown = jnp.exp(log)
    left = left_half(T)
    row = lax.broadcasted_iota(jnp.int32, (T, T), 0)
    col = lax.broadcasted_iota(jnp.int32, (T, T), 1)
    causal = row >= col
    b_pair = split(act_ref[0, :, DI : DI + STATE])
    c_pair = split(act_ref[0, :, DI + STATE :])
    inner = mm3(c_pair, b_pair, NT)
    for j in range(PAIRS):
        fed = split(act_ref[0, :, cols(j)] * spread(step, j, left))
        rhs = two_heads(fed[0], fed[1], left)
        mats = []
        for head in (2 * j, 2 * j + 1):
            gap = log[:, head : head + 1] - log_turned[head : head + 1, :]
            mats.append(inner * jnp.exp(jnp.where(causal, gap, MASKED)))
        mixing = split(jnp.concatenate(mats, axis=1))
        wide = mm(mixing[0], rhs)
        out = wide[:, :LANES] + (wide[:, LANES:] + mm(mixing[1], rhs[:, :LANES]))
        crossed = mm3(c_pair, split(enter_ref[0, 0, :, cols(j)]))
        out_ref[0, :, cols(j)] = out + spread(grown, j, left) * crossed


def gate_kernel(
    act_ref, log_ref, aux_ref, local_ref, gate_ref, ng_ref, start_ref, rows_ref, sel_ref,
    normed_ref, mixed_grad_ref, gate_grad_ref, lg_ref, enter_ref, final_ref, sums_ref,
    scan_s, gated_s, adj, q_high, q_low,
):
    s, c = pl.program_id(0), pl.program_id(1)

    @pl.when(c == 0)
    def _():
        adj[...] = jnp.zeros_like(adj)

    @pl.when((s == 0) & (c == 0))
    def _():
        sums_ref[...] = jnp.zeros_like(sums_ref)

    log = log_ref[0]
    before = aux_ref[0, 0, 0:1, :]
    end = aux_ref[0, 0, 1:2, :]
    left = left_half(T)
    since = jnp.exp(before + log)
    grown = jnp.exp(log)
    decay = jnp.exp(end)
    c_rows = act_ref[0, :, DI + STATE :]
    c_pair = split(c_rows)
    c_turned = split(c_rows.T)
    squares = jnp.zeros((T, LANES), F32)
    products = jnp.zeros((T, LANES), F32)
    for j in range(PAIRS):
        at = cols(j)
        crossed = mm3(c_pair, split(start_ref[0, :, at]))
        scan = local_ref[0, :, at] + spread(since, j, left) * crossed
        gate = gate_ref[0, :, at]
        mixed = scan + rows_ref[1:2, at] * act_ref[0, :, at]
        gated = mixed * (gate * sigmoid(gate))
        scan_s[:, at] = scan
        gated_s[:, at] = gated
        squares = squares + gated * gated
        products = products + ng_ref[0, :, at] * rows_ref[0:1, at] * gated
    inv = lax.rsqrt(jnp.sum(squares, axis=-1, keepdims=True) / DI + EPSILON)
    mean = jnp.sum(products, axis=-1, keepdims=True) / DI
    pull = inv * inv * mean
    for j in range(PAIRS):
        at = cols(j)
        scan = scan_s[:, at]
        gated = gated_s[:, at]
        gate = gate_ref[0, :, at]
        x = act_ref[0, :, at]
        gain = rows_ref[0:1, at]
        ng = ng_ref[0, :, at]
        sig = sigmoid(gate)
        unit = gated * inv
        normed_ref[0, :, at] = (unit * gain).astype(BF16)
        sums_ref[0:8, at] = sums_ref[0:8, at] + fold(ng * unit)
        gated_grad = inv * (ng * gain - gated * pull)
        mixed = scan + rows_ref[1:2, at] * x
        mixed_grad = gated_grad * (gate * sig)
        mixed_grad_ref[0, :, at] = mixed_grad
        gate_grad_ref[0, :, at] = (
            gated_grad * mixed * sig * (1.0 + gate * (1.0 - sig))
        ).astype(BF16)
        sums_ref[8:16, at] = sums_ref[8:16, at] + fold(x * mixed_grad)
        q = split(mixed_grad * scan)
        q_high[:, at] = q[0]
        q_low[:, at] = q[1]
        prior = adj[:, at]
        enter_ref[0, 0, :, at] = prior
        fed = split(mixed_grad * spread(grown, j, left))
        adj[:, at] = prior * spread(decay, j, left[0:1]) + mm3(c_turned, fed)
    lg_ref[0] = mm(q_high[...], sel_ref[...]) + mm(q_low[...], sel_ref[...])

    @pl.when(c == pl.num_programs(1) - 1)
    def _():
        final_ref[0] = adj[...]


def adjoint_kernel(
    act_ref, log_ref, step_ref, aux_ref, grad_ref, enter_ref, start_ref, adj_ref,
    xadj_ref, bc_ref,
):
    log = log_ref[0]
    log_turned = log.T
    step = step_ref[0]
    before = aux_ref[0, 0, 0:1, :]
    end = aux_ref[0, 0, 1:2, :]
    left = left_half(T)
    row = lax.broadcasted_iota(jnp.int32, (T, T), 0)
    col = lax.broadcasted_iota(jnp.int32, (T, T), 1)
    later = col >= row
    b_rows = act_ref[0, :, DI : DI + STATE]
    c_rows = act_ref[0, :, DI + STATE :]
    b_pair = split(b_rows)
    c_pair = split(c_rows)
    inner = mm3(b_pair, c_pair, NT)
    grown = jnp.exp(log)
    to_end = jnp.exp(end - log)
    reach = jnp.exp(before)
    weighted = jnp.zeros((T, T), F32)
    b_total = jnp.zeros((T, STATE), F32)
    c_total = jnp.zeros((T, STATE), F32)
    for j in range(PAIRS):
        at = cols(j)
        grad = grad_ref[0, :, at]
        fed = act_ref[0, :, at] * spread(step, j, left)
        high, low = split(grad)
        rhs = two_heads(high, low, left)
        decays = []
        for head in (2 * j, 2 * j + 1):
            gap = log_turned[head : head + 1, :] - log[:, head : head + 1]
            decays.append(jnp.exp(jnp.where(later, gap, MASKED)))
        mixing = split(jnp.concatenate([inner * decays[0], inner * decays[1]], axis=1))
        wide = mm(mixing[0], rhs)
        out = wide[:, :LANES] + (wide[:, LANES:] + mm(mixing[1], rhs[:, :LANES]))
        short = fed.astype(BF16)
        zero = jnp.zeros_like(short)
        stacked = jnp.concatenate(
            [jnp.where(left, short, zero), jnp.where(left, zero, short)], axis=0
        )
        dots = mm(stacked, high, NT)
        weighted = weighted + (decays[0] * dots[:T] + decays[1] * dots[T:])
        adj = split(adj_ref[0, 0, :, at])
        reached = spread(to_end, j, left)
        xadj_ref[0, :, at] = out + reached * mm3(b_pair, adj)
        b_total = b_total + mm((fed * reached).astype(BF16), adj[0], NT)
        entering = enter_ref[0, 0, :, at] + spread(reach, j, left[0:1]) * start_ref[0, :, at]
        c_total = c_total + mm3(split(grad * spread(grown, j, left)), split(entering), NT)
    bc_ref[0, :, 0:STATE] = b_total + mm(weighted.astype(BF16), c_pair[0])
    bc_ref[0, :, STATE:] = c_total + mm(weighted.T.astype(BF16), b_pair[0])


def finish_kernel(
    act_ref, log_ref, step_ref, aux_ref, total_ref, grad_ref, xadj_ref, bc_ref, lg_ref,
    end_ref, conv_ref, prev_ref, halo_ref, dt_ref, tail_ref, taps_ref, heads_ref, rows_ref,
    sel_ref,
    out_ref, head_ref, last_ref, sums_ref, head_sums_ref,
    window, pre_s, q_high, q_low, carry,
):
    s, c = pl.program_id(0), pl.program_id(1)
    first = c == pl.num_programs(1) - 1

    @pl.when(c == 0)
    def _():
        pre_s[T : T + 8, :] = jnp.zeros((8, CONV_CH), F32)
        carry[...] = tail_ref[0]

    @pl.when((s == 0) & (c == 0))
    def _():
        sums_ref[...] = jnp.zeros_like(sums_ref)
        head_sums_ref[...] = jnp.zeros_like(head_sums_ref)

    @pl.when(first)
    def _():
        window[8:16, :] = halo_ref[0].astype(F32)

    @pl.when(jnp.logical_not(first))
    def _():
        window[8:16, :] = prev_ref[0].astype(F32)[8:16, :]

    window[16 : 16 + T, :] = conv_ref[0].astype(F32)
    log = log_ref[0]
    step = step_ref[0]
    before = aux_ref[0, 0, 0:1, :]
    end = aux_ref[0, 0, 1:2, :]
    left = left_half(T)
    remain = jnp.exp((total_ref[0, 0:1, :] - before - end) + (end - log))
    b_pair = split(act_ref[0, :, DI : DI + STATE])
    b_total = bc_ref[0, :, 0:STATE]

    def through(at, act_grad):
        pre, before_rows = convolve(window, taps_ref, at, 16 - (CONV - 1))
        sig = sigmoid(pre)
        pre_grad = act_grad * sig * (1.0 + pre * (1.0 - sig))
        pre_s[0:T, at] = pre_grad
        for tap in range(CONV):
            rows = slice(8 * tap, 8 * tap + 8)
            sums_ref[rows, at] = sums_ref[rows, at] + fold(pre_grad * before_rows[tap])
        sums_ref[32:40, at] = sums_ref[32:40, at] + fold(pre_grad)
        into = pre_grad * taps_ref[CONV - 1 : CONV, at]
        for tap in range(CONV - 1):
            ahead = CONV - 1 - tap
            into = into + pre_s[ahead : ahead + T, at] * taps_ref[tap : tap + 1, at]
        out_ref[0, :, at] = into.astype(BF16)

        @pl.when(c == 0)
        def _():
            last_ref[0, :, at] = into[T - 8 :, :]

        pre_s[T : T + 8, at] = pre_grad[0:8, :]

        @pl.when(first)
        def _():
            head_ref[0, :, at] = pre_grad[0:8, :]

    for j in range(PAIRS):
        at = cols(j)
        x = act_ref[0, :, at]
        stepped = spread(step, j, left)
        left_over = spread(remain, j, left)
        end_pair = split(end_ref[0, :, at])
        xadj = xadj_ref[0, :, at] + left_over * mm3(b_pair, end_pair)
        b_total = b_total + mm((x * stepped * left_over).astype(BF16), end_pair[0], NT)
        q = split(x * xadj)
        q_high[:, at] = q[0]
        q_low[:, at] = q[1]
        through(at, stepped * xadj + rows_ref[1:2, at] * grad_ref[0, :, at])
    through(slice(DI, DI + STATE), b_total)
    through(slice(DI + STATE, DI + 2 * STATE), bc_ref[0, :, STATE:])

    direct = mm(q_high[...], sel_ref[...]) + mm(q_low[...], sel_ref[...])
    log_grad = running(lg_ref[0] - step * direct, True) + carry[0:1, :]
    carry[0:1, :] = log_grad[0:1, :]
    rate = heads_ref[1:2, :]
    step_grad = direct + log_grad * rate
    step_pre_grad = step_grad * sigmoid(dt_ref[0] + heads_ref[0:1, :])
    out_ref[0, :, CONV_CH:] = step_pre_grad.astype(BF16)
    head_sums_ref[0:8, :] = head_sums_ref[0:8, :] + fold(log_grad * step * rate)
    head_sums_ref[8:16, :] = head_sums_ref[8:16, :] + fold(step_pre_grad)


def call(kernel, grid, ins, outs, scratch, flops, moved):
    return pl.pallas_call(
        kernel,
        grid=grid,
        in_specs=ins,
        out_specs=[spec for spec, _ in outs],
        out_shape=[shape for _, shape in outs],
        scratch_shapes=scratch,
        compiler_params=pltpu.CompilerParams(
            dimension_semantics=("arbitrary", "arbitrary"), vmem_limit_bytes=56 * 2**20
        ),
        cost_estimate=pl.CostEstimate(flops=flops, bytes_accessed=moved, transcendentals=0),
    )


def flip(value, axis, bit):
    count = lax.axis_size(axis)
    return lax.ppermute(value, axis, [(i, i ^ bit) for i in range(count)])


def shifted(value, axis, steps):
    count = lax.axis_size(axis)
    initial, last = (max(0, -steps), min(count, count - steps))
    return lax.ppermute(value, axis, [(source, source + steps) for source in range(initial, last)])


def bits_of(mesh_axes):
    names = []
    for axis in mesh_axes:
        bit = lax.axis_size(axis) // 2
        while bit:
            names.append((axis, bit))
            bit //= 2
    return names


def orders(names):
    core = names[-1:]
    rest = names[:-1]
    dp = [n for n in rest if n[0] == names[0][0]]
    seq = [n for n in rest if n[0] != names[0][0]]
    return [
        core + dp[::-1] + seq[::-1],
        core + dp + seq[::-1],
        core + seq[::-1] + dp,
    ]


def my_bit(name):
    return (lax.axis_index(name[0]) // name[1]) % 2


def scatter_sum(value, axes, parts):
    names = bits_of(axes)
    rows = value.shape[0] >> len(names)
    pieces = []
    for order, (begin, stop) in zip(orders(names), parts):
        a = value[:, begin:stop].reshape((2,) * len(names) + (rows, stop - begin))
        live = list(names)
        for name in order:
            d = live.index(name)
            b = my_bit(name)
            mine = lax.dynamic_index_in_dim(a, b, d, False)
            other = lax.dynamic_index_in_dim(a, 1 - b, d, False)
            a = mine + flip(other, *name)
            live.pop(d)
        pieces.append(a)
    return jnp.concatenate(pieces, axis=-1) if len(pieces) > 1 else pieces[0]


def after(value, *others):
    return lax.optimization_barrier((value,) + others)[0]


def in_order(blocks, me):
    bit = 1
    while bit < len(blocks):
        swap = (me // bit) % 2 == 1
        blocks = [jnp.where(swap, blocks[i ^ bit], block) for i, block in enumerate(blocks)]
        bit *= 2
    return jnp.stack(blocks)


def gather(value):
    seq, dp = lax.axis_size("seq"), lax.axis_size("dp")
    me = lax.axis_index("seq")
    chips = [value] + [flip(value, "seq", 2 * hop) for hop in range(1, seq // 2)]
    held = in_order(chips, me // 2)
    held = in_order(
        [held] + [flip(held, "dp", hop) for hop in range(1, dp)], lax.axis_index("dp")
    )
    other = flip(held, "seq", 1)
    even = me % 2 == 0
    both = jnp.stack([jnp.where(even, held, other), jnp.where(even, other, held)], axis=2)
    return both.reshape(-1, value.shape[1])


def total_sum(value, axes):
    for name in bits_of(axes):
        value = value + flip(value, *name)
    return value


def lanes_of(log_decay):
    return jnp.repeat(jnp.exp(log_decay[:, :HEADS]), HEADDIM, axis=1)[:, None, :]


class Entering:
    def __init__(self, state, logs, axis, reverse):
        self.axis = axis
        self.sign = -1 if reverse else 1
        self.state, self.logs = state, logs
        self.odd = lax.axis_index(axis) % 2
        self.late = self.odd == (0 if reverse else 1)
        self.partner = flip(state, axis, 1)
        self.partner_logs = flip(logs, axis, 1)
        self.chips = lax.axis_size(axis) // 2

    def half(self, value):
        return lax.dynamic_slice_in_dim(value, self.odd * (DI // 2), DI // 2, 2)

    def chip_total(self, *beside):
        self.partner, *beside = lax.optimization_barrier((self.partner,) + beside)
        here, there = self.half(self.state), self.half(self.partner)
        decay_here = self.half(lanes_of(self.logs))
        decay_there = self.half(lanes_of(self.partner_logs))
        total = jnp.where(self.late, decay_here * there + here, decay_there * here + there)
        self.total, self.decay = total, decay_here * decay_there
        self.got = shifted(total, self.axis, 2 * self.sign)
        return beside

    def first_hop(self, *beside):
        self.window, *beside = lax.optimization_barrier((self.got,) + beside)
        self.window_decay = shifted(self.decay, self.axis, 2 * self.sign)
        self.tail = self.decay * self.window + self.total
        self.tail_decay = self.decay * self.window_decay
        return beside

    def last_hops(self, *beside):
        hop = 2
        while hop < self.chips:
            got = shifted(self.tail, self.axis, 2 * self.sign * hop)
            if hop == 2:
                got, *beside = lax.optimization_barrier((got,) + beside)
            got_decay = shifted(self.tail_decay, self.axis, 2 * self.sign * hop)
            self.window = self.window_decay * got + self.window
            self.window_decay = self.window_decay * got_decay
            hop *= 2
            if hop < self.chips:
                self.tail = self.tail_decay * got + self.tail
                self.tail_decay = self.tail_decay * got_decay
        self.whole = flip(self.window, self.axis, 1)
        return beside

    def result(self, *beside):
        self.whole, *beside = lax.optimization_barrier((self.whole,) + beside)
        both = jnp.where(
            self.odd == 0,
            jnp.concatenate([self.window, self.whole], axis=2),
            jnp.concatenate([self.whole, self.window], axis=2),
        )
        state = jnp.where(self.late, lanes_of(self.partner_logs) * both + self.partner, both)
        return [state] + beside


def thirds(width):
    cut = width // LANES // 3 * LANES
    return [(0, cut), (cut, 2 * cut), (2 * cut, width)]


def on_device(
    hidden_in,
    lengths,
    w_in,
    conv_w,
    conv_b,
    g_norm,
    g_gate,
    w_out,
    a_log,
    dt_bias,
    d_skip,
    out_cotangent,
):
    axes = ("dp", "seq")
    devices = lax.axis_size("dp") * lax.axis_size("seq")
    slots, tokens, _ = hidden_in.shape
    blocks = tokens // T
    rows = slots * tokens
    grid = (slots, blocks)
    share = D // devices

    small = jnp.concatenate(
        [conv_w.reshape(-1), conv_b, g_norm, g_gate], axis=0
    )
    per_row = -(-small.shape[0] // share)
    small = jnp.pad(small, (0, per_row * share - small.shape[0])).reshape(share, per_row)
    front = jnp.concatenate([w_in[:, DI:], small], axis=1)
    front_full = gather(front)
    w_conv = front_full[:, :CONV_CH]
    w_dt = jnp.pad(front_full[:, CONV_CH : CONV_CH + HEADS], ((0, 0), (0, LANES - HEADS)))
    extra = front_full[:, CONV_CH + HEADS :].reshape(devices, -1)
    lane = CONV_CH // devices
    taps_full = jnp.moveaxis(extra[:, : CONV * lane].reshape(devices, CONV, lane), 0, 1)
    taps_full = taps_full.reshape(CONV, CONV_CH).astype(F32)
    at = CONV * lane
    bias_full = extra[:, at : at + lane].reshape(1, CONV_CH).astype(F32)
    at += lane
    norm_gain = extra[:, at : at + share].reshape(D).astype(F32)
    at += share
    gate_gain = extra[:, at : at + DI // devices].reshape(1, DI).astype(F32)
    back = jnp.concatenate([w_in[:, :DI], w_out.T], axis=1)
    back = lax.all_gather(back, axes, axis=0, tiled=True)
    w_gate, w_out_turned = back[:, :DI], back[:, DI:]

    taps_rows = jnp.concatenate([taps_full, bias_full, jnp.zeros((3, CONV_CH), F32)], axis=0)
    rate = -jnp.exp(a_log)
    heads_rows = jnp.pad(jnp.stack([dt_bias, rate]), ((0, 6), (0, LANES - HEADS)))
    skip_row = jnp.repeat(d_skip, HEADDIM)[None]
    gain_rows = jnp.concatenate([gate_gain, skip_row, jnp.zeros((6, DI), F32)], axis=0)
    select = (
        jnp.arange(DI, dtype=jnp.int32)[:, None] // HEADDIM
        == jnp.arange(LANES, dtype=jnp.int32)[None]
    ).astype(BF16)

    place = lax.axis_index("seq") * tokens + jnp.arange(tokens, dtype=jnp.int32)
    keep = (place[None, :] < lengths[:, None]).astype(F32)
    residual = hidden_in.astype(F32)
    inv_rms = lax.rsqrt(jnp.mean(residual * residual, axis=-1, keepdims=True) + EPSILON)
    normed = (residual * inv_rms * norm_gain).astype(BF16).reshape(rows, D)
    conv_in = jnp.dot(normed, w_conv, preferred_element_type=F32).astype(BF16)
    conv_in = conv_in.reshape(slots, tokens, CONV_CH)
    step_raw = jnp.dot(normed, w_dt, preferred_element_type=F32).reshape(slots, tokens, LANES)
    halo = shifted(conv_in[:, tokens - 8 :, :], "seq", 1)

    def tile(width, dtype=F32, flip_order=False, height=T):
        if flip_order:
            spec = pl.BlockSpec((1, height, width), lambda s, c: (s, blocks - 1 - c, 0))
        else:
            spec = pl.BlockSpec((1, height, width), lambda s, c: (s, c, 0))
        return spec, jax.ShapeDtypeStruct((slots, tokens, width), dtype)

    def per_block(height, width, flip_order=False):
        if flip_order:
            spec = pl.BlockSpec((1, 1, height, width), lambda s, c: (s, blocks - 1 - c, 0, 0))
        else:
            spec = pl.BlockSpec((1, 1, height, width), lambda s, c: (s, c, 0, 0))
        return spec, jax.ShapeDtypeStruct((slots, blocks, height, width), F32)

    def per_slot(height, width):
        spec = pl.BlockSpec((1, height, width), lambda s, c: (s, 0, 0))
        return spec, jax.ShapeDtypeStruct((slots, height, width), F32)

    def fixed(height, width):
        spec = pl.BlockSpec((height, width), lambda s, c: (0, 0))
        return spec, jax.ShapeDtypeStruct((height, width), F32)

    def specs(*pairs):
        return [spec for spec, _ in pairs]

    act, log, step, aux, enter, final, total = call(
        states_kernel,
        grid,
        specs(tile(CONV_CH), per_slot(8, CONV_CH), tile(LANES), fixed(8, CONV_CH), fixed(8, LANES)),
        [
            tile(CONV_CH), tile(LANES), tile(LANES), per_block(8, LANES),
            per_block(STATE, DI), per_slot(STATE, DI), per_slot(8, LANES),
        ],
        [pltpu.VMEM((T + 8, CONV_CH), F32), pltpu.VMEM((STATE, DI), F32), pltpu.VMEM((8, LANES), F32)],
        6 * rows * STATE * DI,
        rows * (CONV_CH * 6 + DI * 4),
    )(conv_in, halo, step_raw, taps_rows, heads_rows)
    logs = total[:, 0, :]
    forward = Entering(final, logs, "seq", False)
    gate_pre = jnp.dot(after(normed, final), w_gate, preferred_element_type=F32)
    (gate_pre,) = forward.chip_total(gate_pre.reshape(slots, tokens, DI))
    cotangent = out_cotangent.astype(F32)
    branch_grad = (cotangent * keep[..., None]).astype(BF16).reshape(rows, D)
    norm_grad = jnp.dot(
        after(branch_grad, forward.total), w_out_turned, preferred_element_type=F32
    )
    (norm_grad,) = forward.first_hop(norm_grad.reshape(slots, tokens, DI))
    (local,) = call(
        local_kernel,
        grid,
        specs(tile(CONV_CH), tile(LANES), tile(LANES), per_block(STATE, DI)),
        [tile(DI)],
        [],
        12 * rows * T * DI,
        rows * (CONV_CH + 2 * DI) * 4,
    )(after(act, forward.tail), log, step, enter)
    (local,) = forward.last_hops(local)
    (start,) = forward.result()

    gated_norm, mixed_grad, gate_grad, lg, adj_enter, adj_final, gate_sums = call(
        gate_kernel,
        grid,
        specs(
            tile(CONV_CH, flip_order=True), tile(LANES, flip_order=True),
            per_block(8, LANES, True), tile(DI, flip_order=True), tile(DI, flip_order=True),
            tile(DI, flip_order=True), per_slot(STATE, DI), fixed(8, DI), fixed(DI, LANES),
        ),
        [
            tile(DI, BF16, True), tile(DI, F32, True), tile(DI, BF16, True),
            tile(LANES, F32, True), per_block(STATE, DI, True), per_slot(STATE, DI), fixed(16, DI),
        ],
        [
            pltpu.VMEM((T, DI), F32), pltpu.VMEM((T, DI), F32), pltpu.VMEM((STATE, DI), F32),
            pltpu.VMEM((T, DI), BF16), pltpu.VMEM((T, DI), BF16),
        ],
        12 * rows * STATE * DI,
        rows * (CONV_CH * 4 + DI * 24),
    )(act, log, aux, local, gate_pre, norm_grad, start, gain_rows, select)
    gated_norm = gated_norm.reshape(rows, DI)
    gate_grad = gate_grad.reshape(rows, DI)
    backward = Entering(adj_final, logs, "seq", True)

    w_out_grad = lax.dot_general(
        branch_grad, gated_norm, (((0,), (0,)), ((), ())), preferred_element_type=F32
    )
    (w_out_grad,) = backward.chip_total(w_out_grad)
    w_gate_grad = lax.dot_general(
        normed, after(gate_grad, backward.total), (((0,), (0,)), ((), ())), preferred_element_type=F32
    )
    branch = lax.dot_general(
        after(gated_norm, backward.total), w_out_turned, NT, preferred_element_type=F32
    )
    block_out = (residual + keep[..., None] * branch.reshape(slots, tokens, D)).astype(BF16)
    w_gate_grad, block_out = backward.first_hop(w_gate_grad, block_out)
    back_owned = lax.psum_scatter(
        jnp.concatenate([w_gate_grad, w_out_grad], axis=1), axes, scatter_dimension=0, tiled=True
    )
    w_gate_owned, w_out_owned = back_owned[:, :DI], back_owned[:, DI:]

    xadj, bc_grad = call(
        adjoint_kernel,
        grid,
        specs(
            tile(CONV_CH), tile(LANES), tile(LANES), per_block(8, LANES), tile(DI),
            per_block(STATE, DI), per_slot(STATE, DI), per_block(STATE, DI),
        ),
        [tile(DI), tile(2 * STATE)],
        [],
        30 * rows * T * DI,
        rows * (CONV_CH + 4 * DI) * 4,
    )(
        act, log, step, aux, after(mixed_grad, backward.tail), enter, start, adj_enter,
    )
    (xadj,) = backward.last_hops(xadj)
    normed_grad = lax.dot_general(
        after(gate_grad, backward.window), w_gate, NT, preferred_element_type=F32
    )
    end_adj, normed_grad = backward.result(normed_grad)

    end_state = lanes_of(logs) * start + final
    tail = jnp.sum(end_adj * end_state, axis=1).reshape(slots, HEADS, HEADDIM).sum(-1)
    tail = jnp.broadcast_to(jnp.pad(tail, ((0, 0), (0, LANES - HEADS)))[:, None], (slots, 8, LANES))
    wide = CONV_CH + LANES
    prev = pl.BlockSpec(
        (1, 16, CONV_CH), lambda s, c: (s, jnp.maximum((blocks - 1 - c) * (T // 16) - 1, 0), 0)
    )
    proj_grad, head_rows, last_rows, conv_sums, head_sums = call(
        finish_kernel,
        grid,
        specs(
            tile(CONV_CH, flip_order=True), tile(LANES, flip_order=True), tile(LANES, flip_order=True),
            per_block(8, LANES, True), per_slot(8, LANES), tile(DI, flip_order=True),
            tile(DI, flip_order=True), tile(2 * STATE, flip_order=True), tile(LANES, flip_order=True),
            per_slot(STATE, DI), tile(CONV_CH, flip_order=True), (prev, None), per_slot(8, CONV_CH),
            tile(LANES, flip_order=True), per_slot(8, LANES), fixed(8, CONV_CH), fixed(8, LANES),
            fixed(8, DI), fixed(DI, LANES),
        ),
        [
            tile(wide, BF16, True), per_slot(8, CONV_CH), per_slot(8, CONV_CH),
            fixed(40, CONV_CH), fixed(16, LANES),
        ],
        [
            pltpu.VMEM((T + 16, CONV_CH), F32), pltpu.VMEM((T + 8, CONV_CH), F32),
            pltpu.VMEM((T, DI), BF16), pltpu.VMEM((T, DI), BF16), pltpu.VMEM((8, LANES), F32),
        ],
        12 * rows * STATE * DI,
        rows * (CONV_CH * 8 + DI * 8),
    )(
        act, log, step, aux, total, mixed_grad, xadj, bc_grad, lg, end_adj, conv_in, conv_in, halo,
        step_raw, tail, taps_rows, heads_rows, gain_rows, select,
    )

    ahead = shifted(head_rows, "seq", -1)
    ahead = jnp.concatenate([jnp.zeros((slots, 8, CONV_CH), F32), ahead], axis=1)
    for tap in range(CONV):
        begin = CONV - 1 - tap
        last_rows = last_rows + ahead[:, begin : begin + 8] * taps_full[tap]
    proj_grad = lax.dynamic_update_slice(
        proj_grad, last_rows.astype(BF16), (0, tokens - 8, 0)
    ).reshape(rows, wide)

    w_front_grad = lax.dot_general(
        normed, proj_grad, (((0,), (0,)), ((), ())), preferred_element_type=F32
    )
    w_front_owned = scatter_sum(w_front_grad, axes, thirds(wide))
    w_front = jnp.concatenate([w_conv, w_dt], axis=1)
    normed_grad = normed_grad + lax.dot_general(after(proj_grad, w_front_grad), w_front, NT, preferred_element_type=F32)
    normed_grad = normed_grad.reshape(slots, tokens, D)
    g_norm_grad = jnp.sum(normed_grad * residual * inv_rms, axis=(0, 1))
    scaled_in = normed_grad * norm_gain
    input_grad = cotangent + inv_rms * (
        scaled_in
        - residual * inv_rms * inv_rms * jnp.mean(scaled_in * residual, axis=-1, keepdims=True)
    )

    sums = conv_sums.reshape(CONV + 1, 8, CONV_CH).sum(1)
    d_skip_grad = gate_sums[8:].sum(0).reshape(HEADS, HEADDIM).sum(-1)
    head_grads = head_sums.reshape(2, 8, LANES).sum(1)[:, :HEADS]
    vectors = jnp.concatenate(
        [
            sums.reshape(-1), g_norm_grad, gate_sums[:8].sum(0), head_grads.reshape(-1), d_skip_grad,
        ]
    )
    count = vectors.shape[0]
    vectors = jnp.pad(vectors, (0, -count % 1024)).reshape(-1, LANES)
    vectors = total_sum(vectors, axes).reshape(-1)
    me = lax.axis_index("dp") * lax.axis_size("seq") + lax.axis_index("seq")

    def owned(begin, length):
        per = length // devices
        return lax.dynamic_slice_in_dim(vectors, begin + me * per, per)

    conv_w_grad = jnp.stack([owned(k * CONV_CH, CONV_CH) for k in range(CONV)])
    conv_b_grad = owned(CONV * CONV_CH, CONV_CH)
    at = (CONV + 1) * CONV_CH
    w_front_owned = w_front_owned[:, : CONV_CH + HEADS]
    heads_at = at + D + DI
    return (
        block_out,
        input_grad,
        jnp.concatenate([w_gate_owned, w_front_owned], axis=1),
        conv_w_grad,
        conv_b_grad,
        owned(at, D),
        owned(at + D, DI),
        w_out_owned.T,
        vectors[heads_at : heads_at + HEADS],
        vectors[heads_at + HEADS : heads_at + 2 * HEADS],
        vectors[heads_at + 2 * HEADS : heads_at + 3 * HEADS],
    )


def solution(mesh):
    placed = (
        P("dp", "seq", None),
        P("dp"),
        P(("dp", "seq"), None),
        P(None, ("dp", "seq")),
        P(("dp", "seq")),
        P(("dp", "seq")),
        P(("dp", "seq")),
        P(None, ("dp", "seq")),
        P(),
        P(),
        P(),
        P("dp", "seq", None),
    )
    return jax.shard_map(
        on_device,
        mesh=mesh,
        in_specs=placed,
        out_specs=(
            P("dp", "seq", None),
            P("dp", "seq", None),
            P(("dp", "seq"), None),
            P(None, ("dp", "seq")),
            P(("dp", "seq")),
            P(("dp", "seq")),
            P(("dp", "seq")),
            P(None, ("dp", "seq")),
            P(),
            P(),
            P(),
        ),
        check_vma=False,
    )
```

```python
import functools

import jax
import jax.numpy as jnp
from jax import lax
from jax.experimental import pallas as pl
from jax.experimental.pallas import tpu as pltpu
from jax.sharding import PartitionSpec as P

D = 768
HEADS = 24
HEADDIM = 64
STATE = 128
CONV = 4
DI = 1536
CONV_CH = 1792
PROJ = 3352
T = 128
PAIRS = HEADS // 2
LANES = 128
EPSILON = 1e-05
MASKED = -1e30
F32 = jnp.float32
BF16 = jnp.bfloat16
NN = (((1,), (0,)), ((), ()))
NT = (((1,), (1,)), ((), ()))


def mm(a, b, dims=NN):
    return lax.dot_general(a, b, dims, preferred_element_type=F32)


def split(v):
    high = v.astype(BF16)
    return high, (v - high.astype(F32)).astype(BF16)


def mm3(a, b, dims=NN):
    return mm(a[0], b[0], dims) + (mm(a[0], b[1], dims) + mm(a[1], b[0], dims))


def left_half(rows):
    return lax.broadcasted_iota(jnp.int32, (rows, LANES), 1) < HEADDIM


def spread(values, pair, left):
    return jnp.where(
        left, values[:, 2 * pair : 2 * pair + 1], values[:, 2 * pair + 1 : 2 * pair + 2]
    )


def cols(j):
    return slice(j * LANES, (j + 1) * LANES)


def running(v, reverse):
    row = lax.broadcasted_iota(jnp.int32, v.shape, 0)
    hop = 1
    while hop < T:
        moved = pltpu.roll(v, T - hop if reverse else hop, 0)
        inside = row < T - hop if reverse else row >= hop
        v = v + jnp.where(inside, moved, 0.0)
        hop *= 2
    return v


def fold(v):
    return jnp.sum(v.reshape(v.shape[0] // 8, 8, v.shape[-1]), axis=0)


def two_heads(high, low, left):
    zero = jnp.zeros_like(high)
    top = jnp.concatenate([jnp.where(left, high, zero), jnp.where(left, low, zero)], axis=1)
    bottom = jnp.concatenate([jnp.where(left, zero, high), jnp.where(left, zero, low)], axis=1)
    return jnp.concatenate([top, bottom], axis=0)


def sigmoid(v):
    return 0.5 * jnp.tanh(0.5 * v) + 0.5


def convolve(window, taps_ref, j, first):
    at = cols(j)
    total = taps_ref[CONV : CONV + 1, at]
    rows = [window[j, first + tap : first + tap + T, :] for tap in range(CONV)]
    for tap in range(CONV):
        total = total + rows[tap] * taps_ref[tap : tap + 1, at]
    return total, rows


def states_kernel(
    conv_ref, halo_ref, dt_ref, taps_ref, heads_ref,
    x_ref, bc_ref, log_ref, step_ref, aux_ref, enter_ref, final_ref, total_ref,
    window, state, before,
):
    c = pl.program_id(1)

    @pl.when(c == 0)
    def _():
        for j in range(CONV_CH // LANES):
            window[j, 0:8, :] = halo_ref[0, :, cols(j)].astype(F32)
        state[...] = jnp.zeros_like(state)
        before[...] = jnp.zeros_like(before)

    for j in range(CONV_CH // LANES):
        window[j, 8 : 8 + T, :] = conv_ref[0, :, cols(j)].astype(F32)
        pre, _ = convolve(window, taps_ref, j, 8 - (CONV - 1))
        if j < PAIRS:
            x_ref[0, :, cols(j)] = pre * sigmoid(pre)
        else:
            bc_ref[0, :, cols(j - PAIRS)] = pre * sigmoid(pre)
        window[j, 0:8, :] = window[j, T : T + 8, :]

    step = jax.nn.softplus(dt_ref[0] + heads_ref[0:1, :])
    log = running(step * heads_ref[1:2, :], False)
    end = log[T - 1 : T, :]
    step_ref[0] = step
    log_ref[0] = log
    weight = jnp.exp(end - log) * step
    decay = jnp.exp(end)
    left = left_half(T)
    aux_ref[0, 0] = jnp.concatenate([before[0:1, :], end, jnp.zeros((6, LANES), F32)], axis=0)
    before[0:1, :] = before[0:1, :] + end
    b_turned = split(bc_ref[0, :, 0:STATE].T)
    for j in range(PAIRS):
        prior = state[:, cols(j)]
        enter_ref[0, 0, :, cols(j)] = prior
        fed = split(x_ref[0, :, cols(j)] * spread(weight, j, left))
        state[:, cols(j)] = prior * spread(decay, j, left[0:1]) + mm3(b_turned, fed)

    @pl.when(c == pl.num_programs(1) - 1)
    def _():
        final_ref[0] = state[...]
        total_ref[0] = before[...]


def local_kernel(x_ref, bc_ref, log_ref, step_ref, enter_ref, rows_ref, out_ref):
    log = log_ref[0]
    log_turned = log.T
    step = step_ref[0]
    grown = jnp.exp(log)
    left = left_half(T)
    row = lax.broadcasted_iota(jnp.int32, (T, T), 0)
    col = lax.broadcasted_iota(jnp.int32, (T, T), 1)
    causal = row >= col
    b_pair = split(bc_ref[0, :, 0:STATE])
    c_pair = split(bc_ref[0, :, STATE:])
    inner = mm3(c_pair, b_pair, NT)
    for j in range(PAIRS):
        x = x_ref[0, :, cols(j)]
        fed = split(x * spread(step, j, left))
        rhs = two_heads(fed[0], fed[1], left)
        mats = []
        for head in (2 * j, 2 * j + 1):
            gap = log[:, head : head + 1] - log_turned[head : head + 1, :]
            mats.append(inner * jnp.exp(jnp.where(causal, gap, MASKED)))
        mixing = split(jnp.concatenate(mats, axis=1))
        wide = mm(mixing[0], rhs)
        out = wide[:, :LANES] + (wide[:, LANES:] + mm(mixing[1], rhs[:, :LANES]))
        crossed = mm3(c_pair, split(enter_ref[0, 0, :, cols(j)]))
        skipped = rows_ref[1:2, cols(j)] * x
        out_ref[0, :, cols(j)] = (out + skipped) + spread(grown, j, left) * crossed


def gate_kernel(
    c_ref, log_ref, aux_ref, local_ref, gate_ref, ng_ref, start_ref, rows_ref, sel_ref,
    normed_ref, mixed_grad_ref, gate_grad_ref, lg_ref, enter_ref, final_ref, sums_ref,
    mixed_s, gated_s, adj, q_high, q_low,
):
    s, c = pl.program_id(0), pl.program_id(1)

    @pl.when(c == 0)
    def _():
        adj[...] = jnp.zeros_like(adj)

    @pl.when((s == 0) & (c == 0))
    def _():
        sums_ref[...] = jnp.zeros_like(sums_ref)

    log = log_ref[0]
    before = aux_ref[0, 0, 0:1, :]
    end = aux_ref[0, 0, 1:2, :]
    left = left_half(T)
    since = jnp.exp(before + log)
    grown = jnp.exp(log)
    decay = jnp.exp(end)
    c_rows = c_ref[0]
    c_pair = split(c_rows)
    c_turned = split(c_rows.T)
    squares = jnp.zeros((T, LANES), F32)
    products = jnp.zeros((T, LANES), F32)
    for j in range(PAIRS):
        at = cols(j)
        crossed = mm3(c_pair, split(start_ref[0, :, at]))
        mixed = local_ref[0, :, at] + spread(since, j, left) * crossed
        gate = gate_ref[0, :, at]
        gated = mixed * (gate * sigmoid(gate))
        mixed_s[:, at] = mixed
        gated_s[:, at] = gated
        squares = squares + gated * gated
        products = products + ng_ref[0, :, at] * rows_ref[0:1, at] * gated
    inv = lax.rsqrt(jnp.sum(squares, axis=-1, keepdims=True) / DI + EPSILON)
    mean = jnp.sum(products, axis=-1, keepdims=True) / DI
    pull = inv * inv * mean
    for j in range(PAIRS):
        at = cols(j)
        mixed = mixed_s[:, at]
        gated = gated_s[:, at]
        gate = gate_ref[0, :, at]
        gain = rows_ref[0:1, at]
        ng = ng_ref[0, :, at]
        sig = sigmoid(gate)
        unit = gated * inv
        normed_ref[0, :, at] = (unit * gain).astype(BF16)
        sums_ref[:, at] = sums_ref[:, at] + fold(ng * unit)
        gated_grad = inv * (ng * gain - gated * pull)
        mixed_grad = gated_grad * (gate * sig)
        mixed_grad_ref[0, :, at] = mixed_grad
        gate_grad_ref[0, :, at] = (
            gated_grad * mixed * sig * (1.0 + gate * (1.0 - sig))
        ).astype(BF16)
        q = split(mixed_grad * mixed)
        q_high[:, at] = q[0]
        q_low[:, at] = q[1]
        prior = adj[:, at]
        enter_ref[0, 0, :, at] = prior
        fed = split(mixed_grad * spread(grown, j, left))
        adj[:, at] = prior * spread(decay, j, left[0:1]) + mm3(c_turned, fed)
    lg_ref[0] = mm(q_high[...], sel_ref[...]) + mm(q_low[...], sel_ref[...])

    @pl.when(c == pl.num_programs(1) - 1)
    def _():
        final_ref[0] = adj[...]


def adjoint_kernel(
    x_ref, bc_ref, log_ref, step_ref, aux_ref, grad_ref, enter_ref, start_ref, adj_ref, sel_ref,
    xadj_ref, bc_grad_ref, skip_ref,
    q_high, q_low,
):
    log = log_ref[0]
    log_turned = log.T
    step = step_ref[0]
    before = aux_ref[0, 0, 0:1, :]
    end = aux_ref[0, 0, 1:2, :]
    left = left_half(T)
    row = lax.broadcasted_iota(jnp.int32, (T, T), 0)
    col = lax.broadcasted_iota(jnp.int32, (T, T), 1)
    later = col >= row
    b_pair = split(bc_ref[0, :, 0:STATE])
    c_pair = split(bc_ref[0, :, STATE:])
    inner = mm3(b_pair, c_pair, NT)
    grown = jnp.exp(log)
    to_end = jnp.exp(end - log)
    reach = jnp.exp(before)
    weighted = jnp.zeros((T, T), F32)
    b_total = jnp.zeros((T, STATE), F32)
    c_total = jnp.zeros((T, STATE), F32)
    for j in range(PAIRS):
        at = cols(j)
        grad = grad_ref[0, :, at]
        x = x_ref[0, :, at]
        q = split(x * grad)
        q_high[:, at] = q[0]
        q_low[:, at] = q[1]
        fed = x * spread(step, j, left)
        high, low = split(grad)
        rhs = two_heads(high, low, left)
        decays = []
        for head in (2 * j, 2 * j + 1):
            gap = log_turned[head : head + 1, :] - log[:, head : head + 1]
            decays.append(jnp.exp(jnp.where(later, gap, MASKED)))
        mixing = split(jnp.concatenate([inner * decays[0], inner * decays[1]], axis=1))
        wide = mm(mixing[0], rhs)
        out = wide[:, :LANES] + (wide[:, LANES:] + mm(mixing[1], rhs[:, :LANES]))
        short = fed.astype(BF16)
        zero = jnp.zeros_like(short)
        stacked = jnp.concatenate(
            [jnp.where(left, short, zero), jnp.where(left, zero, short)], axis=0
        )
        dots = mm(stacked, high, NT)
        weighted = weighted + (decays[0] * dots[:T] + decays[1] * dots[T:])
        adj = split(adj_ref[0, 0, :, at])
        reached = spread(to_end, j, left)
        xadj_ref[0, :, at] = out + reached * mm3(b_pair, adj)
        b_total = b_total + mm((fed * reached).astype(BF16), adj[0], NT)
        entering = enter_ref[0, 0, :, at] + spread(reach, j, left[0:1]) * start_ref[0, :, at]
        c_total = c_total + mm3(split(grad * spread(grown, j, left)), split(entering), NT)
    skip_ref[0] = mm(q_high[...], sel_ref[...]) + mm(q_low[...], sel_ref[...])
    bc_grad_ref[0, :, 0:STATE] = b_total + mm(weighted.astype(BF16), c_pair[0])
    bc_grad_ref[0, :, STATE:] = c_total + mm(weighted.T.astype(BF16), b_pair[0])


def finish_kernel(
    x_ref, bc_ref, log_ref, step_ref, aux_ref, total_ref, grad_ref, xadj_ref, bc_grad_ref, lg_ref,
    skip_ref, end_ref, conv_ref, prev_ref, halo_ref, dt_ref, tail_ref, taps_ref, heads_ref, rows_ref,
    sel_ref,
    out_ref, head_ref, last_ref, sums_ref, head_sums_ref,
    window, pre_s, last_s, q_high, q_low, carry,
):
    slices = CONV_CH // LANES
    s, c = pl.program_id(0), pl.program_id(1)
    first = c == pl.num_programs(1) - 1

    @pl.when(c == 0)
    def _():
        pre_s[:, T : T + 8, :] = jnp.zeros((slices, 8, LANES), F32)
        carry[...] = tail_ref[0]

    @pl.when((s == 0) & (c == 0))
    def _():
        sums_ref[...] = jnp.zeros_like(sums_ref)
        head_sums_ref[...] = jnp.zeros_like(head_sums_ref)

    @pl.when(first)
    def _():
        for j in range(slices):
            window[j, 8:16, :] = halo_ref[0, :, cols(j)].astype(F32)

    @pl.when(jnp.logical_not(first))
    def _():
        for j in range(slices):
            window[j, 8:16, :] = prev_ref[0, :, cols(j)].astype(F32)[8:16, :]

    log = log_ref[0]
    step = step_ref[0]
    before = aux_ref[0, 0, 0:1, :]
    end = aux_ref[0, 0, 1:2, :]
    left = left_half(T)
    remain = jnp.exp((total_ref[0, 0:1, :] - before - end) + (end - log))
    b_pair = split(bc_ref[0, :, 0:STATE])
    b_total = bc_grad_ref[0, :, 0:STATE]

    def through(j, act_grad):
        at = cols(j)
        window[j, 16 : 16 + T, :] = conv_ref[0, :, cols(j)].astype(F32)
        pre, before_rows = convolve(window, taps_ref, j, 16 - (CONV - 1))
        sig = sigmoid(pre)
        pre_grad = act_grad * sig * (1.0 + pre * (1.0 - sig))
        pre_s[j, 0:T, :] = pre_grad
        for tap in range(CONV):
            rows = slice(8 * tap, 8 * tap + 8)
            sums_ref[rows, at] = sums_ref[rows, at] + fold(pre_grad * before_rows[tap])
        sums_ref[32:40, at] = sums_ref[32:40, at] + fold(pre_grad)
        into = pre_grad * taps_ref[CONV - 1 : CONV, cols(j)]
        for tap in range(CONV - 1):
            ahead = CONV - 1 - tap
            into = into + pre_s[j, ahead : ahead + T, :] * taps_ref[tap : tap + 1, cols(j)]
        out_ref[0, :, at] = into.astype(BF16)
        last_s[:, at] = into[T - 8 :, :]
        pre_s[j, T : T + 8, :] = pre_grad[0:8, :]

    for j in range(PAIRS):
        at = cols(j)
        x = x_ref[0, :, at]
        stepped = spread(step, j, left)
        left_over = spread(remain, j, left)
        end_pair = split(end_ref[0, :, at])
        xadj = xadj_ref[0, :, at] + left_over * mm3(b_pair, end_pair)
        b_total = b_total + mm((x * stepped * left_over).astype(BF16), end_pair[0], NT)
        q = split(x * xadj)
        q_high[:, at] = q[0]
        q_low[:, at] = q[1]
        through(j, stepped * xadj + rows_ref[1:2, at] * grad_ref[0, :, at])
    through(PAIRS, b_total)
    through(PAIRS + 1, bc_grad_ref[0, :, STATE:])

    direct = mm(q_high[...], sel_ref[...]) + mm(q_low[...], sel_ref[...])
    skipped = skip_ref[0]
    log_grad = lg_ref[0] - heads_ref[2:3, :] * skipped - step * direct
    log_grad = running(log_grad, True) + carry[0:1, :]
    carry[0:1, :] = log_grad[0:1, :]
    rate = heads_ref[1:2, :]
    step_grad = direct + log_grad * rate
    step_pre_grad = step_grad * sigmoid(dt_ref[0] + heads_ref[0:1, :])
    out_ref[0, :, CONV_CH:] = step_pre_grad.astype(BF16)
    head_sums_ref[0:8, :] = head_sums_ref[0:8, :] + fold(log_grad * step * rate)
    head_sums_ref[8:16, :] = head_sums_ref[8:16, :] + fold(step_pre_grad)
    head_sums_ref[16:24, :] = head_sums_ref[16:24, :] + fold(skipped)

    @pl.when(c == 0)
    def _():
        last_ref[0] = last_s[...]

    @pl.when(first)
    def _():
        for j in range(slices):
            head_ref[0, :, cols(j)] = pre_s[j, 0:8, :]


def input_kernel(
    proj_ref, gate_ref, front_ref, w_gate_ref, hidden_ref, cot_ref, gain_ref, out_ref, sums_ref
):
    @pl.when(pl.program_id(0) == 0)
    def _():
        sums_ref[...] = jnp.zeros_like(sums_ref)

    x = hidden_ref[...].astype(F32)
    inv = lax.rsqrt(jnp.mean(x * x, axis=-1, keepdims=True) + EPSILON)
    unit = x * inv
    grad = mm(proj_ref[...], front_ref[...], NT) + mm(gate_ref[...], w_gate_ref[...], NT)
    sums_ref[...] = sums_ref[...] + fold(grad * unit)
    scaled = grad * gain_ref[0:1, :]
    mean = jnp.mean(scaled * unit, axis=-1, keepdims=True)
    out_ref[...] = cot_ref[...].astype(F32) + inv * (scaled - unit * mean)


def call(kernel, grid, ins, outs, scratch, flops, moved):
    return pl.pallas_call(
        kernel,
        grid=grid,
        in_specs=ins,
        out_specs=[spec for spec, _ in outs],
        out_shape=[shape for _, shape in outs],
        scratch_shapes=scratch,
        compiler_params=pltpu.CompilerParams(
            dimension_semantics=("arbitrary",) * len(grid), vmem_limit_bytes=56 * 2**20
        ),
        cost_estimate=pl.CostEstimate(flops=flops, bytes_accessed=moved, transcendentals=0),
    )


def flip(value, axis, bit):
    count = lax.axis_size(axis)
    return lax.ppermute(value, axis, [(i, i ^ bit) for i in range(count)])


def shifted(value, axis, steps):
    count = lax.axis_size(axis)
    initial, last = (max(0, -steps), min(count, count - steps))
    return lax.ppermute(value, axis, [(source, source + steps) for source in range(initial, last)])


def bits_of(axes):
    names = []
    for axis in axes:
        bit = lax.axis_size(axis) // 2
        while bit:
            names.append((axis, bit))
            bit //= 2
    return names


def my_bit(name):
    return (lax.axis_index(name[0]) // name[1]) % 2


def total_sum(value, axes):
    for name in bits_of(axes)[::-1]:
        value = value + flip(value, *name)
    return value


class ScatterSum:
    def __init__(self, value, axes):
        self.names = bits_of(axes)
        core = self.names[-1]
        width = value.shape[-1]
        a = value.reshape((2,) * len(self.names) + (-1, width))
        self.mine, self.sent = self.halves(a, len(self.names) - 1, core)
        self.arrived = flip(self.sent, *core)
        cut = width // LANES // 3 * LANES
        self.parts = [(0, cut), (cut, 2 * cut), (2 * cut, width)]

    def halves(self, a, d, name):
        b = my_bit(name)
        return (
            lax.dynamic_index_in_dim(a, b, d, False),
            lax.dynamic_index_in_dim(a, 1 - b, d, False),
        )

    def begin(self):
        rest = self.names[:-1]
        dp = [n for n in rest if n[0] == self.names[0][0]]
        seq = [n for n in rest if n[0] != self.names[0][0]]
        self.orders = [dp[::-1] + seq[::-1], dp + seq[::-1], seq[::-1] + dp]
        self.kept, self.got, sent = [], [], []
        for order, (begin, stop) in zip(self.orders, self.parts):
            a = self.mine[..., begin:stop] + self.arrived[..., begin:stop]
            mine, other = self.halves(a, rest.index(order[0]), order[0])
            self.kept.append(mine)
            sent.append(other)
        sent = lax.optimization_barrier(tuple(sent))
        self.got = [flip(other, *order[0]) for other, order in zip(sent, self.orders)]
        return sent

    def finish(self, *beside):
        *self.got, beside = lax.optimization_barrier((*self.got, beside))
        pieces = []
        for order, kept, got in zip(self.orders, self.kept, self.got):
            live = [name for name in self.names[:-1] if name != order[0]]
            a = kept + got
            for name in order[1:]:
                d = live.index(name)
                mine, other = self.halves(a, d, name)
                a = mine + flip(other, *name)
                live.pop(d)
            pieces.append(a)
        return jnp.concatenate(pieces, axis=-1), beside


def after(value, *others):
    return lax.optimization_barrier((value,) + others)[0]


def in_order(blocks, me):
    bit = 1
    while bit < len(blocks):
        swap = (me // bit) % 2 == 1
        blocks = [jnp.where(swap, blocks[i ^ bit], block) for i, block in enumerate(blocks)]
        bit *= 2
    return jnp.stack(blocks)


def gather(value):
    seq, dp = lax.axis_size("seq"), lax.axis_size("dp")
    me = lax.axis_index("seq")
    chips = [value] + [flip(value, "seq", 2 * hop) for hop in range(1, seq // 2)]
    held = in_order(chips, me // 2)
    held = in_order(
        [held] + [flip(held, "dp", hop) for hop in range(1, dp)], lax.axis_index("dp")
    )
    other = flip(held, "seq", 1)
    even = me % 2 == 0
    both = jnp.stack([jnp.where(even, held, other), jnp.where(even, other, held)], axis=2)
    return both.reshape(-1, value.shape[1])


def lanes_of(log_decay):
    return jnp.repeat(jnp.exp(log_decay[:, :HEADS]), HEADDIM, axis=1)[:, None, :]


class Entering:
    def __init__(self, state, logs, axis, reverse):
        self.axis = axis
        self.sign = -1 if reverse else 1
        self.state, self.logs = state, logs
        self.odd = lax.axis_index(axis) % 2
        self.late = self.odd == (0 if reverse else 1)
        self.partner = flip(state, axis, 1)
        self.partner_logs = flip(logs, axis, 1)
        self.chips = lax.axis_size(axis) // 2

    def half(self, value):
        return lax.dynamic_slice_in_dim(value, self.odd * (DI // 2), DI // 2, 2)

    def chip_total(self, *beside):
        self.partner, *beside = lax.optimization_barrier((self.partner,) + beside)
        here, there = self.half(self.state), self.half(self.partner)
        decay_here = self.half(lanes_of(self.logs))
        decay_there = self.half(lanes_of(self.partner_logs))
        total = jnp.where(self.late, decay_here * there + here, decay_there * here + there)
        self.total, self.decay = total, decay_here * decay_there
        self.got = shifted(total, self.axis, 2 * self.sign)
        return beside

    def first_hop(self, *beside):
        self.window, *beside = lax.optimization_barrier((self.got,) + beside)
        self.window_decay = shifted(self.decay, self.axis, 2 * self.sign)
        self.tail = self.decay * self.window + self.total
        self.tail_decay = self.decay * self.window_decay
        return beside

    def last_hops(self, *beside):
        hop = 2
        while hop < self.chips:
            got = shifted(self.tail, self.axis, 2 * self.sign * hop)
            if hop == 2:
                got, *beside = lax.optimization_barrier((got,) + beside)
            got_decay = shifted(self.tail_decay, self.axis, 2 * self.sign * hop)
            self.window = self.window_decay * got + self.window
            self.window_decay = self.window_decay * got_decay
            hop *= 2
            if hop < self.chips:
                self.tail = self.tail_decay * got + self.tail
                self.tail_decay = self.tail_decay * got_decay
        self.whole = flip(self.window, self.axis, 1)
        return beside

    def result(self, *beside):
        self.whole, *beside = lax.optimization_barrier((self.whole,) + beside)
        both = jnp.where(
            self.odd == 0,
            jnp.concatenate([self.window, self.whole], axis=2),
            jnp.concatenate([self.whole, self.window], axis=2),
        )
        state = jnp.where(self.late, lanes_of(self.partner_logs) * both + self.partner, both)
        return [state] + beside


def on_device(
    hidden_in,
    lengths,
    w_in,
    conv_w,
    conv_b,
    g_norm,
    g_gate,
    w_out,
    a_log,
    dt_bias,
    d_skip,
    out_cotangent,
):
    axes = ("dp", "seq")
    devices = lax.axis_size("dp") * lax.axis_size("seq")
    slots, tokens, _ = hidden_in.shape
    blocks = tokens // T
    rows = slots * tokens
    grid = (slots, blocks)
    share = D // devices

    small = jnp.concatenate(
        [conv_w.reshape(-1), conv_b, g_norm, g_gate], axis=0
    )
    per_row = -(-small.shape[0] // share)
    small = jnp.pad(small, (0, per_row * share - small.shape[0])).reshape(share, per_row)
    front = jnp.concatenate([w_in[:, DI:], small], axis=1)
    front_full = gather(front)
    w_conv = front_full[:, :CONV_CH]
    w_dt = jnp.pad(front_full[:, CONV_CH : CONV_CH + HEADS], ((0, 0), (0, LANES - HEADS)))
    extra = front_full[:, CONV_CH + HEADS :].reshape(devices, -1)
    lane = CONV_CH // devices
    taps_full = jnp.moveaxis(extra[:, : CONV * lane].reshape(devices, CONV, lane), 0, 1)
    taps_full = taps_full.reshape(CONV, CONV_CH).astype(F32)
    at = CONV * lane
    bias_full = extra[:, at : at + lane].reshape(1, CONV_CH).astype(F32)
    at += lane
    norm_gain = extra[:, at : at + share].reshape(D).astype(F32)
    at += share
    gate_gain = extra[:, at : at + DI // devices].reshape(1, DI).astype(F32)
    back = jnp.concatenate([w_in[:, :DI], w_out.T], axis=1)
    back = lax.all_gather(back, axes, axis=0, tiled=True)
    w_gate, w_out_turned = lax.optimization_barrier((back[:, :DI], back[:, DI:]))

    taps_rows = jnp.concatenate([taps_full, bias_full, jnp.zeros((3, CONV_CH), F32)], axis=0)
    rate = -jnp.exp(a_log)
    heads_rows = jnp.pad(jnp.stack([dt_bias, rate, d_skip]), ((0, 5), (0, LANES - HEADS)))
    skip_row = jnp.repeat(d_skip, HEADDIM)[None]
    gain_rows = jnp.concatenate([gate_gain, skip_row, jnp.zeros((6, DI), F32)], axis=0)
    select = (
        jnp.arange(DI, dtype=jnp.int32)[:, None] // HEADDIM
        == jnp.arange(LANES, dtype=jnp.int32)[None]
    ).astype(BF16)

    place = lax.axis_index("seq") * tokens + jnp.arange(tokens, dtype=jnp.int32)
    keep = (place[None, :] < lengths[:, None]).astype(F32)
    residual = hidden_in.astype(F32)
    inv_rms = lax.rsqrt(jnp.mean(residual * residual, axis=-1, keepdims=True) + EPSILON)
    normed = (residual * inv_rms * norm_gain).astype(BF16).reshape(rows, D)
    conv_in = jnp.dot(normed, w_conv, preferred_element_type=F32).astype(BF16)
    conv_in = conv_in.reshape(slots, tokens, CONV_CH)
    step_raw = jnp.dot(normed, w_dt, preferred_element_type=F32).reshape(slots, tokens, LANES)
    halo = shifted(conv_in[:, tokens - 8 :, :], "seq", 1)

    def tile(width, dtype=F32, flip_order=False, height=T):
        if flip_order:
            spec = pl.BlockSpec((1, height, width), lambda s, c: (s, blocks - 1 - c, 0))
        else:
            spec = pl.BlockSpec((1, height, width), lambda s, c: (s, c, 0))
        return spec, jax.ShapeDtypeStruct((slots, tokens, width), dtype)

    def per_block(height, width, flip_order=False):
        if flip_order:
            spec = pl.BlockSpec((1, 1, height, width), lambda s, c: (s, blocks - 1 - c, 0, 0))
        else:
            spec = pl.BlockSpec((1, 1, height, width), lambda s, c: (s, c, 0, 0))
        return spec, jax.ShapeDtypeStruct((slots, blocks, height, width), F32)

    def columns(width, whole, index):
        spec = pl.BlockSpec((1, T, width), lambda s, c: (s, blocks - 1 - c, index))
        return spec, jax.ShapeDtypeStruct((slots, tokens, whole), F32)

    def per_slot(height, width, index=0):
        spec = pl.BlockSpec((1, height, width), lambda s, c: (s, 0, index))
        return spec, jax.ShapeDtypeStruct((slots, height, width), F32)

    def fixed(height, width):
        spec = pl.BlockSpec((height, width), lambda s, c: (0, 0))
        return spec, jax.ShapeDtypeStruct((height, width), F32)

    def specs(*pairs):
        return [spec for spec, _ in pairs]

    x, bc, log, step, aux, enter, final, total = call(
        states_kernel,
        grid,
        specs(tile(CONV_CH), per_slot(8, CONV_CH), tile(LANES), fixed(8, CONV_CH), fixed(8, LANES)),
        [
            tile(DI), tile(2 * STATE), tile(LANES), tile(LANES), per_block(8, LANES),
            per_block(STATE, DI), per_slot(STATE, DI), per_slot(8, LANES),
        ],
        [pltpu.VMEM((CONV_CH // LANES, T + 8, LANES), F32), pltpu.VMEM((STATE, DI), F32), pltpu.VMEM((8, LANES), F32)],
        6 * rows * STATE * DI,
        rows * (CONV_CH * 6 + DI * 4),
    )(conv_in, halo, step_raw, taps_rows, heads_rows)
    logs = total[:, 0, :]
    forward = Entering(final, logs, "seq", False)
    gate_pre = jnp.dot(after(normed, final), w_gate, preferred_element_type=F32)
    (gate_pre,) = forward.chip_total(gate_pre.reshape(slots, tokens, DI))
    cotangent = out_cotangent.astype(F32)
    branch_grad = (cotangent * keep[..., None]).astype(BF16).reshape(rows, D)
    norm_grad = jnp.dot(
        after(branch_grad, forward.total), w_out_turned, preferred_element_type=F32
    )
    (norm_grad,) = forward.first_hop(norm_grad.reshape(slots, tokens, DI))
    (local,) = call(
        local_kernel,
        grid,
        specs(
            tile(DI), tile(2 * STATE), tile(LANES), tile(LANES), per_block(STATE, DI), fixed(8, DI)
        ),
        [tile(DI)],
        [],
        12 * rows * T * DI,
        rows * (CONV_CH + 2 * DI) * 4,
    )(after(x, forward.tail), bc, log, step, enter, gain_rows)
    (local,) = forward.last_hops(local)
    (start,) = forward.result()

    gated_norm, mixed_grad, gate_grad, lg, adj_enter, adj_final, gate_sums = call(
        gate_kernel,
        grid,
        specs(
            columns(STATE, 2 * STATE, 1), tile(LANES, flip_order=True),
            per_block(8, LANES, True), tile(DI, flip_order=True), tile(DI, flip_order=True),
            tile(DI, flip_order=True), per_slot(STATE, DI), fixed(8, DI), fixed(DI, LANES),
        ),
        [
            tile(DI, BF16, True), tile(DI, F32, True), tile(DI, BF16, True),
            tile(LANES, F32, True), per_block(STATE, DI, True), per_slot(STATE, DI), fixed(8, DI),
        ],
        [
            pltpu.VMEM((T, DI), F32), pltpu.VMEM((T, DI), F32), pltpu.VMEM((STATE, DI), F32),
            pltpu.VMEM((T, DI), BF16), pltpu.VMEM((T, DI), BF16),
        ],
        12 * rows * STATE * DI,
        rows * (CONV_CH * 4 + DI * 24),
    )(bc, log, aux, local, gate_pre, norm_grad, start, gain_rows, select)
    gated_norm = gated_norm.reshape(rows, DI)
    gate_grad = gate_grad.reshape(rows, DI)
    backward = Entering(adj_final, logs, "seq", True)

    w_out_grad = lax.dot_general(
        branch_grad, gated_norm, (((0,), (0,)), ((), ())), preferred_element_type=F32
    )
    (w_out_grad,) = backward.chip_total(w_out_grad)
    w_gate_grad = lax.dot_general(
        normed, after(gate_grad, backward.total), (((0,), (0,)), ((), ())), preferred_element_type=F32
    )
    branch = lax.dot_general(
        after(gated_norm, backward.total), w_out_turned, NT, preferred_element_type=F32
    )
    block_out = (residual + keep[..., None] * branch.reshape(slots, tokens, D)).astype(BF16)
    early = jnp.zeros((D, 2 * DI), F32)
    early = lax.dynamic_update_slice(early, w_out_grad, (0, DI))
    early = lax.dynamic_update_slice(early, w_gate_grad, (0, 0))
    early, block_out = backward.first_hop(early, block_out)
    back_owned = lax.psum_scatter(
        early, axes, scatter_dimension=0, tiled=True
    )
    w_gate_owned, w_out_owned = back_owned[:, :DI], back_owned[:, DI:]

    xadj, bc_grad, skipped = call(
        adjoint_kernel,
        grid,
        specs(
            tile(DI), tile(2 * STATE), tile(LANES), tile(LANES), per_block(8, LANES), tile(DI),
            per_block(STATE, DI), per_slot(STATE, DI), per_block(STATE, DI), fixed(DI, LANES),
        ),
        [tile(DI), tile(2 * STATE), tile(LANES)],
        [pltpu.VMEM((T, DI), BF16), pltpu.VMEM((T, DI), BF16)],
        30 * rows * T * DI,
        rows * (CONV_CH + 4 * DI) * 4,
    )(
        x, bc, log, step, aux, after(mixed_grad, backward.tail), enter, start, adj_enter, select
    )
    (xadj,) = backward.last_hops(xadj)
    (end_adj,) = backward.result()

    end_state = lanes_of(logs) * start + final
    tail = jnp.sum(end_adj * end_state, axis=1).reshape(slots, HEADS, HEADDIM).sum(-1)
    tail = jnp.broadcast_to(jnp.pad(tail, ((0, 0), (0, LANES - HEADS)))[:, None], (slots, 8, LANES))
    prev = pl.BlockSpec(
        (1, 16, CONV_CH), lambda s, c: (s, jnp.maximum((blocks - 1 - c) * (T // 16) - 1, 0), 0)
    )
    def flipped(width, dtype=F32):
        return tile(width, dtype, True)

    wide = CONV_CH + LANES
    slices = CONV_CH // LANES
    proj_grad, head_rows, last_rows, conv_sums, head_sums = call(
        finish_kernel,
        grid,
        specs(
            flipped(DI), flipped(2 * STATE), flipped(LANES), flipped(LANES),
            per_block(8, LANES, True), per_slot(8, LANES), flipped(DI), flipped(DI),
            flipped(2 * STATE), flipped(LANES), flipped(LANES), per_slot(STATE, DI),
            flipped(CONV_CH), (prev, None), per_slot(8, CONV_CH), flipped(LANES),
            per_slot(8, LANES), fixed(8, CONV_CH), fixed(8, LANES), fixed(8, DI), fixed(DI, LANES),
        ),
        [
            flipped(wide, BF16), per_slot(8, CONV_CH), per_slot(8, CONV_CH), fixed(40, CONV_CH),
            fixed(24, LANES),
        ],
        [
            pltpu.VMEM((slices, T + 16, LANES), F32), pltpu.VMEM((slices, T + 8, LANES), F32),
            pltpu.VMEM((8, CONV_CH), F32), pltpu.VMEM((T, DI), BF16), pltpu.VMEM((T, DI), BF16),
            pltpu.VMEM((8, LANES), F32),
        ],
        12 * rows * STATE * DI,
        rows * (CONV_CH * 8 + DI * 8),
    )(
        x, bc, log, step, aux, total, mixed_grad, xadj, bc_grad, lg, skipped, end_adj, conv_in,
        conv_in, halo, step_raw, tail, taps_rows, heads_rows, gain_rows, select,
    )

    ahead = shifted(head_rows, "seq", -1)
    ahead = jnp.concatenate([jnp.zeros((slots, 8, CONV_CH), F32), ahead], axis=1)
    for tap in range(CONV):
        begin = CONV - 1 - tap
        last_rows = last_rows + ahead[:, begin : begin + 8] * taps_full[tap]
    proj_grad = lax.dynamic_update_slice(
        proj_grad, last_rows.astype(BF16), (0, tokens - 8, 0)
    ).reshape(rows, wide)

    sums = conv_sums.reshape(CONV + 1, 8, devices, lane).sum(1)
    gate_gain_grad = gate_sums.reshape(8, devices, -1).sum(0)
    head_grads = head_sums.reshape(3, 8, LANES).sum(1)[:, :HEADS].reshape(1, -1)
    vectors = jnp.concatenate(
        [
            jnp.moveaxis(sums, 1, 0).reshape(devices, -1), gate_gain_grad,
            jnp.broadcast_to(head_grads, (devices, 3 * HEADS)),
        ],
        axis=1,
    )
    count = vectors.shape[1]
    spare = -(-count // share)
    vectors = jnp.pad(vectors, ((0, 0), (0, spare * share - count))).reshape(D, spare)

    def weight_grad(grad):
        return lax.dot_general(normed, grad, (((0,), (0,)), ((), ())), preferred_element_type=F32)

    w_front_grad = lax.dynamic_update_slice(
        weight_grad(proj_grad), vectors, (0, CONV_CH + HEADS)
    )
    scatter = ScatterSum(w_front_grad, axes)
    w_front = jnp.concatenate([w_conv, w_dt], axis=1)
    tall = 2 * T

    def strip(width, dtype=BF16):
        spec = pl.BlockSpec((tall, width), lambda r: (r, 0))
        return spec, jax.ShapeDtypeStruct((rows, width), dtype)

    def whole(height, width):
        spec = pl.BlockSpec((height, width), lambda r: (0, 0))
        return spec, jax.ShapeDtypeStruct((height, width), F32)

    input_grad, norm_sums = call(
        input_kernel,
        (rows // tall,),
        specs(
            strip(wide), strip(DI), whole(D, wide), whole(D, DI), strip(D), strip(D), whole(1, D)
        ),
        [strip(D, F32), whole(8, D)],
        [],
        2 * rows * D * (wide + DI),
        rows * (wide + DI) * 2 + rows * D * 8,
    )(
        after(proj_grad, *scatter.begin()), gate_grad, w_front, w_gate, hidden_in.reshape(rows, D),
        out_cotangent.reshape(rows, D), norm_gain[None],
    )
    input_grad = input_grad.reshape(slots, tokens, D)
    me = lax.axis_index("dp") * lax.axis_size("seq") + lax.axis_index("seq")
    front_owned, (input_grad, norm_sums) = scatter.finish(input_grad, norm_sums)
    g_norm_grad = total_sum(norm_sums.sum(0).reshape(-1, LANES), axes).reshape(-1)
    g_norm_grad = lax.dynamic_slice_in_dim(g_norm_grad, me * share, share)
    front = CONV_CH + HEADS
    vectors = front_owned[:, front : front + spare].reshape(-1)
    at = CONV * lane
    gate_at = at + lane
    heads_at = gate_at + DI // devices
    return (
        block_out,
        input_grad,
        jnp.concatenate([w_gate_owned, front_owned[:, :front]], axis=1),
        vectors[:at].reshape(CONV, lane),
        vectors[at:gate_at],
        g_norm_grad,
        vectors[gate_at:heads_at],
        w_out_owned.T,
        vectors[heads_at : heads_at + HEADS],
        vectors[heads_at + HEADS : heads_at + 2 * HEADS],
        vectors[heads_at + 2 * HEADS : heads_at + 3 * HEADS],
    )


def solution(mesh):
    placed = (
        P("dp", "seq", None),
        P("dp"),
        P(("dp", "seq"), None),
        P(None, ("dp", "seq")),
        P(("dp", "seq")),
        P(("dp", "seq")),
        P(("dp", "seq")),
        P(None, ("dp", "seq")),
        P(),
        P(),
        P(),
        P("dp", "seq", None),
    )
    return jax.shard_map(
        on_device,
        mesh=mesh,
        in_specs=placed,
        out_specs=(
            P("dp", "seq", None),
            P("dp", "seq", None),
            P(("dp", "seq"), None),
            P(None, ("dp", "seq")),
            P(("dp", "seq")),
            P(("dp", "seq")),
            P(("dp", "seq")),
            P(None, ("dp", "seq")),
            P(),
            P(),
            P(),
        ),
        check_vma=False,
    )
```

```python
import functools

import jax
import jax.numpy as jnp
from jax import lax
from jax.experimental import pallas as pl
from jax.experimental.pallas import tpu as pltpu
from jax.sharding import PartitionSpec as P

D = 768
HEADS = 24
HEADDIM = 64
STATE = 128
CONV = 4
DI = 1536
CONV_CH = 1792
PROJ = 3352
T = 128
PAIRS = HEADS // 2
LANES = 128
EPSILON = 1e-05
MASKED = -1e30
F32 = jnp.float32
BF16 = jnp.bfloat16
NN = (((1,), (0,)), ((), ()))
NT = (((1,), (1,)), ((), ()))


def mm(a, b, dims=NN):
    return lax.dot_general(a, b, dims, preferred_element_type=F32)


def split(v):
    high = v.astype(BF16)
    return high, (v - high.astype(F32)).astype(BF16)


def mm3(a, b, dims=NN):
    return mm(a[0], b[0], dims) + (mm(a[0], b[1], dims) + mm(a[1], b[0], dims))


def left_half(rows):
    return lax.broadcasted_iota(jnp.int32, (rows, LANES), 1) < HEADDIM


def spread(values, pair, left):
    return jnp.where(
        left, values[:, 2 * pair : 2 * pair + 1], values[:, 2 * pair + 1 : 2 * pair + 2]
    )


def cols(j):
    return slice(j * LANES, (j + 1) * LANES)


def running(v, reverse):
    row = lax.broadcasted_iota(jnp.int32, v.shape, 0)
    hop = 1
    while hop < T:
        moved = pltpu.roll(v, T - hop if reverse else hop, 0)
        inside = row < T - hop if reverse else row >= hop
        v = v + jnp.where(inside, moved, 0.0)
        hop *= 2
    return v


def fold(v):
    return jnp.sum(v.reshape(v.shape[0] // 8, 8, v.shape[-1]), axis=0)


def two_heads(high, low, left):
    zero = jnp.zeros_like(high)
    top = jnp.concatenate([jnp.where(left, high, zero), jnp.where(left, low, zero)], axis=1)
    bottom = jnp.concatenate([jnp.where(left, zero, high), jnp.where(left, zero, low)], axis=1)
    return jnp.concatenate([top, bottom], axis=0)


def sigmoid(v):
    return 0.5 * jnp.tanh(0.5 * v) + 0.5


def convolve(window, taps_ref, j, first):
    at = cols(j)
    total = taps_ref[CONV : CONV + 1, at]
    rows = [window[j, first + tap : first + tap + T, :] for tap in range(CONV)]
    for tap in range(CONV):
        total = total + rows[tap] * taps_ref[tap : tap + 1, at]
    return total, rows


def states_kernel(
    hidden_ref, before_ref, front_ref, gain_ref, taps_ref, heads_ref,
    normed_ref, conv_ref, halo_ref, dt_ref, x_ref, bc_ref, log_ref, step_ref, aux_ref, enter_ref,
    final_ref, total_ref,
    window, state, before,
):
    c = pl.program_id(1)

    def norm(rows):
        rows = rows.astype(F32)
        inv = lax.rsqrt(jnp.mean(rows * rows, axis=-1, keepdims=True) + EPSILON)
        return (rows * inv * gain_ref[0:1, :]).astype(BF16)

    @pl.when(c == 0)
    def _():
        earlier = norm(before_ref[0])
        for j in range(CONV_CH // LANES):
            rows = mm(earlier, front_ref[:, cols(j)]).astype(BF16)
            halo_ref[0, :, cols(j)] = rows
            window[j, 0:8, :] = rows.astype(F32)
        state[...] = jnp.zeros_like(state)
        before[...] = jnp.zeros_like(before)

    normed = norm(hidden_ref[0])
    normed_ref[0] = normed
    for k in range(CONV_CH // LANES // 2):
        two = slice(2 * k * LANES, 2 * (k + 1) * LANES)
        rows = mm(normed, front_ref[:, two]).astype(BF16)
        conv_ref[0, :, two] = rows
        for j in (2 * k, 2 * k + 1):
            window[j, 8 : 8 + T, :] = rows[:, cols(j - 2 * k)].astype(F32)
            pre, _ = convolve(window, taps_ref, j, 8 - (CONV - 1))
            if j < PAIRS:
                x_ref[0, :, cols(j)] = pre * sigmoid(pre)
            else:
                bc_ref[0, :, cols(j - PAIRS)] = pre * sigmoid(pre)
            window[j, 0:8, :] = window[j, T : T + 8, :]

    dt = mm(normed, front_ref[:, CONV_CH : CONV_CH + LANES])
    dt_ref[0] = dt
    step = jax.nn.softplus(dt + heads_ref[0:1, :])
    log = running(step * heads_ref[1:2, :], False)
    end = log[T - 1 : T, :]
    step_ref[0] = step
    log_ref[0] = log
    weight = jnp.exp(end - log) * step
    decay = jnp.exp(end)
    left = left_half(T)
    aux_ref[0, 0] = jnp.concatenate([before[0:1, :], end, jnp.zeros((6, LANES), F32)], axis=0)
    before[0:1, :] = before[0:1, :] + end
    b_turned = split(bc_ref[0, :, 0:STATE].T)
    for j in range(PAIRS):
        prior = state[:, cols(j)]
        enter_ref[0, 0, :, cols(j)] = prior
        fed = split(x_ref[0, :, cols(j)] * spread(weight, j, left))
        state[:, cols(j)] = prior * spread(decay, j, left[0:1]) + mm3(b_turned, fed)

    @pl.when(c == pl.num_programs(1) - 1)
    def _():
        final_ref[0] = state[...]
        total_ref[0] = before[...]


def local_kernel(x_ref, bc_ref, log_ref, step_ref, enter_ref, rows_ref, out_ref):
    log = log_ref[0]
    log_turned = log.T
    step = step_ref[0]
    grown = jnp.exp(log)
    left = left_half(T)
    row = lax.broadcasted_iota(jnp.int32, (T, T), 0)
    col = lax.broadcasted_iota(jnp.int32, (T, T), 1)
    causal = row >= col
    b_pair = split(bc_ref[0, :, 0:STATE])
    c_pair = split(bc_ref[0, :, STATE:])
    inner = mm3(c_pair, b_pair, NT)
    for j in range(PAIRS):
        x = x_ref[0, :, cols(j)]
        fed = split(x * spread(step, j, left))
        rhs = two_heads(fed[0], fed[1], left)
        mats = []
        for head in (2 * j, 2 * j + 1):
            gap = log[:, head : head + 1] - log_turned[head : head + 1, :]
            mats.append(inner * jnp.exp(jnp.where(causal, gap, MASKED)))
        mixing = split(jnp.concatenate(mats, axis=1))
        wide = mm(mixing[0], rhs)
        out = wide[:, :LANES] + (wide[:, LANES:] + mm(mixing[1], rhs[:, :LANES]))
        crossed = mm3(c_pair, split(enter_ref[0, 0, :, cols(j)]))
        skipped = rows_ref[1:2, cols(j)] * x
        out_ref[0, :, cols(j)] = (out + skipped) + spread(grown, j, left) * crossed


def gate_kernel(
    c_ref, log_ref, aux_ref, local_ref, gate_ref, ng_ref, start_ref, rows_ref, sel_ref,
    normed_ref, mixed_grad_ref, gate_grad_ref, lg_ref, enter_ref, final_ref, sums_ref,
    mixed_s, gated_s, adj, q_high, q_low,
):
    s, c = pl.program_id(0), pl.program_id(1)

    @pl.when(c == 0)
    def _():
        adj[...] = jnp.zeros_like(adj)

    @pl.when((s == 0) & (c == 0))
    def _():
        sums_ref[...] = jnp.zeros_like(sums_ref)

    log = log_ref[0]
    before = aux_ref[0, 0, 0:1, :]
    end = aux_ref[0, 0, 1:2, :]
    left = left_half(T)
    since = jnp.exp(before + log)
    grown = jnp.exp(log)
    decay = jnp.exp(end)
    c_rows = c_ref[0]
    c_pair = split(c_rows)
    c_turned = split(c_rows.T)
    squares = jnp.zeros((T, LANES), F32)
    products = jnp.zeros((T, LANES), F32)
    for j in range(PAIRS):
        at = cols(j)
        crossed = mm3(c_pair, split(start_ref[0, :, at]))
        mixed = local_ref[0, :, at] + spread(since, j, left) * crossed
        gate = gate_ref[0, :, at]
        gated = mixed * (gate * sigmoid(gate))
        mixed_s[:, at] = mixed
        gated_s[:, at] = gated
        squares = squares + gated * gated
        products = products + ng_ref[0, :, at] * rows_ref[0:1, at] * gated
    inv = lax.rsqrt(jnp.sum(squares, axis=-1, keepdims=True) / DI + EPSILON)
    mean = jnp.sum(products, axis=-1, keepdims=True) / DI
    pull = inv * inv * mean
    for j in range(PAIRS):
        at = cols(j)
        mixed = mixed_s[:, at]
        gated = gated_s[:, at]
        gate = gate_ref[0, :, at]
        gain = rows_ref[0:1, at]
        ng = ng_ref[0, :, at]
        sig = sigmoid(gate)
        unit = gated * inv
        normed_ref[0, :, at] = (unit * gain).astype(BF16)
        sums_ref[:, at] = sums_ref[:, at] + fold(ng * unit)
        gated_grad = inv * (ng * gain - gated * pull)
        mixed_grad = gated_grad * (gate * sig)
        mixed_grad_ref[0, :, at] = mixed_grad
        gate_grad_ref[0, :, at] = (
            gated_grad * mixed * sig * (1.0 + gate * (1.0 - sig))
        ).astype(BF16)
        q = split(mixed_grad * mixed)
        q_high[:, at] = q[0]
        q_low[:, at] = q[1]
        prior = adj[:, at]
        enter_ref[0, 0, :, at] = prior
        fed = split(mixed_grad * spread(grown, j, left))
        adj[:, at] = prior * spread(decay, j, left[0:1]) + mm3(c_turned, fed)
    lg_ref[0] = mm(q_high[...], sel_ref[...]) + mm(q_low[...], sel_ref[...])

    @pl.when(c == pl.num_programs(1) - 1)
    def _():
        final_ref[0] = adj[...]


def adjoint_kernel(
    x_ref, bc_ref, log_ref, step_ref, aux_ref, grad_ref, enter_ref, start_ref, adj_ref, sel_ref,
    xadj_ref, bc_grad_ref, skip_ref,
    q_high, q_low,
):
    log = log_ref[0]
    log_turned = log.T
    step = step_ref[0]
    before = aux_ref[0, 0, 0:1, :]
    end = aux_ref[0, 0, 1:2, :]
    left = left_half(T)
    row = lax.broadcasted_iota(jnp.int32, (T, T), 0)
    col = lax.broadcasted_iota(jnp.int32, (T, T), 1)
    later = col >= row
    b_pair = split(bc_ref[0, :, 0:STATE])
    c_pair = split(bc_ref[0, :, STATE:])
    inner = mm3(b_pair, c_pair, NT)
    grown = jnp.exp(log)
    to_end = jnp.exp(end - log)
    reach = jnp.exp(before)
    weighted = jnp.zeros((T, T), F32)
    b_total = jnp.zeros((T, STATE), F32)
    c_total = jnp.zeros((T, STATE), F32)
    for j in range(PAIRS):
        at = cols(j)
        grad = grad_ref[0, :, at]
        x = x_ref[0, :, at]
        q = split(x * grad)
        q_high[:, at] = q[0]
        q_low[:, at] = q[1]
        fed = x * spread(step, j, left)
        high, low = split(grad)
        rhs = two_heads(high, low, left)
        decays = []
        for head in (2 * j, 2 * j + 1):
            gap = log_turned[head : head + 1, :] - log[:, head : head + 1]
            decays.append(jnp.exp(jnp.where(later, gap, MASKED)))
        mixing = split(jnp.concatenate([inner * decays[0], inner * decays[1]], axis=1))
        wide = mm(mixing[0], rhs)
        out = wide[:, :LANES] + (wide[:, LANES:] + mm(mixing[1], rhs[:, :LANES]))
        short = fed.astype(BF16)
        zero = jnp.zeros_like(short)
        stacked = jnp.concatenate(
            [jnp.where(left, short, zero), jnp.where(left, zero, short)], axis=0
        )
        dots = mm(stacked, high, NT)
        weighted = weighted + (decays[0] * dots[:T] + decays[1] * dots[T:])
        adj = split(adj_ref[0, 0, :, at])
        reached = spread(to_end, j, left)
        xadj_ref[0, :, at] = out + reached * mm3(b_pair, adj)
        b_total = b_total + mm((fed * reached).astype(BF16), adj[0], NT)
        entering = enter_ref[0, 0, :, at] + spread(reach, j, left[0:1]) * start_ref[0, :, at]
        c_total = c_total + mm3(split(grad * spread(grown, j, left)), split(entering), NT)
    skip_ref[0] = mm(q_high[...], sel_ref[...]) + mm(q_low[...], sel_ref[...])
    bc_grad_ref[0, :, 0:STATE] = b_total + mm(weighted.astype(BF16), c_pair[0])
    bc_grad_ref[0, :, STATE:] = c_total + mm(weighted.T.astype(BF16), b_pair[0])


def finish_kernel(
    x_ref, bc_ref, log_ref, step_ref, aux_ref, total_ref, grad_ref, xadj_ref, bc_grad_ref, lg_ref,
    skip_ref, end_ref, conv_ref, prev_ref, halo_ref, dt_ref, tail_ref, taps_ref, heads_ref, rows_ref,
    sel_ref,
    out_ref, head_ref, last_ref, sums_ref, head_sums_ref,
    window, pre_s, last_s, q_high, q_low, carry,
):
    slices = CONV_CH // LANES
    s, c = pl.program_id(0), pl.program_id(1)
    first = c == pl.num_programs(1) - 1

    @pl.when(c == 0)
    def _():
        pre_s[:, T : T + 8, :] = jnp.zeros((slices, 8, LANES), F32)
        carry[...] = tail_ref[0]

    @pl.when((s == 0) & (c == 0))
    def _():
        sums_ref[...] = jnp.zeros_like(sums_ref)
        head_sums_ref[...] = jnp.zeros_like(head_sums_ref)

    @pl.when(first)
    def _():
        for j in range(slices):
            window[j, 8:16, :] = halo_ref[0, :, cols(j)].astype(F32)

    @pl.when(jnp.logical_not(first))
    def _():
        for j in range(slices):
            window[j, 8:16, :] = prev_ref[0, :, cols(j)].astype(F32)[8:16, :]

    log = log_ref[0]
    step = step_ref[0]
    before = aux_ref[0, 0, 0:1, :]
    end = aux_ref[0, 0, 1:2, :]
    left = left_half(T)
    remain = jnp.exp((total_ref[0, 0:1, :] - before - end) + (end - log))
    b_pair = split(bc_ref[0, :, 0:STATE])
    b_total = bc_grad_ref[0, :, 0:STATE]

    def through(j, act_grad):
        at = cols(j)
        window[j, 16 : 16 + T, :] = conv_ref[0, :, cols(j)].astype(F32)
        pre, before_rows = convolve(window, taps_ref, j, 16 - (CONV - 1))
        sig = sigmoid(pre)
        pre_grad = act_grad * sig * (1.0 + pre * (1.0 - sig))
        pre_s[j, 0:T, :] = pre_grad
        for tap in range(CONV):
            rows = slice(8 * tap, 8 * tap + 8)
            sums_ref[rows, at] = sums_ref[rows, at] + fold(pre_grad * before_rows[tap])
        sums_ref[32:40, at] = sums_ref[32:40, at] + fold(pre_grad)
        into = pre_grad * taps_ref[CONV - 1 : CONV, cols(j)]
        for tap in range(CONV - 1):
            ahead = CONV - 1 - tap
            into = into + pre_s[j, ahead : ahead + T, :] * taps_ref[tap : tap + 1, cols(j)]
        out_ref[0, :, at] = into.astype(BF16)
        last_s[:, at] = into[T - 8 :, :]
        pre_s[j, T : T + 8, :] = pre_grad[0:8, :]

    for j in range(PAIRS):
        at = cols(j)
        x = x_ref[0, :, at]
        stepped = spread(step, j, left)
        left_over = spread(remain, j, left)
        end_pair = split(end_ref[0, :, at])
        xadj = xadj_ref[0, :, at] + left_over * mm3(b_pair, end_pair)
        b_total = b_total + mm((x * stepped * left_over).astype(BF16), end_pair[0], NT)
        q = split(x * xadj)
        q_high[:, at] = q[0]
        q_low[:, at] = q[1]
        through(j, stepped * xadj + rows_ref[1:2, at] * grad_ref[0, :, at])
    through(PAIRS, b_total)
    through(PAIRS + 1, bc_grad_ref[0, :, STATE:])

    direct = mm(q_high[...], sel_ref[...]) + mm(q_low[...], sel_ref[...])
    skipped = skip_ref[0]
    log_grad = lg_ref[0] - heads_ref[2:3, :] * skipped - step * direct
    log_grad = running(log_grad, True) + carry[0:1, :]
    carry[0:1, :] = log_grad[0:1, :]
    rate = heads_ref[1:2, :]
    step_grad = direct + log_grad * rate
    step_pre_grad = step_grad * sigmoid(dt_ref[0] + heads_ref[0:1, :])
    out_ref[0, :, CONV_CH:] = step_pre_grad.astype(BF16)
    head_sums_ref[0:8, :] = head_sums_ref[0:8, :] + fold(log_grad * step * rate)
    head_sums_ref[8:16, :] = head_sums_ref[8:16, :] + fold(step_pre_grad)
    head_sums_ref[16:24, :] = head_sums_ref[16:24, :] + fold(skipped)

    @pl.when(c == 0)
    def _():
        last_ref[0] = last_s[...]

    @pl.when(first)
    def _():
        for j in range(slices):
            head_ref[0, :, cols(j)] = pre_s[j, 0:8, :]


def input_kernel(
    proj_ref, gate_ref, front_ref, w_gate_ref, hidden_ref, cot_ref, gain_ref, *refs
):
    out_ref, sums_ref = refs[-2:]
    @pl.when(pl.program_id(0) == 0)
    def _():
        sums_ref[...] = jnp.zeros_like(sums_ref)

    x = hidden_ref[...].astype(F32)
    inv = lax.rsqrt(jnp.mean(x * x, axis=-1, keepdims=True) + EPSILON)
    unit = x * inv
    grad = mm(proj_ref[...], front_ref[...], NT) + mm(gate_ref[...], w_gate_ref[...], NT)
    sums_ref[...] = sums_ref[...] + fold(grad * unit)
    scaled = grad * gain_ref[0:1, :]
    mean = jnp.mean(scaled * unit, axis=-1, keepdims=True)
    out_ref[...] = cot_ref[...].astype(F32) + inv * (scaled - unit * mean)


def call(kernel, grid, ins, outs, scratch, flops, moved, aliases=None):
    return pl.pallas_call(
        kernel,
        input_output_aliases=aliases or {},
        grid=grid,
        in_specs=ins,
        out_specs=[spec for spec, _ in outs],
        out_shape=[shape for _, shape in outs],
        scratch_shapes=scratch,
        compiler_params=pltpu.CompilerParams(
            dimension_semantics=("arbitrary",) * len(grid), vmem_limit_bytes=56 * 2**20
        ),
        cost_estimate=pl.CostEstimate(flops=flops, bytes_accessed=moved, transcendentals=0),
    )


def flip(value, axis, bit):
    count = lax.axis_size(axis)
    return lax.ppermute(value, axis, [(i, i ^ bit) for i in range(count)])


def shifted(value, axis, steps):
    count = lax.axis_size(axis)
    initial, last = (max(0, -steps), min(count, count - steps))
    return lax.ppermute(value, axis, [(source, source + steps) for source in range(initial, last)])


def bits_of(axes):
    names = []
    for axis in axes:
        bit = lax.axis_size(axis) // 2
        while bit:
            names.append((axis, bit))
            bit //= 2
    return names


def my_bit(name):
    return (lax.axis_index(name[0]) // name[1]) % 2


def total_sum(value, axes):
    for name in bits_of(axes)[::-1]:
        value = value + flip(value, *name)
    return value


class ScatterSum:
    def __init__(self, value, axes):
        self.names = bits_of(axes)
        core = self.names[-1]
        width = value.shape[-1]
        a = value.reshape((2,) * len(self.names) + (-1, width))
        d = len(self.names) - 1
        sent = lax.dynamic_index_in_dim(a, 1 - my_bit(core), d, False)
        sent, a = lax.optimization_barrier((sent, a))
        self.mine = lax.dynamic_index_in_dim(a, my_bit(core), d, False)
        self.arrived = flip(sent, *core)
        cut = width // LANES // 3 * LANES
        self.parts = [(0, cut), (cut, 2 * cut), (2 * cut, width)]

    def halves(self, a, d, name):
        b = my_bit(name)
        return (
            lax.dynamic_index_in_dim(a, b, d, False),
            lax.dynamic_index_in_dim(a, 1 - b, d, False),
        )

    def begin(self):
        rest = self.names[:-1]
        dp = [n for n in rest if n[0] == self.names[0][0]]
        seq = [n for n in rest if n[0] != self.names[0][0]]
        self.orders = [dp[::-1] + seq[::-1], dp + seq[::-1], seq[::-1] + dp]
        self.kept, self.got, sent = [], [], []
        for order, (begin, stop) in zip(self.orders, self.parts):
            a = self.mine[..., begin:stop] + self.arrived[..., begin:stop]
            mine, other = self.halves(a, rest.index(order[0]), order[0])
            self.kept.append(mine)
            sent.append(other)
        sent = lax.optimization_barrier(tuple(sent))
        self.got = [flip(other, *order[0]) for other, order in zip(sent, self.orders)]
        return sent

    def second(self, *beside):
        *got, beside = lax.optimization_barrier((*self.got, beside))
        self.live = []
        sent = []
        for k, order in enumerate(self.orders):
            live = [name for name in self.names[:-1] if name != order[0]]
            a = self.kept[k] + got[k]
            if len(order) > 1:
                d = live.index(order[1])
                self.kept[k], other = self.halves(a, d, order[1])
                live.pop(d)
                sent.append(other)
            self.live.append(live)
        sent = lax.optimization_barrier(tuple(sent))
        self.got = [flip(other, *order[1]) for other, order in zip(sent, self.orders)]
        return sent, beside

    def finish(self, *beside):
        *got, beside = lax.optimization_barrier((*self.got, beside))
        pieces = []
        for order, live, kept, arrived in zip(self.orders, self.live, self.kept, got):
            a = kept + arrived
            for name in order[2:]:
                d = live.index(name)
                mine, other = self.halves(a, d, name)
                a = mine + flip(other, *name)
                live.pop(d)
            pieces.append(a)
        return jnp.concatenate(pieces, axis=-1), beside


def after(value, *others):
    return lax.optimization_barrier((value,) + others)[0]


def in_order(blocks, me):
    bit = 1
    while bit < len(blocks):
        swap = (me // bit) % 2 == 1
        blocks = [jnp.where(swap, blocks[i ^ bit], block) for i, block in enumerate(blocks)]
        bit *= 2
    return jnp.stack(blocks)


def gather(value):
    seq, dp = lax.axis_size("seq"), lax.axis_size("dp")
    me = lax.axis_index("seq")
    chips = [value] + [flip(value, "seq", 2 * hop) for hop in range(1, seq // 2)]
    held = in_order(chips, me // 2)
    held = in_order(
        [held] + [flip(held, "dp", hop) for hop in range(1, dp)], lax.axis_index("dp")
    )
    other = flip(held, "seq", 1)
    even = me % 2 == 0
    both = jnp.stack([jnp.where(even, held, other), jnp.where(even, other, held)], axis=2)
    return both.reshape(-1, value.shape[1])


def lanes_of(log_decay):
    return jnp.repeat(jnp.exp(log_decay[:, :HEADS]), HEADDIM, axis=1)[:, None, :]


class Entering:
    def __init__(self, state, logs, axis, reverse):
        self.axis = axis
        self.sign = -1 if reverse else 1
        self.state, self.logs = state, logs
        self.odd = lax.axis_index(axis) % 2
        self.late = self.odd == (0 if reverse else 1)
        self.partner = flip(state, axis, 1)
        self.partner_logs = flip(logs, axis, 1)
        self.chips = lax.axis_size(axis) // 2

    def half(self, value):
        return lax.dynamic_slice_in_dim(value, self.odd * (DI // 2), DI // 2, 2)

    def chip_total(self, *beside):
        self.partner, *beside = lax.optimization_barrier((self.partner,) + beside)
        here, there = self.half(self.state), self.half(self.partner)
        decay_here = self.half(lanes_of(self.logs))
        decay_there = self.half(lanes_of(self.partner_logs))
        total = jnp.where(self.late, decay_here * there + here, decay_there * here + there)
        self.total, self.decay = total, decay_here * decay_there
        self.got = shifted(total, self.axis, 2 * self.sign)
        return beside

    def first_hop(self, *beside):
        self.window, *beside = lax.optimization_barrier((self.got,) + beside)
        self.window_decay = shifted(self.decay, self.axis, 2 * self.sign)
        self.tail = self.decay * self.window + self.total
        self.tail_decay = self.decay * self.window_decay
        return beside

    def last_hops(self, *beside):
        hop = 2
        while hop < self.chips:
            got = shifted(self.tail, self.axis, 2 * self.sign * hop)
            if hop == 2:
                got, *beside = lax.optimization_barrier((got,) + beside)
            got_decay = shifted(self.tail_decay, self.axis, 2 * self.sign * hop)
            self.window = self.window_decay * got + self.window
            self.window_decay = self.window_decay * got_decay
            hop *= 2
            if hop < self.chips:
                self.tail = self.tail_decay * got + self.tail
                self.tail_decay = self.tail_decay * got_decay
        self.whole = flip(self.window, self.axis, 1)
        return beside

    def result(self, *beside):
        self.whole, *beside = lax.optimization_barrier((self.whole,) + beside)
        both = jnp.where(
            self.odd == 0,
            jnp.concatenate([self.window, self.whole], axis=2),
            jnp.concatenate([self.whole, self.window], axis=2),
        )
        state = jnp.where(self.late, lanes_of(self.partner_logs) * both + self.partner, both)
        return [state] + beside


def on_device(
    hidden_in,
    lengths,
    w_in,
    conv_w,
    conv_b,
    g_norm,
    g_gate,
    w_out,
    a_log,
    dt_bias,
    d_skip,
    out_cotangent,
):
    axes = ("dp", "seq")
    devices = lax.axis_size("dp") * lax.axis_size("seq")
    slots, tokens, _ = hidden_in.shape
    blocks = tokens // T
    rows = slots * tokens
    grid = (slots, blocks)
    share = D // devices

    small = jnp.concatenate(
        [conv_w.reshape(-1), conv_b, g_norm, g_gate], axis=0
    )
    per_row = -(-small.shape[0] // share)
    small = jnp.pad(small, (0, per_row * share - small.shape[0])).reshape(share, per_row)
    wide = CONV_CH + LANES
    front = jnp.pad(w_in[:, DI:], ((0, 0), (0, LANES - HEADS)))
    earlier = shifted(hidden_in[:, tokens - 8 :, :], "seq", 1)
    front_full = gather(jnp.concatenate([front, small], axis=1))
    extra = front_full[:, wide:].reshape(devices, -1)
    lane = CONV_CH // devices
    taps_full = jnp.moveaxis(extra[:, : CONV * lane].reshape(devices, CONV, lane), 0, 1)
    taps_full = taps_full.reshape(CONV, CONV_CH).astype(F32)
    at = CONV * lane
    bias_full = extra[:, at : at + lane].reshape(1, CONV_CH).astype(F32)
    at += lane
    norm_gain = extra[:, at : at + share].reshape(D).astype(F32)
    at += share
    gate_gain = extra[:, at : at + DI // devices].reshape(1, DI).astype(F32)
    back = jnp.concatenate([w_in[:, :DI], w_out.T], axis=1)
    back = lax.all_gather(back, axes, axis=0, tiled=True)
    w_gate, w_out_turned = lax.optimization_barrier((back[:, :DI], back[:, DI:]))

    taps_rows = jnp.concatenate([taps_full, bias_full, jnp.zeros((3, CONV_CH), F32)], axis=0)
    rate = -jnp.exp(a_log)
    heads_rows = jnp.pad(jnp.stack([dt_bias, rate, d_skip]), ((0, 5), (0, LANES - HEADS)))
    skip_row = jnp.repeat(d_skip, HEADDIM)[None]
    gain_rows = jnp.concatenate([gate_gain, skip_row, jnp.zeros((6, DI), F32)], axis=0)
    select = (
        jnp.arange(DI, dtype=jnp.int32)[:, None] // HEADDIM
        == jnp.arange(LANES, dtype=jnp.int32)[None]
    ).astype(BF16)

    place = lax.axis_index("seq") * tokens + jnp.arange(tokens, dtype=jnp.int32)
    keep = (place[None, :] < lengths[:, None]).astype(F32)
    residual = hidden_in.astype(F32)

    def tile(width, dtype=F32, flip_order=False, height=T):
        if flip_order:
            spec = pl.BlockSpec((1, height, width), lambda s, c: (s, blocks - 1 - c, 0))
        else:
            spec = pl.BlockSpec((1, height, width), lambda s, c: (s, c, 0))
        return spec, jax.ShapeDtypeStruct((slots, tokens, width), dtype)

    def per_block(height, width, flip_order=False):
        if flip_order:
            spec = pl.BlockSpec((1, 1, height, width), lambda s, c: (s, blocks - 1 - c, 0, 0))
        else:
            spec = pl.BlockSpec((1, 1, height, width), lambda s, c: (s, c, 0, 0))
        return spec, jax.ShapeDtypeStruct((slots, blocks, height, width), F32)

    def columns(width, whole, index):
        spec = pl.BlockSpec((1, T, width), lambda s, c: (s, blocks - 1 - c, index))
        return spec, jax.ShapeDtypeStruct((slots, tokens, whole), F32)

    def per_slot(height, width, dtype=F32):
        spec = pl.BlockSpec((1, height, width), lambda s, c: (s, 0, 0))
        return spec, jax.ShapeDtypeStruct((slots, height, width), dtype)

    def fixed(height, width):
        spec = pl.BlockSpec((height, width), lambda s, c: (0, 0))
        return spec, jax.ShapeDtypeStruct((height, width), F32)

    def specs(*pairs):
        return [spec for spec, _ in pairs]

    normed, conv_in, halo, step_raw, x, bc, log, step, aux, enter, final, total = call(
        states_kernel,
        grid,
        specs(
            tile(D), per_slot(8, D), fixed(D, wide), fixed(1, D), fixed(8, CONV_CH), fixed(8, LANES)
        ),
        [
            tile(D, BF16), tile(CONV_CH, BF16), per_slot(8, CONV_CH, BF16), tile(LANES), tile(DI),
            tile(2 * STATE), tile(LANES), tile(LANES), per_block(8, LANES), per_block(STATE, DI),
            per_slot(STATE, DI), per_slot(8, LANES),
        ],
        [
            pltpu.VMEM((CONV_CH // LANES, T + 8, LANES), F32), pltpu.VMEM((STATE, DI), F32),
            pltpu.VMEM((8, LANES), F32),
        ],
        6 * rows * STATE * DI + 2 * rows * D * wide,
        rows * (CONV_CH * 6 + DI * 4),
    )(hidden_in, earlier, front_full, norm_gain[None], taps_rows, heads_rows)
    normed = normed.reshape(rows, D)
    logs = total[:, 0, :]
    forward = Entering(final, logs, "seq", False)
    gate_pre = jnp.dot(after(normed, final), w_gate, preferred_element_type=F32)
    (gate_pre,) = forward.chip_total(gate_pre.reshape(slots, tokens, DI))
    cotangent = out_cotangent.astype(F32)
    branch_grad = (cotangent * keep[..., None]).astype(BF16).reshape(rows, D)
    norm_grad = jnp.dot(
        after(branch_grad, forward.total), w_out_turned, preferred_element_type=F32
    )
    (norm_grad,) = forward.first_hop(norm_grad.reshape(slots, tokens, DI))
    (local,) = call(
        local_kernel,
        grid,
        specs(
            tile(DI), tile(2 * STATE), tile(LANES), tile(LANES), per_block(STATE, DI), fixed(8, DI)
        ),
        [tile(DI)],
        [],
        12 * rows * T * DI,
        rows * (CONV_CH + 2 * DI) * 4,
    )(after(x, forward.tail), bc, log, step, enter, gain_rows)
    (local,) = forward.last_hops(local)
    (start,) = forward.result()

    gated_norm, mixed_grad, gate_grad, lg, adj_enter, adj_final, gate_sums = call(
        gate_kernel,
        grid,
        specs(
            columns(STATE, 2 * STATE, 1), tile(LANES, flip_order=True),
            per_block(8, LANES, True), tile(DI, flip_order=True), tile(DI, flip_order=True),
            tile(DI, flip_order=True), per_slot(STATE, DI), fixed(8, DI), fixed(DI, LANES),
        ),
        [
            tile(DI, BF16, True), tile(DI, F32, True), tile(DI, BF16, True),
            tile(LANES, F32, True), per_block(STATE, DI, True), per_slot(STATE, DI), fixed(8, DI),
        ],
        [
            pltpu.VMEM((T, DI), F32), pltpu.VMEM((T, DI), F32), pltpu.VMEM((STATE, DI), F32),
            pltpu.VMEM((T, DI), BF16), pltpu.VMEM((T, DI), BF16),
        ],
        12 * rows * STATE * DI,
        rows * (CONV_CH * 4 + DI * 24),
    )(bc, log, aux, local, gate_pre, norm_grad, start, gain_rows, select)
    gated_norm = gated_norm.reshape(rows, DI)
    gate_grad = gate_grad.reshape(rows, DI)
    backward = Entering(adj_final, logs, "seq", True)

    w_out_grad = lax.dot_general(
        branch_grad, gated_norm, (((0,), (0,)), ((), ())), preferred_element_type=F32
    )
    (w_out_grad,) = backward.chip_total(w_out_grad)
    w_gate_grad = lax.dot_general(
        normed, after(gate_grad, backward.total), (((0,), (0,)), ((), ())), preferred_element_type=F32
    )
    branch = lax.dot_general(
        after(gated_norm, backward.total), w_out_turned, NT, preferred_element_type=F32
    )
    block_out = (residual + keep[..., None] * branch.reshape(slots, tokens, D)).astype(BF16)
    early = jnp.concatenate([w_gate_grad, w_out_grad], axis=1)
    early, block_out = backward.first_hop(early, block_out)
    early = lax.psum_scatter(early, axes, scatter_dimension=0, tiled=True)

    xadj, bc_grad, skipped = call(
        adjoint_kernel,
        grid,
        specs(
            tile(DI), tile(2 * STATE), tile(LANES), tile(LANES), per_block(8, LANES), tile(DI),
            per_block(STATE, DI), per_slot(STATE, DI), per_block(STATE, DI), fixed(DI, LANES),
        ),
        [tile(DI), tile(2 * STATE), tile(LANES)],
        [pltpu.VMEM((T, DI), BF16), pltpu.VMEM((T, DI), BF16)],
        30 * rows * T * DI,
        rows * (CONV_CH + 4 * DI) * 4,
    )(
        x, bc, log, step, aux, after(mixed_grad, backward.tail), enter, start, adj_enter, select
    )
    (xadj,) = backward.last_hops(xadj)
    (end_adj,) = backward.result()

    end_state = lanes_of(logs) * start + final
    tail = jnp.sum(end_adj * end_state, axis=1).reshape(slots, HEADS, HEADDIM).sum(-1)
    tail = jnp.broadcast_to(jnp.pad(tail, ((0, 0), (0, LANES - HEADS)))[:, None], (slots, 8, LANES))
    prev = pl.BlockSpec(
        (1, 16, CONV_CH), lambda s, c: (s, jnp.maximum((blocks - 1 - c) * (T // 16) - 1, 0), 0)
    )
    def flipped(width, dtype=F32):
        return tile(width, dtype, True)

    slices = CONV_CH // LANES
    proj_grad, head_rows, last_rows, conv_sums, head_sums = call(
        finish_kernel,
        grid,
        specs(
            flipped(DI), flipped(2 * STATE), flipped(LANES), flipped(LANES),
            per_block(8, LANES, True), per_slot(8, LANES), flipped(DI), flipped(DI),
            flipped(2 * STATE), flipped(LANES), flipped(LANES), per_slot(STATE, DI),
            flipped(CONV_CH), (prev, None), per_slot(8, CONV_CH), flipped(LANES),
            per_slot(8, LANES), fixed(8, CONV_CH), fixed(8, LANES), fixed(8, DI), fixed(DI, LANES),
        ),
        [
            flipped(wide, BF16), per_slot(8, CONV_CH), per_slot(8, CONV_CH), fixed(40, CONV_CH),
            fixed(24, LANES),
        ],
        [
            pltpu.VMEM((slices, T + 16, LANES), F32), pltpu.VMEM((slices, T + 8, LANES), F32),
            pltpu.VMEM((8, CONV_CH), F32), pltpu.VMEM((T, DI), BF16), pltpu.VMEM((T, DI), BF16),
            pltpu.VMEM((8, LANES), F32),
        ],
        12 * rows * STATE * DI,
        rows * (CONV_CH * 8 + DI * 8),
    )(
        x, bc, log, step, aux, total, mixed_grad, xadj, bc_grad, lg, skipped, end_adj, conv_in,
        conv_in, halo, step_raw, tail, taps_rows, heads_rows, gain_rows, select,
    )

    ahead = shifted(head_rows, "seq", -1)
    ahead = jnp.concatenate([jnp.zeros((slots, 8, CONV_CH), F32), ahead], axis=1)
    for tap in range(CONV):
        begin = CONV - 1 - tap
        last_rows = last_rows + ahead[:, begin : begin + 8] * taps_full[tap]
    proj_grad = lax.dynamic_update_slice(
        proj_grad, last_rows.astype(BF16), (0, tokens - 8, 0)
    ).reshape(rows, wide)

    w_front_grad = lax.dot_general(
        normed, proj_grad, (((0,), (0,)), ((), ())), preferred_element_type=F32
    )
    scatter = ScatterSum(w_front_grad, axes)
    tall = min(2 * T, rows // 2)

    strips = rows // tall // 2

    def input_half(half, sent, *done):
        def strip(width, dtype=BF16):
            spec = pl.BlockSpec((tall, width), lambda r: (r + half * strips, 0))
            return spec, jax.ShapeDtypeStruct((rows, width), dtype)

        def whole(height, width):
            spec = pl.BlockSpec((height, width), lambda r: (0, 0))
            return spec, jax.ShapeDtypeStruct((height, width), F32)

        ins = [
            strip(wide), strip(DI), whole(D, wide), whole(D, DI), strip(D), strip(D), whole(1, D)
        ]
        return call(
            input_kernel,
            (strips,),
            specs(*ins) + [pl.BlockSpec(memory_space=pl.ANY)] * len(done),
            [strip(D, F32), whole(8, D)],
            [],
            rows * D * (wide + DI),
            (rows * (wide + DI) * 2 + rows * D * 8) // 2,
            {len(ins): 0} if done else None,
        )(
            after(proj_grad, *sent), gate_grad, front_full, w_gate, hidden_in.reshape(rows, D),
            out_cotangent.reshape(rows, D), norm_gain[None], *done,
        )

    input_grad, norm_sums = input_half(0, scatter.begin())
    sent, (input_grad, norm_sums, early) = scatter.second(input_grad, norm_sums, early)
    w_gate_owned, w_out_owned = early[:, :DI], early[:, DI:]
    input_grad, more_sums = input_half(1, sent, input_grad)
    front_owned, (input_grad, norm_sums) = scatter.finish(input_grad, norm_sums + more_sums)
    input_grad = input_grad.reshape(slots, tokens, D)

    vectors = jnp.concatenate(
        [
            conv_sums.reshape(CONV + 1, 8, CONV_CH).sum(1).reshape(-1), norm_sums.sum(0),
            gate_sums.sum(0), head_sums.reshape(3, 8, LANES).sum(1).reshape(-1),
        ]
    )
    vectors = total_sum(vectors.reshape(-1, LANES), axes).reshape(-1)
    me = lax.axis_index("dp") * lax.axis_size("seq") + lax.axis_index("seq")

    def owned(begin, length):
        per = length // devices
        return lax.dynamic_slice_in_dim(vectors, begin + me * per, per)

    norm_at = (CONV + 1) * CONV_CH
    gate_at = norm_at + D
    heads_at = gate_at + DI
    return (
        block_out,
        input_grad,
        jnp.concatenate([w_gate_owned, front_owned[:, : CONV_CH + HEADS]], axis=1),
        jnp.stack([owned(k * CONV_CH, CONV_CH) for k in range(CONV)]),
        owned(CONV * CONV_CH, CONV_CH),
        owned(norm_at, D),
        owned(gate_at, DI),
        w_out_owned.T,
        vectors[heads_at : heads_at + HEADS],
        vectors[heads_at + LANES : heads_at + LANES + HEADS],
        vectors[heads_at + 2 * LANES : heads_at + 2 * LANES + HEADS],
    )


def solution(mesh):
    placed = (
        P("dp", "seq", None),
        P("dp"),
        P(("dp", "seq"), None),
        P(None, ("dp", "seq")),
        P(("dp", "seq")),
        P(("dp", "seq")),
        P(("dp", "seq")),
        P(None, ("dp", "seq")),
        P(),
        P(),
        P(),
        P("dp", "seq", None),
    )
    return jax.shard_map(
        on_device,
        mesh=mesh,
        in_specs=placed,
        out_specs=(
            P("dp", "seq", None),
            P("dp", "seq", None),
            P(("dp", "seq"), None),
            P(None, ("dp", "seq")),
            P(("dp", "seq")),
            P(("dp", "seq")),
            P(("dp", "seq")),
            P(None, ("dp", "seq")),
            P(),
            P(),
            P(),
        ),
        check_vma=False,
    )
```

```python
import functools

import jax
import jax.numpy as jnp
from jax import lax
from jax.experimental import pallas as pl
from jax.experimental.pallas import tpu as pltpu
from jax.sharding import PartitionSpec as P

D = 768
HEADS = 24
HEADDIM = 64
STATE = 128
CONV = 4
DI = 1536
CONV_CH = 1792
PROJ = 3352
T = 128
PAIRS = HEADS // 2
LANES = 128
EPSILON = 1e-05
MASKED = -1e30
F32 = jnp.float32
BF16 = jnp.bfloat16
NN = (((1,), (0,)), ((), ()))
NT = (((1,), (1,)), ((), ()))


def mm(a, b, dims=NN):
    return lax.dot_general(a, b, dims, preferred_element_type=F32)


def split(v):
    high = v.astype(BF16)
    return high, (v - high.astype(F32)).astype(BF16)


def mm3(a, b, dims=NN):
    return mm(a[0], b[0], dims) + (mm(a[0], b[1], dims) + mm(a[1], b[0], dims))


def left_half(rows):
    return lax.broadcasted_iota(jnp.int32, (rows, LANES), 1) < HEADDIM


def spread(values, pair, left):
    return jnp.where(
        left, values[:, 2 * pair : 2 * pair + 1], values[:, 2 * pair + 1 : 2 * pair + 2]
    )


def pick(values, pair, left):
    index = jnp.where(left, 2 * pair, 2 * pair + 1)
    return jnp.take_along_axis(values, index, axis=1, mode="promise_in_bounds")


def two_columns(values, pair):
    return [
        jnp.broadcast_to(values[:, head : head + 1], (values.shape[0], LANES))
        for head in (2 * pair, 2 * pair + 1)
    ]


def cols(j):
    return slice(j * LANES, (j + 1) * LANES)


def running(v, reverse):
    row = lax.broadcasted_iota(jnp.int32, v.shape, 0)
    hop = 1
    while hop < T:
        moved = pltpu.roll(v, T - hop if reverse else hop, 0)
        inside = row < T - hop if reverse else row >= hop
        v = v + jnp.where(inside, moved, 0.0)
        hop *= 2
    return v


def fold(v):
    return jnp.sum(v.reshape(v.shape[0] // 8, 8, v.shape[-1]), axis=0)


def two_heads(high, low, left):
    zero = jnp.zeros_like(high)
    top = jnp.concatenate([jnp.where(left, high, zero), jnp.where(left, low, zero)], axis=1)
    bottom = jnp.concatenate([jnp.where(left, zero, high), jnp.where(left, zero, low)], axis=1)
    return jnp.concatenate([top, bottom], axis=0)


def sigmoid(v):
    return 0.5 * jnp.tanh(0.5 * v) + 0.5


def convolve(window, taps_ref, j, first):
    at = cols(j)
    total = taps_ref[CONV : CONV + 1, at]
    rows = [window[j, first + tap : first + tap + T, :] for tap in range(CONV)]
    for tap in range(CONV):
        total = total + rows[tap] * taps_ref[tap : tap + 1, at]
    return total, rows


def states_kernel(
    hidden_ref, before_ref, front_ref, gain_ref, taps_ref, heads_ref,
    normed_ref, conv_ref, halo_ref, dt_ref, x_ref, bc_ref, log_ref, step_ref, aux_ref, enter_ref,
    final_ref, total_ref,
    window, state, before,
):
    c = pl.program_id(1)

    def norm(rows):
        rows = rows.astype(F32)
        inv = lax.rsqrt(jnp.mean(rows * rows, axis=-1, keepdims=True) + EPSILON)
        return (rows * inv * gain_ref[0:1, :]).astype(BF16)

    @pl.when(c == 0)
    def _():
        earlier = norm(before_ref[0])
        for j in range(CONV_CH // LANES):
            rows = mm(earlier, front_ref[:, cols(j)]).astype(BF16)
            halo_ref[0, :, cols(j)] = rows
            window[j, 0:8, :] = rows.astype(F32)
        state[...] = jnp.zeros_like(state)
        before[...] = jnp.zeros_like(before)

    normed = norm(hidden_ref[0])
    normed_ref[0] = normed
    for k in range(CONV_CH // LANES // 2):
        two = slice(2 * k * LANES, 2 * (k + 1) * LANES)
        rows = mm(normed, front_ref[:, two]).astype(BF16)
        conv_ref[0, :, two] = rows
        for j in (2 * k, 2 * k + 1):
            window[j, 8 : 8 + T, :] = rows[:, cols(j - 2 * k)].astype(F32)
            pre, _ = convolve(window, taps_ref, j, 8 - (CONV - 1))
            if j < PAIRS:
                x_ref[0, :, cols(j)] = pre * sigmoid(pre)
            else:
                bc_ref[0, :, cols(j - PAIRS)] = pre * sigmoid(pre)
            window[j, 0:8, :] = window[j, T : T + 8, :]

    dt = mm(normed, front_ref[:, CONV_CH : CONV_CH + LANES])
    dt_ref[0] = dt
    step = jax.nn.softplus(dt + heads_ref[0:1, :])
    log = running(step * heads_ref[1:2, :], False)
    end = log[T - 1 : T, :]
    step_ref[0] = step
    log_ref[0] = log
    weight = jnp.exp(end - log) * step
    decay = jnp.exp(end)
    left = left_half(T)
    aux_ref[0, 0] = jnp.concatenate([before[0:1, :], end, jnp.zeros((6, LANES), F32)], axis=0)
    before[0:1, :] = before[0:1, :] + end
    b_turned = split(bc_ref[0, :, 0:STATE].T)
    for j in range(PAIRS):
        prior = state[:, cols(j)]
        enter_ref[0, 0, :, cols(j)] = prior
        fed = split(x_ref[0, :, cols(j)] * spread(weight, j, left))
        state[:, cols(j)] = prior * spread(decay, j, left[0:1]) + mm3(b_turned, fed)

    @pl.when(c == pl.num_programs(1) - 1)
    def _():
        final_ref[0] = state[...]
        total_ref[0] = before[...]


def local_kernel(x_ref, bc_ref, log_ref, step_ref, enter_ref, rows_ref, out_ref):
    log = log_ref[0]
    log_turned = log.T
    step = step_ref[0]
    left = left_half(T)
    row = lax.broadcasted_iota(jnp.int32, (T, T), 0)
    col = lax.broadcasted_iota(jnp.int32, (T, T), 1)
    causal = row >= col
    b_pair = split(bc_ref[0, :, 0:STATE])
    c_pair = split(bc_ref[0, :, STATE:])
    inner = mm3(c_pair, b_pair, NT)
    for j in range(PAIRS):
        x = x_ref[0, :, cols(j)]
        fed = split(x * spread(step, j, left))
        rhs = two_heads(fed[0], fed[1], left)
        mats = []
        logs = two_columns(log, j)
        for k in range(2):
            gap = logs[k] - log_turned[2 * j + k : 2 * j + k + 1, :]
            mats.append(inner * jnp.exp(jnp.where(causal, gap, MASKED)))
        mixing = split(jnp.concatenate(mats, axis=1))
        wide = mm(mixing[0], rhs)
        out = wide[:, :LANES] + (wide[:, LANES:] + mm(mixing[1], rhs[:, :LANES]))
        crossed = mm3(c_pair, split(enter_ref[0, 0, :, cols(j)]))
        skipped = rows_ref[1:2, cols(j)] * x
        out_ref[0, :, cols(j)] = (out + skipped) + jnp.exp(jnp.where(left, *logs)) * crossed


def gate_kernel(
    c_ref, log_ref, aux_ref, local_ref, gate_ref, ng_ref, start_ref, rows_ref, sel_ref,
    normed_ref, mixed_grad_ref, gate_grad_ref, lg_ref, enter_ref, final_ref, sums_ref,
    mixed_s, gated_s, adj, q_high, q_low,
):
    s, c = pl.program_id(0), pl.program_id(1)

    @pl.when(c == 0)
    def _():
        adj[...] = jnp.zeros_like(adj)

    @pl.when((s == 0) & (c == 0))
    def _():
        sums_ref[...] = jnp.zeros_like(sums_ref)

    log = log_ref[0]
    before = aux_ref[0, 0, 0:1, :]
    end = aux_ref[0, 0, 1:2, :]
    left = left_half(T)
    since = jnp.exp(before + log)
    grown = jnp.exp(log)
    decay = jnp.exp(end)
    c_rows = c_ref[0]
    c_pair = split(c_rows)
    c_turned = split(c_rows.T)
    squares = jnp.zeros((T, LANES), F32)
    products = jnp.zeros((T, LANES), F32)
    for j in range(PAIRS):
        at = cols(j)
        crossed = mm3(c_pair, split(start_ref[0, :, at]))
        mixed = local_ref[0, :, at] + spread(since, j, left) * crossed
        gate = gate_ref[0, :, at]
        gated = mixed * (gate * sigmoid(gate))
        mixed_s[:, at] = mixed
        gated_s[:, at] = gated
        squares = squares + gated * gated
        products = products + ng_ref[0, :, at] * rows_ref[0:1, at] * gated
    inv = lax.rsqrt(jnp.sum(squares, axis=-1, keepdims=True) / DI + EPSILON)
    mean = jnp.sum(products, axis=-1, keepdims=True) / DI
    pull = inv * inv * mean
    for j in range(PAIRS):
        at = cols(j)
        mixed = mixed_s[:, at]
        gated = gated_s[:, at]
        gate = gate_ref[0, :, at]
        gain = rows_ref[0:1, at]
        ng = ng_ref[0, :, at]
        sig = sigmoid(gate)
        unit = gated * inv
        normed_ref[0, :, at] = (unit * gain).astype(BF16)
        sums_ref[:, at] = sums_ref[:, at] + fold(ng * unit)
        gated_grad = inv * (ng * gain - gated * pull)
        mixed_grad = gated_grad * (gate * sig)
        mixed_grad_ref[0, :, at] = mixed_grad
        gate_grad_ref[0, :, at] = (
            gated_grad * mixed * sig * (1.0 + gate * (1.0 - sig))
        ).astype(BF16)
        q = split(mixed_grad * mixed)
        q_high[:, at] = q[0]
        q_low[:, at] = q[1]
        prior = adj[:, at]
        enter_ref[0, 0, :, at] = prior
        fed = split(mixed_grad * spread(grown, j, left))
        adj[:, at] = prior * spread(decay, j, left[0:1]) + mm3(c_turned, fed)
    lg_ref[0] = mm(q_high[...], sel_ref[...]) + mm(q_low[...], sel_ref[...])

    @pl.when(c == pl.num_programs(1) - 1)
    def _():
        final_ref[0] = adj[...]


def adjoint_kernel(
    x_ref, bc_ref, log_ref, step_ref, aux_ref, grad_ref, enter_ref, start_ref, adj_ref, sel_ref,
    xadj_ref, bc_grad_ref, skip_ref,
    q_high, q_low, fed_s, adj_s, grads_s, states_s,
):
    log = log_ref[0]
    log_turned = log.T
    step = step_ref[0]
    before = aux_ref[0, 0, 0:1, :]
    end = aux_ref[0, 0, 1:2, :]
    left = left_half(T)
    row = lax.broadcasted_iota(jnp.int32, (T, T), 0)
    col = lax.broadcasted_iota(jnp.int32, (T, T), 1)
    later = col >= row
    b_pair = split(bc_ref[0, :, 0:STATE])
    c_pair = split(bc_ref[0, :, STATE:])
    inner = mm3(b_pair, c_pair, NT)
    reach = jnp.exp(before)
    weighted = jnp.zeros((T, T), F32)
    for j in range(PAIRS):
        at = cols(j)
        grad = grad_ref[0, :, at]
        x = x_ref[0, :, at]
        q = split(x * grad)
        q_high[:, at] = q[0]
        q_low[:, at] = q[1]
        fed = x * spread(step, j, left)
        high, low = split(grad)
        rhs = two_heads(high, low, left)
        decays = []
        logs = two_columns(log, j)
        for k in range(2):
            gap = log_turned[2 * j + k : 2 * j + k + 1, :] - logs[k]
            decays.append(jnp.exp(jnp.where(later, gap, MASKED)))
        both = jnp.where(left, *logs)
        mixing = split(jnp.concatenate([inner * decays[0], inner * decays[1]], axis=1))
        wide = mm(mixing[0], rhs)
        out = wide[:, :LANES] + (wide[:, LANES:] + mm(mixing[1], rhs[:, :LANES]))
        short = fed.astype(BF16)
        zero = jnp.zeros_like(short)
        stacked = jnp.concatenate(
            [jnp.where(left, short, zero), jnp.where(left, zero, short)], axis=0
        )
        dots = mm(stacked, high, NT)
        weighted = weighted + (decays[0] * dots[:T] + decays[1] * dots[T:])
        adj = split(adj_ref[0, 0, :, at])
        reached = jnp.exp(spread(end, j, left[0:1]) - both)
        xadj_ref[0, :, at] = out + reached * mm3(b_pair, adj)
        fed_s[:, at] = (fed * reached).astype(BF16)
        adj_s[:, at] = adj[0]
        entering = enter_ref[0, 0, :, at] + spread(reach, j, left[0:1]) * start_ref[0, :, at]
        states_s[0:STATE, at], states_s[STATE:, at] = split(entering)
        grads_s[0:T, at], grads_s[T:, at] = split(grad * jnp.exp(both))
    b_total = mm(fed_s[...], adj_s[...], NT)
    c_parts = mm(grads_s[...], states_s[...], NT)
    c_total = c_parts[:T, :STATE] + (c_parts[:T, STATE:] + c_parts[T:, :STATE])
    skip_ref[0] = mm(q_high[...], sel_ref[...]) + mm(q_low[...], sel_ref[...])
    bc_grad_ref[0, :, 0:STATE] = b_total + mm(weighted.astype(BF16), c_pair[0])
    bc_grad_ref[0, :, STATE:] = c_total + mm(weighted.T.astype(BF16), b_pair[0])


def finish_kernel(
    x_ref, bc_ref, log_ref, step_ref, aux_ref, total_ref, grad_ref, xadj_ref, bc_grad_ref, lg_ref,
    skip_ref, end_ref, start_ref, final_ref, conv_ref, prev_ref, halo_ref, dt_ref, taps_ref, heads_ref,
    rows_ref, sel_ref,
    out_ref, head_ref, last_ref, sums_ref, head_sums_ref,
    window, pre_s, last_s, q_high, q_low, carry,
):
    slices = CONV_CH // LANES
    s, c = pl.program_id(0), pl.program_id(1)
    first = c == pl.num_programs(1) - 1

    @pl.when(c == 0)
    def _():
        pre_s[:, T : T + 8, :] = jnp.zeros((slices, 8, LANES), F32)
        passed = jnp.exp(total_ref[0])
        tail = jnp.zeros((8, LANES), F32)
        for j in range(PAIRS):
            at = cols(j)
            decay = spread(passed[0:1, :], j, left_half(1))
            leaving = decay * start_ref[0, :, at] + final_ref[0, :, at]
            high, low = split(fold(end_ref[0, :, at] * leaving))
            tail = tail + (mm(high, sel_ref[at, :]) + mm(low, sel_ref[at, :]))
        carry[...] = jnp.broadcast_to(jnp.sum(tail, axis=0, keepdims=True), (8, LANES))

    @pl.when((s == 0) & (c == 0))
    def _():
        sums_ref[...] = jnp.zeros_like(sums_ref)
        head_sums_ref[...] = jnp.zeros_like(head_sums_ref)

    @pl.when(first)
    def _():
        for j in range(slices):
            window[j, 8:16, :] = halo_ref[0, :, cols(j)].astype(F32)

    @pl.when(jnp.logical_not(first))
    def _():
        for j in range(slices):
            window[j, 8:16, :] = prev_ref[0, :, cols(j)].astype(F32)[8:16, :]

    log = log_ref[0]
    step = step_ref[0]
    before = aux_ref[0, 0, 0:1, :]
    end = aux_ref[0, 0, 1:2, :]
    left = left_half(T)
    remain = jnp.exp((total_ref[0, 0:1, :] - before - end) + (end - log))
    b_pair = split(bc_ref[0, :, 0:STATE])
    b_total = bc_grad_ref[0, :, 0:STATE]

    def through(j, act_grad):
        at = cols(j)
        window[j, 16 : 16 + T, :] = conv_ref[0, :, cols(j)].astype(F32)
        pre, before_rows = convolve(window, taps_ref, j, 16 - (CONV - 1))
        sig = sigmoid(pre)
        pre_grad = act_grad * sig * (1.0 + pre * (1.0 - sig))
        pre_s[j, 0:T, :] = pre_grad
        for tap in range(CONV):
            rows = slice(8 * tap, 8 * tap + 8)
            sums_ref[rows, at] = sums_ref[rows, at] + fold(pre_grad * before_rows[tap])
        sums_ref[32:40, at] = sums_ref[32:40, at] + fold(pre_grad)
        into = pre_grad * taps_ref[CONV - 1 : CONV, cols(j)]
        for tap in range(CONV - 1):
            ahead = CONV - 1 - tap
            into = into + pre_s[j, ahead : ahead + T, :] * taps_ref[tap : tap + 1, cols(j)]
        out_ref[0, :, at] = into.astype(BF16)
        last_s[:, at] = into[T - 8 :, :]
        pre_s[j, T : T + 8, :] = pre_grad[0:8, :]

    for j in range(PAIRS):
        at = cols(j)
        x = x_ref[0, :, at]
        stepped = pick(step, j, left)
        left_over = pick(remain, j, left)
        end_pair = split(end_ref[0, :, at])
        xadj = xadj_ref[0, :, at] + left_over * mm3(b_pair, end_pair)
        b_total = b_total + mm((x * stepped * left_over).astype(BF16), end_pair[0], NT)
        q = split(x * xadj)
        q_high[:, at] = q[0]
        q_low[:, at] = q[1]
        through(j, stepped * xadj + rows_ref[1:2, at] * grad_ref[0, :, at])
    through(PAIRS, b_total)
    through(PAIRS + 1, bc_grad_ref[0, :, STATE:])

    direct = mm(q_high[...], sel_ref[...]) + mm(q_low[...], sel_ref[...])
    skipped = skip_ref[0]
    log_grad = lg_ref[0] - heads_ref[2:3, :] * skipped - step * direct
    log_grad = running(log_grad, True) + carry[0:1, :]
    carry[0:1, :] = log_grad[0:1, :]
    rate = heads_ref[1:2, :]
    step_grad = direct + log_grad * rate
    step_pre_grad = step_grad * sigmoid(dt_ref[0] + heads_ref[0:1, :])
    out_ref[0, :, CONV_CH:] = step_pre_grad.astype(BF16)
    head_sums_ref[0:8, :] = head_sums_ref[0:8, :] + fold(log_grad * step * rate)
    head_sums_ref[8:16, :] = head_sums_ref[8:16, :] + fold(step_pre_grad)
    head_sums_ref[16:24, :] = head_sums_ref[16:24, :] + fold(skipped)

    @pl.when(c == 0)
    def _():
        last_ref[0] = last_s[...]

    @pl.when(first)
    def _():
        for j in range(slices):
            head_ref[0, :, cols(j)] = pre_s[j, 0:8, :]


def input_kernel(
    proj_ref, gate_ref, front_ref, w_gate_ref, hidden_ref, cot_ref, gain_ref, *refs
):
    out_ref, sums_ref = refs[-2:]
    @pl.when(pl.program_id(0) == 0)
    def _():
        sums_ref[...] = jnp.zeros_like(sums_ref)

    x = hidden_ref[...].astype(F32)
    inv = lax.rsqrt(jnp.mean(x * x, axis=-1, keepdims=True) + EPSILON)
    unit = x * inv
    grad = mm(proj_ref[...], front_ref[...], NT) + mm(gate_ref[...], w_gate_ref[...], NT)
    sums_ref[...] = sums_ref[...] + fold(grad * unit)
    scaled = grad * gain_ref[0:1, :]
    mean = jnp.mean(scaled * unit, axis=-1, keepdims=True)
    out_ref[...] = cot_ref[...].astype(F32) + inv * (scaled - unit * mean)


def call(kernel, grid, ins, outs, scratch, flops, moved, aliases=None):
    return pl.pallas_call(
        kernel,
        input_output_aliases=aliases or {},
        grid=grid,
        in_specs=ins,
        out_specs=[spec for spec, _ in outs],
        out_shape=[shape for _, shape in outs],
        scratch_shapes=scratch,
        compiler_params=pltpu.CompilerParams(
            dimension_semantics=("arbitrary",) * len(grid), vmem_limit_bytes=56 * 2**20
        ),
        cost_estimate=pl.CostEstimate(flops=flops, bytes_accessed=moved, transcendentals=0),
    )


def flip(value, axis, bit):
    count = lax.axis_size(axis)
    return lax.ppermute(value, axis, [(i, i ^ bit) for i in range(count)])


def shifted(value, axis, steps):
    count = lax.axis_size(axis)
    initial, last = (max(0, -steps), min(count, count - steps))
    return lax.ppermute(value, axis, [(source, source + steps) for source in range(initial, last)])


def bits_of(axes):
    names = []
    for axis in axes:
        bit = lax.axis_size(axis) // 2
        while bit:
            names.append((axis, bit))
            bit //= 2
    return names


def my_bit(name):
    return (lax.axis_index(name[0]) // name[1]) % 2


def total_sum(value, sent):
    value = after(value, *sent[:1])
    value = sum((flip(value, "dp", hop) for hop in range(1, lax.axis_size("dp"))), value)
    value = after(value, *sent[1:2])
    hops = range(1, lax.axis_size("seq") // 2)
    value = sum((flip(value, "seq", 2 * hop) for hop in hops), value)
    return value + flip(value, "seq", 1)


class ScatterSum:
    def __init__(self, value, axes):
        self.names = bits_of(axes)
        core = self.names[-1]
        width = value.shape[-1]
        a = value.reshape((2,) * len(self.names) + (-1, width))
        d = len(self.names) - 1
        sent = lax.dynamic_index_in_dim(a, 1 - my_bit(core), d, False)
        sent, a = lax.optimization_barrier((sent, a))
        self.mine = lax.dynamic_index_in_dim(a, my_bit(core), d, False)
        self.arrived = flip(sent, *core)
        cut = width // LANES // 3 * LANES
        self.parts = [(0, cut), (cut, 2 * cut), (2 * cut, width)]

    def halves(self, a, d, name):
        b = my_bit(name)
        return (
            lax.dynamic_index_in_dim(a, b, d, False),
            lax.dynamic_index_in_dim(a, 1 - b, d, False),
        )

    def begin(self):
        rest = self.names[:-1]
        dp = [n for n in rest if n[0] == self.names[0][0]]
        seq = [n for n in rest if n[0] != self.names[0][0]]
        self.orders = [dp[::-1] + seq[::-1], dp + seq[::-1], seq[::-1] + dp]
        self.kept, self.got, sent = [], [], []
        for order, (begin, stop) in zip(self.orders, self.parts):
            a = self.mine[..., begin:stop] + self.arrived[..., begin:stop]
            mine, other = self.halves(a, rest.index(order[0]), order[0])
            self.kept.append(mine)
            sent.append(other)
        sent = lax.optimization_barrier(tuple(sent))
        self.got = [flip(other, *order[0]) for other, order in zip(sent, self.orders)]
        return sent

    def second(self, *beside):
        *got, beside = lax.optimization_barrier((*self.got, beside))
        self.live = []
        sent = []
        for k, order in enumerate(self.orders):
            live = [name for name in self.names[:-1] if name != order[0]]
            a = self.kept[k] + got[k]
            if len(order) > 1:
                d = live.index(order[1])
                self.kept[k], other = self.halves(a, d, order[1])
                live.pop(d)
                sent.append(other)
            self.live.append(live)
        sent = lax.optimization_barrier(tuple(sent))
        self.got = [flip(other, *order[1]) for other, order in zip(sent, self.orders)]
        return sent, beside

    def finish(self, *beside):
        *got, beside = lax.optimization_barrier((*self.got, beside))
        groups = []
        for order, live, kept, arrived in zip(self.orders, self.live, self.kept, got):
            if groups and groups[-1][0] == order[2:]:
                groups[-1][2].append(kept + arrived)
            else:
                groups.append((order[2:], live, [kept + arrived]))
        pieces, sent = [], []
        for k, (order, live, parts) in enumerate(groups):
            a = jnp.concatenate(parts, axis=-1) if len(parts) > 1 else parts[0]
            for name in order:
                d = live.index(name)
                mine, other = self.halves(a, d, name)
                if k == 0:
                    other = lax.optimization_barrier(other)
                    sent.append(other)
                a = mine + flip(other, *name)
                live.pop(d)
            pieces.append(a)
        return jnp.concatenate(pieces, axis=-1), sent, beside


def after(value, *others):
    return lax.optimization_barrier((value,) + others)[0]


def in_order(blocks, me):
    bit = 1
    while bit < len(blocks):
        swap = (me // bit) % 2 == 1
        blocks = [jnp.where(swap, blocks[i ^ bit], block) for i, block in enumerate(blocks)]
        bit *= 2
    return jnp.stack(blocks)


def gather(value):
    seq, dp = lax.axis_size("seq"), lax.axis_size("dp")
    me = lax.axis_index("seq")
    chips = [value] + [flip(value, "seq", 2 * hop) for hop in range(1, seq // 2)]
    held = in_order(chips, me // 2)
    held = in_order(
        [held] + [flip(held, "dp", hop) for hop in range(1, dp)], lax.axis_index("dp")
    )
    other = flip(held, "seq", 1)
    even = me % 2 == 0
    both = jnp.stack([jnp.where(even, held, other), jnp.where(even, other, held)], axis=2)
    return both.reshape(-1, value.shape[1])


def lanes_of(log_decay):
    return jnp.repeat(jnp.exp(log_decay[:, :HEADS]), HEADDIM, axis=1)[:, None, :]


class Entering:
    def __init__(self, state, logs, axis, reverse):
        self.axis = axis
        self.sign = -1 if reverse else 1
        self.state, self.logs = state, logs
        self.odd = lax.axis_index(axis) % 2
        self.late = self.odd == (0 if reverse else 1)
        self.partner = flip(state, axis, 1)
        self.partner_logs = flip(logs, axis, 1)
        self.chips = lax.axis_size(axis) // 2

    def half(self, value):
        return lax.dynamic_slice_in_dim(value, self.odd * (DI // 2), DI // 2, 2)

    def chip_total(self, *beside):
        self.partner, *beside = lax.optimization_barrier((self.partner,) + beside)
        here, there = self.half(self.state), self.half(self.partner)
        decay_here = self.half(lanes_of(self.logs))
        decay_there = self.half(lanes_of(self.partner_logs))
        total = jnp.where(self.late, decay_here * there + here, decay_there * here + there)
        self.total, self.decay = total, decay_here * decay_there
        self.got = shifted(total, self.axis, 2 * self.sign)
        return beside

    def first_hop(self, *beside):
        self.window, *beside = lax.optimization_barrier((self.got,) + beside)
        self.window_decay = shifted(self.decay, self.axis, 2 * self.sign)
        self.tail = self.decay * self.window + self.total
        self.tail_decay = self.decay * self.window_decay
        return beside

    def last_hops(self, *beside):
        hop = 2
        while hop < self.chips:
            got = shifted(self.tail, self.axis, 2 * self.sign * hop)
            if hop == 2:
                got, *beside = lax.optimization_barrier((got,) + beside)
            got_decay = shifted(self.tail_decay, self.axis, 2 * self.sign * hop)
            self.window = self.window_decay * got + self.window
            self.window_decay = self.window_decay * got_decay
            hop *= 2
            if hop < self.chips:
                self.tail = self.tail_decay * got + self.tail
                self.tail_decay = self.tail_decay * got_decay
        self.whole = flip(self.window, self.axis, 1)
        return beside

    def result(self, *beside):
        self.whole, *beside = lax.optimization_barrier((self.whole,) + beside)
        both = jnp.where(
            self.odd == 0,
            jnp.concatenate([self.window, self.whole], axis=2),
            jnp.concatenate([self.whole, self.window], axis=2),
        )
        state = jnp.where(self.late, lanes_of(self.partner_logs) * both + self.partner, both)
        return [state] + beside


def on_device(
    hidden_in,
    lengths,
    w_in,
    conv_w,
    conv_b,
    g_norm,
    g_gate,
    w_out,
    a_log,
    dt_bias,
    d_skip,
    out_cotangent,
):
    axes = ("dp", "seq")
    devices = lax.axis_size("dp") * lax.axis_size("seq")
    slots, tokens, _ = hidden_in.shape
    blocks = tokens // T
    rows = slots * tokens
    grid = (slots, blocks)
    share = D // devices

    small = jnp.concatenate(
        [conv_w.reshape(-1), conv_b, g_norm, g_gate], axis=0
    )
    per_row = -(-small.shape[0] // share)
    small = jnp.pad(small, (0, per_row * share - small.shape[0])).reshape(share, per_row)
    wide = CONV_CH + LANES
    front = jnp.pad(w_in[:, DI:], ((0, 0), (0, LANES - HEADS)))
    earlier = shifted(hidden_in[:, tokens - 8 :, :], "seq", 1)
    front_full = gather(jnp.concatenate([front, small], axis=1))
    extra = front_full[:, wide:].reshape(devices, -1)
    lane = CONV_CH // devices
    taps_full = jnp.moveaxis(extra[:, : CONV * lane].reshape(devices, CONV, lane), 0, 1)
    taps_full = taps_full.reshape(CONV, CONV_CH).astype(F32)
    at = CONV * lane
    bias_full = extra[:, at : at + lane].reshape(1, CONV_CH).astype(F32)
    at += lane
    norm_gain = extra[:, at : at + share].reshape(D).astype(F32)
    at += share
    gate_gain = extra[:, at : at + DI // devices].reshape(1, DI).astype(F32)
    back = jnp.concatenate([w_in[:, :DI], w_out.T], axis=1)
    back = lax.all_gather(back, axes, axis=0, tiled=True)
    w_gate, w_out_turned = lax.optimization_barrier((back[:, :DI], back[:, DI:]))

    taps_rows = jnp.concatenate([taps_full, bias_full, jnp.zeros((3, CONV_CH), F32)], axis=0)
    rate = -jnp.exp(a_log)
    heads_rows = jnp.pad(jnp.stack([dt_bias, rate, d_skip]), ((0, 5), (0, LANES - HEADS)))
    skip_row = jnp.repeat(d_skip, HEADDIM)[None]
    gain_rows = jnp.concatenate([gate_gain, skip_row, jnp.zeros((6, DI), F32)], axis=0)
    select = (
        jnp.arange(DI, dtype=jnp.int32)[:, None] // HEADDIM
        == jnp.arange(LANES, dtype=jnp.int32)[None]
    ).astype(BF16)

    place = lax.axis_index("seq") * tokens + jnp.arange(tokens, dtype=jnp.int32)
    keep = (place[None, :] < lengths[:, None]).astype(F32)
    residual = hidden_in.astype(F32)

    def tile(width, dtype=F32, flip_order=False, height=T):
        if flip_order:
            spec = pl.BlockSpec((1, height, width), lambda s, c: (s, blocks - 1 - c, 0))
        else:
            spec = pl.BlockSpec((1, height, width), lambda s, c: (s, c, 0))
        return spec, jax.ShapeDtypeStruct((slots, tokens, width), dtype)

    def per_block(height, width, flip_order=False):
        if flip_order:
            spec = pl.BlockSpec((1, 1, height, width), lambda s, c: (s, blocks - 1 - c, 0, 0))
        else:
            spec = pl.BlockSpec((1, 1, height, width), lambda s, c: (s, c, 0, 0))
        return spec, jax.ShapeDtypeStruct((slots, blocks, height, width), F32)

    def columns(width, whole, index):
        spec = pl.BlockSpec((1, T, width), lambda s, c: (s, blocks - 1 - c, index))
        return spec, jax.ShapeDtypeStruct((slots, tokens, whole), F32)

    def per_slot(height, width, dtype=F32):
        spec = pl.BlockSpec((1, height, width), lambda s, c: (s, 0, 0))
        return spec, jax.ShapeDtypeStruct((slots, height, width), dtype)

    def fixed(height, width):
        spec = pl.BlockSpec((height, width), lambda s, c: (0, 0))
        return spec, jax.ShapeDtypeStruct((height, width), F32)

    def specs(*pairs):
        return [spec for spec, _ in pairs]

    normed, conv_in, halo, step_raw, x, bc, log, step, aux, enter, final, total = call(
        states_kernel,
        grid,
        specs(
            tile(D), per_slot(8, D), fixed(D, wide), fixed(1, D), fixed(8, CONV_CH), fixed(8, LANES)
        ),
        [
            tile(D, BF16), tile(CONV_CH, BF16), per_slot(8, CONV_CH, BF16), tile(LANES), tile(DI),
            tile(2 * STATE), tile(LANES), tile(LANES), per_block(8, LANES), per_block(STATE, DI),
            per_slot(STATE, DI), per_slot(8, LANES),
        ],
        [
            pltpu.VMEM((CONV_CH // LANES, T + 8, LANES), F32), pltpu.VMEM((STATE, DI), F32),
            pltpu.VMEM((8, LANES), F32),
        ],
        6 * rows * STATE * DI + 2 * rows * D * wide,
        rows * (CONV_CH * 6 + DI * 4),
    )(hidden_in, earlier, front_full, norm_gain[None], taps_rows, heads_rows)
    normed = normed.reshape(rows, D)
    logs = total[:, 0, :]
    forward = Entering(final, logs, "seq", False)
    gate_pre = jnp.dot(after(normed, final), w_gate, preferred_element_type=F32)
    (gate_pre,) = forward.chip_total(gate_pre.reshape(slots, tokens, DI))
    cotangent = out_cotangent.astype(F32)
    branch_grad = (cotangent * keep[..., None]).astype(BF16).reshape(rows, D)
    norm_grad = jnp.dot(
        after(branch_grad, forward.total), w_out_turned, preferred_element_type=F32
    )
    normed_turned = after(normed, forward.total).T
    norm_grad, normed_turned = forward.first_hop(
        norm_grad.reshape(slots, tokens, DI), normed_turned
    )
    (local,) = call(
        local_kernel,
        grid,
        specs(
            tile(DI), tile(2 * STATE), tile(LANES), tile(LANES), per_block(STATE, DI), fixed(8, DI)
        ),
        [tile(DI)],
        [],
        12 * rows * T * DI,
        rows * (CONV_CH + 2 * DI) * 4,
    )(after(x, forward.tail), bc, log, step, enter, gain_rows)
    (local,) = forward.last_hops(local)
    (start,) = forward.result()

    gated_norm, mixed_grad, gate_grad, lg, adj_enter, adj_final, gate_sums = call(
        gate_kernel,
        grid,
        specs(
            columns(STATE, 2 * STATE, 1), tile(LANES, flip_order=True),
            per_block(8, LANES, True), tile(DI, flip_order=True), tile(DI, flip_order=True),
            tile(DI, flip_order=True), per_slot(STATE, DI), fixed(8, DI), fixed(DI, LANES),
        ),
        [
            tile(DI, BF16, True), tile(DI, F32, True), tile(DI, BF16, True),
            tile(LANES, F32, True), per_block(STATE, DI, True), per_slot(STATE, DI), fixed(8, DI),
        ],
        [
            pltpu.VMEM((T, DI), F32), pltpu.VMEM((T, DI), F32), pltpu.VMEM((STATE, DI), F32),
            pltpu.VMEM((T, DI), BF16), pltpu.VMEM((T, DI), BF16),
        ],
        12 * rows * STATE * DI,
        rows * (CONV_CH * 4 + DI * 24),
    )(bc, log, aux, local, gate_pre, norm_grad, start, gain_rows, select)
    gated_norm = gated_norm.reshape(rows, DI)
    gate_grad = gate_grad.reshape(rows, DI)
    backward = Entering(adj_final, logs, "seq", True)

    w_out_grad = lax.dot_general(
        branch_grad, gated_norm, (((0,), (0,)), ((), ())), preferred_element_type=F32
    )
    (w_out_grad,) = backward.chip_total(w_out_grad)
    w_gate_grad = lax.dot_general(
        normed_turned, after(gate_grad, backward.total), NN, preferred_element_type=F32
    )
    branch = lax.dot_general(
        after(gated_norm, backward.total), w_out_turned, NT, preferred_element_type=F32
    )
    block_out = (residual + keep[..., None] * branch.reshape(slots, tokens, D)).astype(BF16)
    early = jnp.concatenate([w_gate_grad, w_out_grad], axis=1)
    early, block_out = backward.first_hop(early, block_out)
    early = lax.psum_scatter(early, axes, scatter_dimension=0, tiled=True)

    xadj, bc_grad, skipped = call(
        adjoint_kernel,
        grid,
        specs(
            tile(DI), tile(2 * STATE), tile(LANES), tile(LANES), per_block(8, LANES), tile(DI),
            per_block(STATE, DI), per_slot(STATE, DI), per_block(STATE, DI), fixed(DI, LANES),
        ),
        [tile(DI), tile(2 * STATE), tile(LANES)],
        [pltpu.VMEM((height, DI), BF16) for height in (T, T, T, STATE, 2 * T, 2 * STATE)],
        30 * rows * T * DI,
        rows * (CONV_CH + 4 * DI) * 4,
    )(
        x, bc, log, step, aux, after(mixed_grad, backward.tail), enter, start, adj_enter, select
    )
    (xadj,) = backward.last_hops(xadj)
    (end_adj,) = backward.result()

    prev = pl.BlockSpec(
        (1, 16, CONV_CH), lambda s, c: (s, jnp.maximum((blocks - 1 - c) * (T // 16) - 1, 0), 0)
    )
    def flipped(width, dtype=F32):
        return tile(width, dtype, True)

    slices = CONV_CH // LANES
    proj_grad, head_rows, last_rows, conv_sums, head_sums = call(
        finish_kernel,
        grid,
        specs(
            flipped(DI), flipped(2 * STATE), flipped(LANES), flipped(LANES),
            per_block(8, LANES, True), per_slot(8, LANES), flipped(DI), flipped(DI),
            flipped(2 * STATE), flipped(LANES), flipped(LANES), per_slot(STATE, DI),
            per_slot(STATE, DI), per_slot(STATE, DI), flipped(CONV_CH), (prev, None),
            per_slot(8, CONV_CH), flipped(LANES), fixed(8, CONV_CH), fixed(8, LANES), fixed(8, DI),
            fixed(DI, LANES),
        ),
        [
            flipped(wide, BF16), per_slot(8, CONV_CH), per_slot(8, CONV_CH), fixed(40, CONV_CH),
            fixed(24, LANES),
        ],
        [
            pltpu.VMEM((slices, T + 16, LANES), F32), pltpu.VMEM((slices, T + 8, LANES), F32),
            pltpu.VMEM((8, CONV_CH), F32), pltpu.VMEM((T, DI), BF16), pltpu.VMEM((T, DI), BF16),
            pltpu.VMEM((8, LANES), F32),
        ],
        12 * rows * STATE * DI,
        rows * (CONV_CH * 8 + DI * 8),
    )(
        x, bc, log, step, aux, total, mixed_grad, xadj, bc_grad, lg, skipped, end_adj, start,
        final, conv_in, conv_in, halo, step_raw, taps_rows, heads_rows, gain_rows, select,
    )

    ahead = shifted(head_rows, "seq", -1)
    ahead = jnp.concatenate([jnp.zeros((slots, 8, CONV_CH), F32), ahead], axis=1)
    for tap in range(CONV):
        begin = CONV - 1 - tap
        last_rows = last_rows + ahead[:, begin : begin + 8] * taps_full[tap]
    proj_grad = lax.dynamic_update_slice(
        proj_grad, last_rows.astype(BF16), (0, tokens - 8, 0)
    ).reshape(rows, wide)

    w_front_grad = jnp.dot(normed_turned, proj_grad, preferred_element_type=F32)
    scatter = ScatterSum(w_front_grad, axes)
    tall = min(2 * T, rows // 2)

    strips = rows // tall // 2

    def input_half(half, sent, *done):
        def strip(width, dtype=BF16):
            spec = pl.BlockSpec((tall, width), lambda r: (r + half * strips, 0))
            return spec, jax.ShapeDtypeStruct((rows, width), dtype)

        def whole(height, width):
            spec = pl.BlockSpec((height, width), lambda r: (0, 0))
            return spec, jax.ShapeDtypeStruct((height, width), F32)

        ins = [
            strip(wide), strip(DI), whole(D, wide), whole(D, DI), strip(D), strip(D), whole(1, D)
        ]
        return call(
            input_kernel,
            (strips,),
            specs(*ins) + [pl.BlockSpec(memory_space=pl.ANY)] * len(done),
            [strip(D, F32), whole(8, D)],
            [],
            rows * D * (wide + DI),
            (rows * (wide + DI) * 2 + rows * D * 8) // 2,
            {len(ins): 0} if done else None,
        )(
            after(proj_grad, *sent), gate_grad, front_full, w_gate, hidden_in.reshape(rows, D),
            out_cotangent.reshape(rows, D), norm_gain[None], *done,
        )

    input_grad, norm_sums = input_half(0, scatter.begin())
    sent, (input_grad, norm_sums, early) = scatter.second(input_grad, norm_sums, early)
    w_gate_owned, w_out_owned = early[:, :DI], early[:, DI:]
    input_grad, more_sums = input_half(1, sent, input_grad)
    front_owned, sent, (input_grad, norm_sums) = scatter.finish(input_grad, norm_sums + more_sums)
    input_grad = input_grad.reshape(slots, tokens, D)

    vectors = jnp.concatenate(
        [
            conv_sums.reshape(CONV + 1, 8, CONV_CH).sum(1).reshape(-1), norm_sums.sum(0),
            gate_sums.sum(0), head_sums.reshape(3, 8, LANES).sum(1).reshape(-1),
        ]
    )
    vectors = total_sum(vectors.reshape(-1, LANES), sent).reshape(-1)
    me = lax.axis_index("dp") * lax.axis_size("seq") + lax.axis_index("seq")

    def owned(begin, length):
        per = length // devices
        return lax.dynamic_slice_in_dim(vectors, begin + me * per, per)

    norm_at = (CONV + 1) * CONV_CH
    gate_at = norm_at + D
    heads_at = gate_at + DI
    return (
        block_out,
        input_grad,
        jnp.concatenate([w_gate_owned, front_owned[:, : CONV_CH + HEADS]], axis=1),
        jnp.stack([owned(k * CONV_CH, CONV_CH) for k in range(CONV)]),
        owned(CONV * CONV_CH, CONV_CH),
        owned(norm_at, D),
        owned(gate_at, DI),
        w_out_owned.T,
        vectors[heads_at : heads_at + HEADS],
        vectors[heads_at + LANES : heads_at + LANES + HEADS],
        vectors[heads_at + 2 * LANES : heads_at + 2 * LANES + HEADS],
    )


def solution(mesh):
    placed = (
        P("dp", "seq", None),
        P("dp"),
        P(("dp", "seq"), None),
        P(None, ("dp", "seq")),
        P(("dp", "seq")),
        P(("dp", "seq")),
        P(("dp", "seq")),
        P(None, ("dp", "seq")),
        P(),
        P(),
        P(),
        P("dp", "seq", None),
    )
    return jax.shard_map(
        on_device,
        mesh=mesh,
        in_specs=placed,
        out_specs=(
            P("dp", "seq", None),
            P("dp", "seq", None),
            P(("dp", "seq"), None),
            P(None, ("dp", "seq")),
            P(("dp", "seq")),
            P(("dp", "seq")),
            P(("dp", "seq")),
            P(None, ("dp", "seq")),
            P(),
            P(),
            P(),
        ),
        check_vma=False,
    )
```

```python
import functools

import jax
import jax.numpy as jnp
from jax import lax
from jax.experimental import pallas as pl
from jax.experimental.pallas import tpu as pltpu
from jax.sharding import PartitionSpec as P

D = 768
HEADS = 24
HEADDIM = 64
STATE = 128
CONV = 4
DI = 1536
CONV_CH = 1792
PROJ = 3352
T = 128
PAIRS = HEADS // 2
LANES = 128
EPSILON = 1e-05
MASKED = -1e30
F32 = jnp.float32
BF16 = jnp.bfloat16
NN = (((1,), (0,)), ((), ()))
NT = (((1,), (1,)), ((), ()))


def mm(a, b, dims=NN):
    return lax.dot_general(a, b, dims, preferred_element_type=F32)


def split(v):
    high = v.astype(BF16)
    return high, (v - high.astype(F32)).astype(BF16)


def mm3(a, b, dims=NN):
    return mm(a[0], b[0], dims) + (mm(a[0], b[1], dims) + mm(a[1], b[0], dims))


def left_half(rows):
    return lax.broadcasted_iota(jnp.int32, (rows, LANES), 1) < HEADDIM


def spread(values, pair, left):
    return jnp.where(
        left, values[:, 2 * pair : 2 * pair + 1], values[:, 2 * pair + 1 : 2 * pair + 2]
    )


def pick(values, pair, left):
    index = jnp.where(left, 2 * pair, 2 * pair + 1)
    return jnp.take_along_axis(values, index, axis=1, mode="promise_in_bounds")


def two_columns(values, pair):
    return [
        jnp.broadcast_to(values[:, head : head + 1], (values.shape[0], LANES))
        for head in (2 * pair, 2 * pair + 1)
    ]


def cols(j):
    return slice(j * LANES, (j + 1) * LANES)


def running(v, reverse):
    row = lax.broadcasted_iota(jnp.int32, v.shape, 0)
    hop = 1
    while hop < T:
        moved = pltpu.roll(v, T - hop if reverse else hop, 0)
        inside = row < T - hop if reverse else row >= hop
        v = v + jnp.where(inside, moved, 0.0)
        hop *= 2
    return v


def fold(v):
    return jnp.sum(v.reshape(v.shape[0] // 8, 8, v.shape[-1]), axis=0)


def two_heads(high, low, left):
    zero = jnp.zeros_like(high)
    top = jnp.concatenate([jnp.where(left, high, zero), jnp.where(left, low, zero)], axis=1)
    bottom = jnp.concatenate([jnp.where(left, zero, high), jnp.where(left, zero, low)], axis=1)
    return jnp.concatenate([top, bottom], axis=0)


def sigmoid(v):
    return 0.5 * jnp.tanh(0.5 * v) + 0.5


def convolve(window, taps_ref, j, first):
    at = cols(j)
    total = taps_ref[CONV : CONV + 1, at]
    rows = [window[j, first + tap : first + tap + T, :] for tap in range(CONV)]
    for tap in range(CONV):
        total = total + rows[tap] * taps_ref[tap : tap + 1, at]
    return total, rows


def states_kernel(
    hidden_ref, before_ref, front_ref, gain_ref, taps_ref, heads_ref,
    normed_ref, conv_ref, halo_ref, dt_ref, x_ref, bc_ref, log_ref, step_ref, aux_ref, enter_ref,
    final_ref, total_ref,
    window, state, before,
):
    c = pl.program_id(1)

    def norm(rows):
        rows = rows.astype(F32)
        inv = lax.rsqrt(jnp.mean(rows * rows, axis=-1, keepdims=True) + EPSILON)
        return (rows * inv * gain_ref[0:1, :]).astype(BF16)

    @pl.when(c == 0)
    def _():
        earlier = norm(before_ref[0])
        for j in range(CONV_CH // LANES):
            rows = mm(earlier, front_ref[:, cols(j)]).astype(BF16)
            halo_ref[0, :, cols(j)] = rows
            window[j, 0:8, :] = rows.astype(F32)
        state[...] = jnp.zeros_like(state)
        before[...] = jnp.zeros_like(before)

    normed = norm(hidden_ref[0])
    normed_ref[0] = normed
    for k in range(CONV_CH // LANES // 2):
        two = slice(2 * k * LANES, 2 * (k + 1) * LANES)
        rows = mm(normed, front_ref[:, two]).astype(BF16)
        conv_ref[0, :, two] = rows
        for j in (2 * k, 2 * k + 1):
            window[j, 8 : 8 + T, :] = rows[:, cols(j - 2 * k)].astype(F32)
            pre, _ = convolve(window, taps_ref, j, 8 - (CONV - 1))
            if j < PAIRS:
                x_ref[0, :, cols(j)] = pre * sigmoid(pre)
            else:
                bc_ref[0, :, cols(j - PAIRS)] = pre * sigmoid(pre)
            window[j, 0:8, :] = window[j, T : T + 8, :]

    dt = mm(normed, front_ref[:, CONV_CH : CONV_CH + LANES])
    dt_ref[0] = dt
    step = jax.nn.softplus(dt + heads_ref[0:1, :])
    log = running(step * heads_ref[1:2, :], False)
    end = log[T - 1 : T, :]
    step_ref[0] = step
    log_ref[0] = log
    weight = jnp.exp(end - log) * step
    decay = jnp.exp(end)
    left = left_half(T)
    aux_ref[0, 0] = jnp.concatenate([before[0:1, :], end, jnp.zeros((6, LANES), F32)], axis=0)
    before[0:1, :] = before[0:1, :] + end
    b_turned = split(bc_ref[0, :, 0:STATE].T)
    for j in range(PAIRS):
        prior = state[:, cols(j)]
        enter_ref[0, 0, :, cols(j)] = prior
        fed = split(x_ref[0, :, cols(j)] * spread(weight, j, left))
        state[:, cols(j)] = prior * spread(decay, j, left[0:1]) + mm3(b_turned, fed)

    @pl.when(c == pl.num_programs(1) - 1)
    def _():
        final_ref[0] = state[...]
        total_ref[0] = before[...]


def local_kernel(x_ref, bc_ref, log_ref, step_ref, enter_ref, rows_ref, out_ref):
    log = log_ref[0]
    log_turned = log.T
    step = step_ref[0]
    left = left_half(T)
    row = lax.broadcasted_iota(jnp.int32, (T, T), 0)
    col = lax.broadcasted_iota(jnp.int32, (T, T), 1)
    causal = row >= col
    b_pair = split(bc_ref[0, :, 0:STATE])
    c_pair = split(bc_ref[0, :, STATE:])
    inner = mm3(c_pair, b_pair, NT)
    for j in range(PAIRS):
        x = x_ref[0, :, cols(j)]
        fed = split(x * spread(step, j, left))
        rhs = two_heads(fed[0], fed[1], left)
        mats = []
        logs = two_columns(log, j)
        for k in range(2):
            gap = logs[k] - log_turned[2 * j + k : 2 * j + k + 1, :]
            mats.append(inner * jnp.exp(jnp.where(causal, gap, MASKED)))
        mixing = split(jnp.concatenate(mats, axis=1))
        wide = mm(mixing[0], rhs)
        out = wide[:, :LANES] + (wide[:, LANES:] + mm(mixing[1], rhs[:, :LANES]))
        crossed = mm3(c_pair, split(enter_ref[0, 0, :, cols(j)]))
        skipped = rows_ref[1:2, cols(j)] * x
        out_ref[0, :, cols(j)] = (out + skipped) + jnp.exp(jnp.where(left, *logs)) * crossed


def gate_kernel(
    c_ref, log_ref, aux_ref, local_ref, gate_ref, ng_ref, start_ref, rows_ref, sel_ref,
    normed_ref, mixed_grad_ref, gate_grad_ref, lg_ref, enter_ref, final_ref, sums_ref,
    mixed_s, gated_s, adj, q_high, q_low,
):
    s, c = pl.program_id(0), pl.program_id(1)

    @pl.when(c == 0)
    def _():
        adj[...] = jnp.zeros_like(adj)

    @pl.when((s == 0) & (c == 0))
    def _():
        sums_ref[...] = jnp.zeros_like(sums_ref)

    log = log_ref[0]
    before = aux_ref[0, 0, 0:1, :]
    end = aux_ref[0, 0, 1:2, :]
    left = left_half(T)
    since = jnp.exp(before + log)
    grown = jnp.exp(log)
    decay = jnp.exp(end)
    c_rows = c_ref[0]
    c_pair = split(c_rows)
    c_turned = split(c_rows.T)
    squares = jnp.zeros((T, LANES), F32)
    products = jnp.zeros((T, LANES), F32)
    for j in range(PAIRS):
        at = cols(j)
        crossed = mm3(c_pair, split(start_ref[0, :, at]))
        mixed = local_ref[0, :, at] + spread(since, j, left) * crossed
        gate = gate_ref[0, :, at]
        gated = mixed * (gate * sigmoid(gate))
        mixed_s[:, at] = mixed
        gated_s[:, at] = gated
        squares = squares + gated * gated
        products = products + ng_ref[0, :, at] * rows_ref[0:1, at] * gated
    inv = lax.rsqrt(jnp.sum(squares, axis=-1, keepdims=True) / DI + EPSILON)
    mean = jnp.sum(products, axis=-1, keepdims=True) / DI
    pull = inv * inv * mean
    for j in range(PAIRS):
        at = cols(j)
        mixed = mixed_s[:, at]
        gated = gated_s[:, at]
        gate = gate_ref[0, :, at]
        gain = rows_ref[0:1, at]
        ng = ng_ref[0, :, at]
        sig = sigmoid(gate)
        unit = gated * inv
        normed_ref[0, :, at] = (unit * gain).astype(BF16)
        sums_ref[:, at] = sums_ref[:, at] + fold(ng * unit)
        gated_grad = inv * (ng * gain - gated * pull)
        mixed_grad = gated_grad * (gate * sig)
        mixed_grad_ref[0, :, at] = mixed_grad
        gate_grad_ref[0, :, at] = (
            gated_grad * mixed * sig * (1.0 + gate * (1.0 - sig))
        ).astype(BF16)
        q = split(mixed_grad * mixed)
        q_high[:, at] = q[0]
        q_low[:, at] = q[1]
        prior = adj[:, at]
        enter_ref[0, 0, :, at] = prior
        fed = split(mixed_grad * spread(grown, j, left))
        adj[:, at] = prior * spread(decay, j, left[0:1]) + mm3(c_turned, fed)
    lg_ref[0] = mm(q_high[...], sel_ref[...]) + mm(q_low[...], sel_ref[...])

    @pl.when(c == pl.num_programs(1) - 1)
    def _():
        final_ref[0] = adj[...]


def adjoint_kernel(
    x_ref, bc_ref, log_ref, step_ref, aux_ref, grad_ref, enter_ref, start_ref, adj_ref, sel_ref,
    xadj_ref, bc_grad_ref, skip_ref,
    q_high, q_low, fed_s, adj_s, grads_s, states_s,
):
    log = log_ref[0]
    log_turned = log.T
    step = step_ref[0]
    before = aux_ref[0, 0, 0:1, :]
    end = aux_ref[0, 0, 1:2, :]
    left = left_half(T)
    row = lax.broadcasted_iota(jnp.int32, (T, T), 0)
    col = lax.broadcasted_iota(jnp.int32, (T, T), 1)
    later = col >= row
    b_pair = split(bc_ref[0, :, 0:STATE])
    c_pair = split(bc_ref[0, :, STATE:])
    inner = mm3(b_pair, c_pair, NT)
    reach = jnp.exp(before)
    weighted = jnp.zeros((T, T), F32)
    for j in range(PAIRS):
        at = cols(j)
        grad = grad_ref[0, :, at]
        x = x_ref[0, :, at]
        q = split(x * grad)
        q_high[:, at] = q[0]
        q_low[:, at] = q[1]
        fed = x * spread(step, j, left)
        high, low = split(grad)
        rhs = two_heads(high, low, left)
        decays = []
        logs = two_columns(log, j)
        for k in range(2):
            gap = log_turned[2 * j + k : 2 * j + k + 1, :] - logs[k]
            decays.append(jnp.exp(jnp.where(later, gap, MASKED)))
        both = jnp.where(left, *logs)
        mixing = split(jnp.concatenate([inner * decays[0], inner * decays[1]], axis=1))
        wide = mm(mixing[0], rhs)
        out = wide[:, :LANES] + (wide[:, LANES:] + mm(mixing[1], rhs[:, :LANES]))
        short = fed.astype(BF16)
        zero = jnp.zeros_like(short)
        stacked = jnp.concatenate(
            [jnp.where(left, short, zero), jnp.where(left, zero, short)], axis=0
        )
        dots = mm(stacked, high, NT)
        weighted = weighted + (decays[0] * dots[:T] + decays[1] * dots[T:])
        adj = split(adj_ref[0, 0, :, at])
        reached = jnp.exp(spread(end, j, left[0:1]) - both)
        xadj_ref[0, :, at] = out + reached * mm3(b_pair, adj)
        fed_s[:, at] = (fed * reached).astype(BF16)
        adj_s[:, at] = adj[0]
        entering = enter_ref[0, 0, :, at] + spread(reach, j, left[0:1]) * start_ref[0, :, at]
        states_s[0:STATE, at], states_s[STATE:, at] = split(entering)
        grads_s[0:T, at], grads_s[T:, at] = split(grad * jnp.exp(both))
    b_total = mm(fed_s[...], adj_s[...], NT)
    c_parts = mm(grads_s[...], states_s[...], NT)
    c_total = c_parts[:T, :STATE] + (c_parts[:T, STATE:] + c_parts[T:, :STATE])
    skip_ref[0] = mm(q_high[...], sel_ref[...]) + mm(q_low[...], sel_ref[...])
    bc_grad_ref[0, :, 0:STATE] = b_total + mm(weighted.astype(BF16), c_pair[0])
    bc_grad_ref[0, :, STATE:] = c_total + mm(weighted.T.astype(BF16), b_pair[0])


def finish_kernel(
    x_ref, bc_ref, log_ref, step_ref, aux_ref, total_ref, grad_ref, xadj_ref, bc_grad_ref, lg_ref,
    skip_ref, end_ref, start_ref, final_ref, conv_ref, prev_ref, halo_ref, dt_ref, taps_ref, heads_ref,
    rows_ref, sel_ref,
    out_ref, head_ref, last_ref, sums_ref, head_sums_ref,
    window, pre_s, last_s, q_high, q_low, carry,
):
    slices = CONV_CH // LANES
    s, c = pl.program_id(0), pl.program_id(1)
    first = c == pl.num_programs(1) - 1

    @pl.when(c == 0)
    def _():
        pre_s[:, T : T + 8, :] = jnp.zeros((slices, 8, LANES), F32)
        passed = jnp.exp(total_ref[0])
        tail = jnp.zeros((8, LANES), F32)
        for j in range(PAIRS):
            at = cols(j)
            decay = spread(passed[0:1, :], j, left_half(1))
            leaving = decay * start_ref[0, :, at] + final_ref[0, :, at]
            high, low = split(fold(end_ref[0, :, at] * leaving))
            tail = tail + (mm(high, sel_ref[at, :]) + mm(low, sel_ref[at, :]))
        carry[...] = jnp.broadcast_to(jnp.sum(tail, axis=0, keepdims=True), (8, LANES))

    @pl.when((s == 0) & (c == 0))
    def _():
        sums_ref[...] = jnp.zeros_like(sums_ref)
        head_sums_ref[...] = jnp.zeros_like(head_sums_ref)

    @pl.when(first)
    def _():
        for j in range(slices):
            window[j, 8:16, :] = halo_ref[0, :, cols(j)].astype(F32)

    @pl.when(jnp.logical_not(first))
    def _():
        for j in range(slices):
            window[j, 8:16, :] = prev_ref[0, :, cols(j)].astype(F32)[8:16, :]

    log = log_ref[0]
    step = step_ref[0]
    before = aux_ref[0, 0, 0:1, :]
    end = aux_ref[0, 0, 1:2, :]
    left = left_half(T)
    remain = jnp.exp((total_ref[0, 0:1, :] - before - end) + (end - log))
    b_pair = split(bc_ref[0, :, 0:STATE])
    b_total = bc_grad_ref[0, :, 0:STATE]

    def through(j, act_grad):
        at = cols(j)
        window[j, 16 : 16 + T, :] = conv_ref[0, :, cols(j)].astype(F32)
        pre, before_rows = convolve(window, taps_ref, j, 16 - (CONV - 1))
        sig = sigmoid(pre)
        pre_grad = act_grad * sig * (1.0 + pre * (1.0 - sig))
        pre_s[j, 0:T, :] = pre_grad
        for tap in range(CONV):
            rows = slice(8 * tap, 8 * tap + 8)
            sums_ref[rows, at] = sums_ref[rows, at] + fold(pre_grad * before_rows[tap])
        sums_ref[32:40, at] = sums_ref[32:40, at] + fold(pre_grad)
        into = pre_grad * taps_ref[CONV - 1 : CONV, cols(j)]
        for tap in range(CONV - 1):
            ahead = CONV - 1 - tap
            into = into + pre_s[j, ahead : ahead + T, :] * taps_ref[tap : tap + 1, cols(j)]
        out_ref[0, :, at] = into.astype(BF16)
        last_s[:, at] = into[T - 8 :, :]
        pre_s[j, T : T + 8, :] = pre_grad[0:8, :]

    for j in range(PAIRS):
        at = cols(j)
        x = x_ref[0, :, at]
        stepped = pick(step, j, left)
        left_over = pick(remain, j, left)
        end_pair = split(end_ref[0, :, at])
        xadj = xadj_ref[0, :, at] + left_over * mm3(b_pair, end_pair)
        b_total = b_total + mm((x * stepped * left_over).astype(BF16), end_pair[0], NT)
        q = split(x * xadj)
        q_high[:, at] = q[0]
        q_low[:, at] = q[1]
        through(j, stepped * xadj + rows_ref[1:2, at] * grad_ref[0, :, at])
    through(PAIRS, b_total)
    through(PAIRS + 1, bc_grad_ref[0, :, STATE:])

    direct = mm(q_high[...], sel_ref[...]) + mm(q_low[...], sel_ref[...])
    skipped = skip_ref[0]
    log_grad = lg_ref[0] - heads_ref[2:3, :] * skipped - step * direct
    log_grad = running(log_grad, True) + carry[0:1, :]
    carry[0:1, :] = log_grad[0:1, :]
    rate = heads_ref[1:2, :]
    step_grad = direct + log_grad * rate
    step_pre_grad = step_grad * sigmoid(dt_ref[0] + heads_ref[0:1, :])
    out_ref[0, :, CONV_CH:] = step_pre_grad.astype(BF16)
    head_sums_ref[0:8, :] = head_sums_ref[0:8, :] + fold(log_grad * step * rate)
    head_sums_ref[8:16, :] = head_sums_ref[8:16, :] + fold(step_pre_grad)
    head_sums_ref[16:24, :] = head_sums_ref[16:24, :] + fold(skipped)

    @pl.when(c == 0)
    def _():
        last_ref[0] = last_s[...]

    @pl.when(first)
    def _():
        for j in range(slices):
            head_ref[0, :, cols(j)] = pre_s[j, 0:8, :]


def input_kernel(
    proj_ref, gate_ref, front_ref, w_gate_ref, hidden_ref, cot_ref, gain_ref, *refs
):
    out_ref, sums_ref = refs[-2:]
    @pl.when(pl.program_id(0) == 0)
    def _():
        sums_ref[...] = jnp.zeros_like(sums_ref)

    x = hidden_ref[...].astype(F32)
    inv = lax.rsqrt(jnp.mean(x * x, axis=-1, keepdims=True) + EPSILON)
    unit = x * inv
    grad = mm(proj_ref[...], front_ref[...], NT) + mm(gate_ref[...], w_gate_ref[...], NT)
    sums_ref[...] = sums_ref[...] + fold(grad * unit)
    scaled = grad * gain_ref[0:1, :]
    mean = jnp.mean(scaled * unit, axis=-1, keepdims=True)
    out_ref[...] = cot_ref[...].astype(F32) + inv * (scaled - unit * mean)


def call(kernel, grid, ins, outs, scratch, flops, moved, aliases=None):
    return pl.pallas_call(
        kernel,
        input_output_aliases=aliases or {},
        grid=grid,
        in_specs=ins,
        out_specs=[spec for spec, _ in outs],
        out_shape=[shape for _, shape in outs],
        scratch_shapes=scratch,
        compiler_params=pltpu.CompilerParams(
            dimension_semantics=("arbitrary",) * len(grid), vmem_limit_bytes=56 * 2**20
        ),
        cost_estimate=pl.CostEstimate(flops=flops, bytes_accessed=moved, transcendentals=0),
    )


def flip(value, axis, bit):
    count = lax.axis_size(axis)
    return lax.ppermute(value, axis, [(i, i ^ bit) for i in range(count)])


def shifted(value, axis, steps):
    count = lax.axis_size(axis)
    initial, last = (max(0, -steps), min(count, count - steps))
    return lax.ppermute(value, axis, [(source, source + steps) for source in range(initial, last)])


def bits_of(axes):
    names = []
    for axis in axes:
        bit = lax.axis_size(axis) // 2
        while bit:
            names.append((axis, bit))
            bit //= 2
    return names


def my_bit(name):
    return (lax.axis_index(name[0]) // name[1]) % 2


def total_sum(value, sent):
    value = after(value, *sent[:1])
    value = sum((flip(value, "dp", hop) for hop in range(1, lax.axis_size("dp"))), value)
    value = after(value, *sent[1:2])
    hops = range(1, lax.axis_size("seq") // 2)
    value = sum((flip(value, "seq", 2 * hop) for hop in hops), value)
    return value + flip(value, "seq", 1)


class ScatterSum:
    def __init__(self, value, axes):
        self.names = bits_of(axes)
        core = self.names[-1]
        width = value.shape[-1]
        a = value.reshape((2,) * len(self.names) + (-1, width))
        d = len(self.names) - 1
        sent = lax.dynamic_index_in_dim(a, 1 - my_bit(core), d, False)
        sent, a = lax.optimization_barrier((sent, a))
        self.mine = lax.dynamic_index_in_dim(a, my_bit(core), d, False)
        self.arrived = flip(sent, *core)
        cut = width // LANES // 3 * LANES
        self.parts = [(0, cut), (cut, 2 * cut), (2 * cut, width)]

    def halves(self, a, d, name):
        b = my_bit(name)
        return (
            lax.dynamic_index_in_dim(a, b, d, False),
            lax.dynamic_index_in_dim(a, 1 - b, d, False),
        )

    def begin(self):
        rest = self.names[:-1]
        dp = [n for n in rest if n[0] == self.names[0][0]]
        seq = [n for n in rest if n[0] != self.names[0][0]]
        self.orders = [dp[::-1] + seq[::-1], dp + seq[::-1], seq[::-1] + dp]
        self.kept, self.got, sent = [], [], []
        for order, (begin, stop) in zip(self.orders, self.parts):
            a = self.mine[..., begin:stop] + self.arrived[..., begin:stop]
            mine, other = self.halves(a, rest.index(order[0]), order[0])
            self.kept.append(mine)
            sent.append(other)
        sent = lax.optimization_barrier(tuple(sent))
        self.got = [flip(other, *order[0]) for other, order in zip(sent, self.orders)]
        return sent

    def second(self, *beside):
        *got, beside = lax.optimization_barrier((*self.got, beside))
        self.live = []
        sent = []
        for k, order in enumerate(self.orders):
            live = [name for name in self.names[:-1] if name != order[0]]
            a = self.kept[k] + got[k]
            if len(order) > 1:
                d = live.index(order[1])
                self.kept[k], other = self.halves(a, d, order[1])
                live.pop(d)
                sent.append(other)
            self.live.append(live)
        sent = lax.optimization_barrier(tuple(sent))
        self.got = [flip(other, *order[1]) for other, order in zip(sent, self.orders)]
        return sent, beside

    def finish(self, *beside):
        *got, beside = lax.optimization_barrier((*self.got, beside))
        groups = []
        for order, live, kept, arrived in zip(self.orders, self.live, self.kept, got):
            if groups and groups[-1][0] == order[2:]:
                groups[-1][2].append(kept + arrived)
            else:
                groups.append((order[2:], live, [kept + arrived]))
        pieces, sent = [], []
        for k, (order, live, parts) in enumerate(groups):
            a = jnp.concatenate(parts, axis=-1) if len(parts) > 1 else parts[0]
            for name in order:
                d = live.index(name)
                mine, other = self.halves(a, d, name)
                if k == 0:
                    other = lax.optimization_barrier(other)
                    sent.append(other)
                a = mine + flip(other, *name)
                live.pop(d)
            pieces.append(a)
        return jnp.concatenate(pieces, axis=-1), sent, beside


def after(value, *others):
    return lax.optimization_barrier((value,) + others)[0]


def in_order(blocks, me):
    bit = 1
    while bit < len(blocks):
        swap = (me // bit) % 2 == 1
        blocks = [jnp.where(swap, blocks[i ^ bit], block) for i, block in enumerate(blocks)]
        bit *= 2
    return jnp.stack(blocks)


def gather(value):
    seq, dp = lax.axis_size("seq"), lax.axis_size("dp")
    me = lax.axis_index("seq")
    chips = [value] + [flip(value, "seq", 2 * hop) for hop in range(1, seq // 2)]
    held = in_order(chips, me // 2)
    held = in_order(
        [held] + [flip(held, "dp", hop) for hop in range(1, dp)], lax.axis_index("dp")
    )
    other = flip(held, "seq", 1)
    even = me % 2 == 0
    both = jnp.stack([jnp.where(even, held, other), jnp.where(even, other, held)], axis=2)
    return both.reshape(-1, value.shape[1])


def lanes_of(log_decay):
    return jnp.repeat(jnp.exp(log_decay[:, :HEADS]), HEADDIM, axis=1)[:, None, :]


class Entering:
    def __init__(self, state, logs, axis, reverse):
        self.axis = axis
        self.sign = -1 if reverse else 1
        self.state, self.logs = state, logs
        self.odd = lax.axis_index(axis) % 2
        self.late = self.odd == (0 if reverse else 1)
        self.partner = flip(state, axis, 1)
        self.partner_logs = flip(logs, axis, 1)
        self.chips = lax.axis_size(axis) // 2

    def half(self, value):
        return lax.dynamic_slice_in_dim(value, self.odd * (DI // 2), DI // 2, 2)

    def chip_total(self, *beside):
        self.partner, *beside = lax.optimization_barrier((self.partner,) + beside)
        here, there = self.half(self.state), self.half(self.partner)
        decay_here = self.half(lanes_of(self.logs))
        decay_there = self.half(lanes_of(self.partner_logs))
        total = jnp.where(self.late, decay_here * there + here, decay_there * here + there)
        self.total, self.decay = total, decay_here * decay_there
        self.got = shifted(total, self.axis, 2 * self.sign)
        return beside

    def first_hop(self, *beside):
        self.window, *beside = lax.optimization_barrier((self.got,) + beside)
        self.window_decay = shifted(self.decay, self.axis, 2 * self.sign)
        self.tail = self.decay * self.window + self.total
        self.tail_decay = self.decay * self.window_decay
        return beside

    def last_hops(self, *beside):
        hop = 2
        while hop < self.chips:
            got = shifted(self.tail, self.axis, 2 * self.sign * hop)
            if hop == 2:
                got, *beside = lax.optimization_barrier((got,) + beside)
            got_decay = shifted(self.tail_decay, self.axis, 2 * self.sign * hop)
            self.window = self.window_decay * got + self.window
            self.window_decay = self.window_decay * got_decay
            hop *= 2
            if hop < self.chips:
                self.tail = self.tail_decay * got + self.tail
                self.tail_decay = self.tail_decay * got_decay
        self.whole = flip(self.window, self.axis, 1)
        return beside

    def result(self, *beside):
        self.whole, *beside = lax.optimization_barrier((self.whole,) + beside)
        both = jnp.where(
            self.odd == 0,
            jnp.concatenate([self.window, self.whole], axis=2),
            jnp.concatenate([self.whole, self.window], axis=2),
        )
        state = jnp.where(self.late, lanes_of(self.partner_logs) * both + self.partner, both)
        return [state] + beside


def on_device(
    hidden_in,
    lengths,
    w_in,
    conv_w,
    conv_b,
    g_norm,
    g_gate,
    w_out,
    a_log,
    dt_bias,
    d_skip,
    out_cotangent,
):
    axes = ("dp", "seq")
    devices = lax.axis_size("dp") * lax.axis_size("seq")
    slots, tokens, _ = hidden_in.shape
    blocks = tokens // T
    rows = slots * tokens
    grid = (slots, blocks)
    share = D // devices

    small = jnp.concatenate(
        [conv_w.reshape(-1), conv_b, g_norm, g_gate], axis=0
    )
    per_row = -(-small.shape[0] // share)
    small = jnp.pad(small, (0, per_row * share - small.shape[0])).reshape(share, per_row)
    wide = CONV_CH + LANES
    front = jnp.pad(w_in[:, DI:], ((0, 0), (0, LANES - HEADS)))
    earlier = shifted(hidden_in[:, tokens - 8 :, :], "seq", 1)
    front_full = gather(jnp.concatenate([front, small], axis=1))
    extra = front_full[:, wide:].reshape(devices, -1)
    lane = CONV_CH // devices
    taps_full = jnp.moveaxis(extra[:, : CONV * lane].reshape(devices, CONV, lane), 0, 1)
    taps_full = taps_full.reshape(CONV, CONV_CH).astype(F32)
    at = CONV * lane
    bias_full = extra[:, at : at + lane].reshape(1, CONV_CH).astype(F32)
    at += lane
    norm_gain = extra[:, at : at + share].reshape(D).astype(F32)
    at += share
    gate_gain = extra[:, at : at + DI // devices].reshape(1, DI).astype(F32)
    back = jnp.concatenate([w_in[:, :DI], w_out.T], axis=1)
    back = lax.all_gather(back, axes, axis=0, tiled=True)

    taps_rows = jnp.concatenate([taps_full, bias_full, jnp.zeros((3, CONV_CH), F32)], axis=0)
    rate = -jnp.exp(a_log)
    heads_rows = jnp.pad(jnp.stack([dt_bias, rate, d_skip]), ((0, 5), (0, LANES - HEADS)))
    skip_row = jnp.repeat(d_skip, HEADDIM)[None]
    gain_rows = jnp.concatenate([gate_gain, skip_row, jnp.zeros((6, DI), F32)], axis=0)
    select = (
        jnp.arange(DI, dtype=jnp.int32)[:, None] // HEADDIM
        == jnp.arange(LANES, dtype=jnp.int32)[None]
    ).astype(BF16)

    place = lax.axis_index("seq") * tokens + jnp.arange(tokens, dtype=jnp.int32)
    keep = (place[None, :] < lengths[:, None]).astype(F32)
    residual = hidden_in.astype(F32)

    def tile(width, dtype=F32, flip_order=False, height=T):
        if flip_order:
            spec = pl.BlockSpec((1, height, width), lambda s, c: (s, blocks - 1 - c, 0))
        else:
            spec = pl.BlockSpec((1, height, width), lambda s, c: (s, c, 0))
        return spec, jax.ShapeDtypeStruct((slots, tokens, width), dtype)

    def per_block(height, width, flip_order=False):
        if flip_order:
            spec = pl.BlockSpec((1, 1, height, width), lambda s, c: (s, blocks - 1 - c, 0, 0))
        else:
            spec = pl.BlockSpec((1, 1, height, width), lambda s, c: (s, c, 0, 0))
        return spec, jax.ShapeDtypeStruct((slots, blocks, height, width), F32)

    def columns(width, whole, index):
        spec = pl.BlockSpec((1, T, width), lambda s, c: (s, blocks - 1 - c, index))
        return spec, jax.ShapeDtypeStruct((slots, tokens, whole), F32)

    def per_slot(height, width, dtype=F32):
        spec = pl.BlockSpec((1, height, width), lambda s, c: (s, 0, 0))
        return spec, jax.ShapeDtypeStruct((slots, height, width), dtype)

    def fixed(height, width):
        spec = pl.BlockSpec((height, width), lambda s, c: (0, 0))
        return spec, jax.ShapeDtypeStruct((height, width), F32)

    def specs(*pairs):
        return [spec for spec, _ in pairs]

    normed, conv_in, halo, step_raw, x, bc, log, step, aux, enter, final, total = call(
        states_kernel,
        grid,
        specs(
            tile(D), per_slot(8, D), fixed(D, wide), fixed(1, D), fixed(8, CONV_CH), fixed(8, LANES)
        ),
        [
            tile(D, BF16), tile(CONV_CH, BF16), per_slot(8, CONV_CH, BF16), tile(LANES), tile(DI),
            tile(2 * STATE), tile(LANES), tile(LANES), per_block(8, LANES), per_block(STATE, DI),
            per_slot(STATE, DI), per_slot(8, LANES),
        ],
        [
            pltpu.VMEM((CONV_CH // LANES, T + 8, LANES), F32), pltpu.VMEM((STATE, DI), F32),
            pltpu.VMEM((8, LANES), F32),
        ],
        6 * rows * STATE * DI + 2 * rows * D * wide,
        rows * (CONV_CH * 6 + DI * 4),
    )(hidden_in, earlier, front_full, norm_gain[None], taps_rows, heads_rows)
    normed = normed.reshape(rows, D)
    logs = total[:, 0, :]
    forward = Entering(final, logs, "seq", False)
    forward.chip_total()
    back = after(back, forward.total)
    w_gate, w_out_turned = lax.optimization_barrier((back[:, :DI], back[:, DI:]))
    gate_pre = jnp.dot(normed, w_gate, preferred_element_type=F32).reshape(slots, tokens, DI)
    cotangent = out_cotangent.astype(F32)
    branch_grad = (cotangent * keep[..., None]).astype(BF16).reshape(rows, D)
    norm_grad = jnp.dot(
        after(branch_grad, forward.total), w_out_turned, preferred_element_type=F32
    )
    normed_turned = after(normed, forward.total).T
    norm_grad, gate_pre, normed_turned = forward.first_hop(
        norm_grad.reshape(slots, tokens, DI), gate_pre, normed_turned
    )
    (local,) = call(
        local_kernel,
        grid,
        specs(
            tile(DI), tile(2 * STATE), tile(LANES), tile(LANES), per_block(STATE, DI), fixed(8, DI)
        ),
        [tile(DI)],
        [],
        12 * rows * T * DI,
        rows * (CONV_CH + 2 * DI) * 4,
    )(after(x, forward.tail), bc, log, step, enter, gain_rows)
    (local,) = forward.last_hops(local)
    (start,) = forward.result()

    gated_norm, mixed_grad, gate_grad, lg, adj_enter, adj_final, gate_sums = call(
        gate_kernel,
        grid,
        specs(
            columns(STATE, 2 * STATE, 1), tile(LANES, flip_order=True),
            per_block(8, LANES, True), tile(DI, flip_order=True), tile(DI, flip_order=True),
            tile(DI, flip_order=True), per_slot(STATE, DI), fixed(8, DI), fixed(DI, LANES),
        ),
        [
            tile(DI, BF16, True), tile(DI, F32, True), tile(DI, BF16, True),
            tile(LANES, F32, True), per_block(STATE, DI, True), per_slot(STATE, DI), fixed(8, DI),
        ],
        [
            pltpu.VMEM((T, DI), F32), pltpu.VMEM((T, DI), F32), pltpu.VMEM((STATE, DI), F32),
            pltpu.VMEM((T, DI), BF16), pltpu.VMEM((T, DI), BF16),
        ],
        12 * rows * STATE * DI,
        rows * (CONV_CH * 4 + DI * 24),
    )(bc, log, aux, local, gate_pre, norm_grad, start, gain_rows, select)
    gated_norm = gated_norm.reshape(rows, DI)
    gate_grad = gate_grad.reshape(rows, DI)
    backward = Entering(adj_final, logs, "seq", True)

    w_out_grad = lax.dot_general(
        branch_grad, gated_norm, (((0,), (0,)), ((), ())), preferred_element_type=F32
    )
    (w_out_grad,) = backward.chip_total(w_out_grad)
    w_gate_grad = lax.dot_general(
        normed_turned, after(gate_grad, backward.total), NN, preferred_element_type=F32
    )
    branch = lax.dot_general(
        after(gated_norm, backward.total), w_out_turned, NT, preferred_element_type=F32
    )
    block_out = (residual + keep[..., None] * branch.reshape(slots, tokens, D)).astype(BF16)
    early = jnp.concatenate([w_gate_grad, w_out_grad], axis=1)
    early, block_out = backward.first_hop(early, block_out)
    early = lax.psum_scatter(early, axes, scatter_dimension=0, tiled=True)

    xadj, bc_grad, skipped = call(
        adjoint_kernel,
        grid,
        specs(
            tile(DI), tile(2 * STATE), tile(LANES), tile(LANES), per_block(8, LANES), tile(DI),
            per_block(STATE, DI), per_slot(STATE, DI), per_block(STATE, DI), fixed(DI, LANES),
        ),
        [tile(DI), tile(2 * STATE), tile(LANES)],
        [pltpu.VMEM((height, DI), BF16) for height in (T, T, T, STATE, 2 * T, 2 * STATE)],
        30 * rows * T * DI,
        rows * (CONV_CH + 4 * DI) * 4,
    )(
        x, bc, log, step, aux, after(mixed_grad, backward.tail), enter, start, adj_enter, select
    )
    (xadj,) = backward.last_hops(xadj)
    (end_adj,) = backward.result()

    prev = pl.BlockSpec(
        (1, 16, CONV_CH), lambda s, c: (s, jnp.maximum((blocks - 1 - c) * (T // 16) - 1, 0), 0)
    )
    def flipped(width, dtype=F32):
        return tile(width, dtype, True)

    slices = CONV_CH // LANES
    proj_grad, head_rows, last_rows, conv_sums, head_sums = call(
        finish_kernel,
        grid,
        specs(
            flipped(DI), flipped(2 * STATE), flipped(LANES), flipped(LANES),
            per_block(8, LANES, True), per_slot(8, LANES), flipped(DI), flipped(DI),
            flipped(2 * STATE), flipped(LANES), flipped(LANES), per_slot(STATE, DI),
            per_slot(STATE, DI), per_slot(STATE, DI), flipped(CONV_CH), (prev, None),
            per_slot(8, CONV_CH), flipped(LANES), fixed(8, CONV_CH), fixed(8, LANES), fixed(8, DI),
            fixed(DI, LANES),
        ),
        [
            flipped(wide, BF16), per_slot(8, CONV_CH), per_slot(8, CONV_CH), fixed(40, CONV_CH),
            fixed(24, LANES),
        ],
        [
            pltpu.VMEM((slices, T + 16, LANES), F32), pltpu.VMEM((slices, T + 8, LANES), F32),
            pltpu.VMEM((8, CONV_CH), F32), pltpu.VMEM((T, DI), BF16), pltpu.VMEM((T, DI), BF16),
            pltpu.VMEM((8, LANES), F32),
        ],
        12 * rows * STATE * DI,
        rows * (CONV_CH * 8 + DI * 8),
    )(
        x, bc, log, step, aux, total, mixed_grad, xadj, bc_grad, lg, skipped, end_adj, start,
        final, conv_in, conv_in, halo, step_raw, taps_rows, heads_rows, gain_rows, select,
    )

    ahead = shifted(head_rows, "seq", -1)
    ahead = jnp.concatenate([jnp.zeros((slots, 8, CONV_CH), F32), ahead], axis=1)
    for tap in range(CONV):
        begin = CONV - 1 - tap
        last_rows = last_rows + ahead[:, begin : begin + 8] * taps_full[tap]
    proj_grad = lax.dynamic_update_slice(
        proj_grad, last_rows.astype(BF16), (0, tokens - 8, 0)
    ).reshape(rows, wide)

    w_front_grad = jnp.dot(normed_turned, proj_grad, preferred_element_type=F32)
    scatter = ScatterSum(w_front_grad, axes)
    tall = min(2 * T, rows // 2)

    strips = rows // tall // 2

    def input_half(half, sent, *done):
        def strip(width, dtype=BF16):
            spec = pl.BlockSpec((tall, width), lambda r: (r + half * strips, 0))
            return spec, jax.ShapeDtypeStruct((rows, width), dtype)

        def whole(height, width):
            spec = pl.BlockSpec((height, width), lambda r: (0, 0))
            return spec, jax.ShapeDtypeStruct((height, width), F32)

        ins = [
            strip(wide), strip(DI), whole(D, wide), whole(D, DI), strip(D), strip(D), whole(1, D)
        ]
        return call(
            input_kernel,
            (strips,),
            specs(*ins) + [pl.BlockSpec(memory_space=pl.ANY)] * len(done),
            [strip(D, F32), whole(8, D)],
            [],
            rows * D * (wide + DI),
            (rows * (wide + DI) * 2 + rows * D * 8) // 2,
            {len(ins): 0} if done else None,
        )(
            after(proj_grad, *sent), gate_grad, front_full, w_gate, hidden_in.reshape(rows, D),
            out_cotangent.reshape(rows, D), norm_gain[None], *done,
        )

    input_grad, norm_sums = input_half(0, scatter.begin())
    sent, (input_grad, norm_sums, early) = scatter.second(input_grad, norm_sums, early)
    w_gate_owned, w_out_owned = early[:, :DI], early[:, DI:]
    input_grad, more_sums = input_half(1, sent, input_grad)
    front_owned, sent, (input_grad, norm_sums) = scatter.finish(input_grad, norm_sums + more_sums)
    input_grad = input_grad.reshape(slots, tokens, D)

    vectors = jnp.concatenate(
        [
            conv_sums.reshape(CONV + 1, 8, CONV_CH).sum(1).reshape(-1), norm_sums.sum(0),
            gate_sums.sum(0), head_sums.reshape(3, 8, LANES).sum(1).reshape(-1),
        ]
    )
    vectors = total_sum(vectors.reshape(-1, LANES), sent).reshape(-1)
    me = lax.axis_index("dp") * lax.axis_size("seq") + lax.axis_index("seq")

    def owned(begin, length):
        per = length // devices
        return lax.dynamic_slice_in_dim(vectors, begin + me * per, per)

    norm_at = (CONV + 1) * CONV_CH
    gate_at = norm_at + D
    heads_at = gate_at + DI
    return (
        block_out,
        input_grad,
        jnp.concatenate([w_gate_owned, front_owned[:, : CONV_CH + HEADS]], axis=1),
        jnp.stack([owned(k * CONV_CH, CONV_CH) for k in range(CONV)]),
        owned(CONV * CONV_CH, CONV_CH),
        owned(norm_at, D),
        owned(gate_at, DI),
        w_out_owned.T,
        vectors[heads_at : heads_at + HEADS],
        vectors[heads_at + LANES : heads_at + LANES + HEADS],
        vectors[heads_at + 2 * LANES : heads_at + 2 * LANES + HEADS],
    )


def solution(mesh):
    placed = (
        P("dp", "seq", None),
        P("dp"),
        P(("dp", "seq"), None),
        P(None, ("dp", "seq")),
        P(("dp", "seq")),
        P(("dp", "seq")),
        P(("dp", "seq")),
        P(None, ("dp", "seq")),
        P(),
        P(),
        P(),
        P("dp", "seq", None),
    )
    return jax.shard_map(
        on_device,
        mesh=mesh,
        in_specs=placed,
        out_specs=(
            P("dp", "seq", None),
            P("dp", "seq", None),
            P(("dp", "seq"), None),
            P(None, ("dp", "seq")),
            P(("dp", "seq")),
            P(("dp", "seq")),
            P(("dp", "seq")),
            P(None, ("dp", "seq")),
            P(),
            P(),
            P(),
        ),
        check_vma=False,
    )
```

```python
import functools

import jax
import jax.numpy as jnp
from jax import lax
from jax.experimental import pallas as pl
from jax.experimental.pallas import tpu as pltpu
from jax.sharding import PartitionSpec as P

D = 768
HEADS = 24
HEADDIM = 64
STATE = 128
CONV = 4
DI = 1536
CONV_CH = 1792
PROJ = 3352
T = 128
PAIRS = HEADS // 2
LANES = 128
EPSILON = 1e-05
MASKED = -1e30
F32 = jnp.float32
BF16 = jnp.bfloat16
NN = (((1,), (0,)), ((), ()))
NT = (((1,), (1,)), ((), ()))


def mm(a, b, dims=NN):
    return lax.dot_general(a, b, dims, preferred_element_type=F32)


def split(v):
    high = v.astype(BF16)
    return high, (v - high.astype(F32)).astype(BF16)


def mm3(a, b, dims=NN):
    return mm(a[0], b[0], dims) + (mm(a[0], b[1], dims) + mm(a[1], b[0], dims))


def left_half(rows):
    return lax.broadcasted_iota(jnp.int32, (rows, LANES), 1) < HEADDIM


def spread(values, pair, left):
    return jnp.where(
        left, values[:, 2 * pair : 2 * pair + 1], values[:, 2 * pair + 1 : 2 * pair + 2]
    )


def pick(values, pair, left):
    index = jnp.where(left, 2 * pair, 2 * pair + 1)
    return jnp.take_along_axis(values, index, axis=1, mode="promise_in_bounds")


def two_columns(values, pair):
    return [
        jnp.broadcast_to(values[:, head : head + 1], (values.shape[0], LANES))
        for head in (2 * pair, 2 * pair + 1)
    ]


def cols(j):
    return slice(j * LANES, (j + 1) * LANES)


def running(v, reverse):
    row = lax.broadcasted_iota(jnp.int32, v.shape, 0)
    hop = 1
    while hop < T:
        moved = pltpu.roll(v, T - hop if reverse else hop, 0)
        inside = row < T - hop if reverse else row >= hop
        v = v + jnp.where(inside, moved, 0.0)
        hop *= 2
    return v


def fold(v):
    return jnp.sum(v.reshape(v.shape[0] // 8, 8, v.shape[-1]), axis=0)


def two_heads(high, low, left):
    zero = jnp.zeros_like(high)
    top = jnp.concatenate([jnp.where(left, high, zero), jnp.where(left, low, zero)], axis=1)
    bottom = jnp.concatenate([jnp.where(left, zero, high), jnp.where(left, zero, low)], axis=1)
    return jnp.concatenate([top, bottom], axis=0)


def sigmoid(v):
    return 0.5 * jnp.tanh(0.5 * v) + 0.5


def convolve(window, taps_ref, j, first):
    at = cols(j)
    total = taps_ref[CONV : CONV + 1, at]
    rows = [window[j, first + tap : first + tap + T, :] for tap in range(CONV)]
    for tap in range(CONV):
        total = total + rows[tap] * taps_ref[tap : tap + 1, at]
    return total, rows


def states_kernel(
    hidden_ref, before_ref, front_ref, gain_ref, taps_ref, heads_ref,
    normed_ref, conv_ref, halo_ref, dt_ref, x_ref, bc_ref, log_ref, step_ref, aux_ref, enter_ref,
    final_ref, total_ref,
    window, state, before,
):
    c = pl.program_id(1)

    def norm(rows):
        rows = rows.astype(F32)
        inv = lax.rsqrt(jnp.mean(rows * rows, axis=-1, keepdims=True) + EPSILON)
        return (rows * inv * gain_ref[0:1, :]).astype(BF16)

    @pl.when(c == 0)
    def _():
        earlier = norm(before_ref[0])
        for j in range(CONV_CH // LANES):
            rows = mm(earlier, front_ref[:, cols(j)]).astype(BF16)
            halo_ref[0, :, cols(j)] = rows
            window[j, 0:8, :] = rows.astype(F32)
        state[...] = jnp.zeros_like(state)
        before[...] = jnp.zeros_like(before)

    normed = norm(hidden_ref[0])
    normed_ref[0] = normed
    for k in range(CONV_CH // LANES // 2):
        two = slice(2 * k * LANES, 2 * (k + 1) * LANES)
        rows = mm(normed, front_ref[:, two]).astype(BF16)
        conv_ref[0, :, two] = rows
        for j in (2 * k, 2 * k + 1):
            window[j, 8 : 8 + T, :] = rows[:, cols(j - 2 * k)].astype(F32)
            pre, _ = convolve(window, taps_ref, j, 8 - (CONV - 1))
            if j < PAIRS:
                x_ref[0, :, cols(j)] = pre * sigmoid(pre)
            else:
                bc_ref[0, :, cols(j - PAIRS)] = pre * sigmoid(pre)
            window[j, 0:8, :] = window[j, T : T + 8, :]

    dt = mm(normed, front_ref[:, CONV_CH : CONV_CH + LANES])
    dt_ref[0] = dt
    step = jax.nn.softplus(dt + heads_ref[0:1, :])
    log = running(step * heads_ref[1:2, :], False)
    end = log[T - 1 : T, :]
    step_ref[0] = step
    log_ref[0] = log
    weight = jnp.exp(end - log) * step
    decay = jnp.exp(end)
    left = left_half(T)
    aux_ref[0, 0] = jnp.concatenate([before[0:1, :], end, jnp.zeros((6, LANES), F32)], axis=0)
    before[0:1, :] = before[0:1, :] + end
    b_turned = split(bc_ref[0, :, 0:STATE].T)
    for j in range(PAIRS):
        prior = state[:, cols(j)]
        enter_ref[0, 0, :, cols(j)] = prior
        fed = split(x_ref[0, :, cols(j)] * spread(weight, j, left))
        state[:, cols(j)] = prior * spread(decay, j, left[0:1]) + mm3(b_turned, fed)

    @pl.when(c == pl.num_programs(1) - 1)
    def _():
        final_ref[0] = state[...]
        total_ref[0] = before[...]


def local_kernel(x_ref, bc_ref, log_ref, step_ref, enter_ref, rows_ref, out_ref):
    log = log_ref[0]
    log_turned = log.T
    step = step_ref[0]
    left = left_half(T)
    row = lax.broadcasted_iota(jnp.int32, (T, T), 0)
    col = lax.broadcasted_iota(jnp.int32, (T, T), 1)
    causal = row >= col
    b_pair = split(bc_ref[0, :, 0:STATE])
    c_pair = split(bc_ref[0, :, STATE:])
    inner = mm3(c_pair, b_pair, NT)
    for j in range(PAIRS):
        x = x_ref[0, :, cols(j)]
        fed = split(x * spread(step, j, left))
        rhs = two_heads(fed[0], fed[1], left)
        mats = []
        logs = two_columns(log, j)
        for k in range(2):
            gap = logs[k] - log_turned[2 * j + k : 2 * j + k + 1, :]
            mats.append(inner * jnp.exp(jnp.where(causal, gap, MASKED)))
        mixing = split(jnp.concatenate(mats, axis=1))
        wide = mm(mixing[0], rhs)
        out = wide[:, :LANES] + (wide[:, LANES:] + mm(mixing[1], rhs[:, :LANES]))
        crossed = mm3(c_pair, split(enter_ref[0, 0, :, cols(j)]))
        skipped = rows_ref[1:2, cols(j)] * x
        out_ref[0, :, cols(j)] = (out + skipped) + jnp.exp(jnp.where(left, *logs)) * crossed


def gate_kernel(
    c_ref, log_ref, aux_ref, local_ref, gate_ref, ng_ref, start_ref, rows_ref, sel_ref,
    normed_ref, mixed_grad_ref, gate_grad_ref, lg_ref, enter_ref, final_ref, sums_ref,
    mixed_s, gated_s, adj, q_high, q_low,
):
    s, c = pl.program_id(0), pl.program_id(1)

    @pl.when(c == 0)
    def _():
        adj[...] = jnp.zeros_like(adj)

    @pl.when((s == 0) & (c == 0))
    def _():
        sums_ref[...] = jnp.zeros_like(sums_ref)

    log = log_ref[0]
    before = aux_ref[0, 0, 0:1, :]
    end = aux_ref[0, 0, 1:2, :]
    left = left_half(T)
    since = jnp.exp(before + log)
    grown = jnp.exp(log)
    decay = jnp.exp(end)
    c_rows = c_ref[0]
    c_pair = split(c_rows)
    c_turned = split(c_rows.T)
    squares = jnp.zeros((T, LANES), F32)
    products = jnp.zeros((T, LANES), F32)
    for j in range(PAIRS):
        at = cols(j)
        crossed = mm3(c_pair, split(start_ref[0, :, at]))
        mixed = local_ref[0, :, at] + spread(since, j, left) * crossed
        gate = gate_ref[0, :, at]
        gated = mixed * (gate * sigmoid(gate))
        mixed_s[:, at] = mixed
        gated_s[:, at] = gated
        squares = squares + gated * gated
        products = products + ng_ref[0, :, at] * rows_ref[0:1, at] * gated
    inv = lax.rsqrt(jnp.sum(squares, axis=-1, keepdims=True) / DI + EPSILON)
    mean = jnp.sum(products, axis=-1, keepdims=True) / DI
    pull = inv * inv * mean
    for j in range(PAIRS):
        at = cols(j)
        mixed = mixed_s[:, at]
        gated = gated_s[:, at]
        gate = gate_ref[0, :, at]
        gain = rows_ref[0:1, at]
        ng = ng_ref[0, :, at]
        sig = sigmoid(gate)
        unit = gated * inv
        normed_ref[0, :, at] = (unit * gain).astype(BF16)
        sums_ref[:, at] = sums_ref[:, at] + fold(ng * unit)
        gated_grad = inv * (ng * gain - gated * pull)
        mixed_grad = gated_grad * (gate * sig)
        mixed_grad_ref[0, :, at] = mixed_grad
        gate_grad_ref[0, :, at] = (
            gated_grad * mixed * sig * (1.0 + gate * (1.0 - sig))
        ).astype(BF16)
        q = split(mixed_grad * mixed)
        q_high[:, at] = q[0]
        q_low[:, at] = q[1]
        prior = adj[:, at]
        enter_ref[0, 0, :, at] = prior
        fed = split(mixed_grad * spread(grown, j, left))
        adj[:, at] = prior * spread(decay, j, left[0:1]) + mm3(c_turned, fed)
    lg_ref[0] = mm(q_high[...], sel_ref[...]) + mm(q_low[...], sel_ref[...])

    @pl.when(c == pl.num_programs(1) - 1)
    def _():
        final_ref[0] = adj[...]


def adjoint_kernel(
    x_ref, bc_ref, log_ref, step_ref, aux_ref, grad_ref, enter_ref, start_ref, adj_ref, sel_ref,
    xadj_ref, bc_grad_ref, skip_ref,
    q_high, q_low, fed_s, adj_s, grads_s, states_s,
):
    log = log_ref[0]
    log_turned = log.T
    step = step_ref[0]
    before = aux_ref[0, 0, 0:1, :]
    end = aux_ref[0, 0, 1:2, :]
    left = left_half(T)
    row = lax.broadcasted_iota(jnp.int32, (T, T), 0)
    col = lax.broadcasted_iota(jnp.int32, (T, T), 1)
    later = col >= row
    b_pair = split(bc_ref[0, :, 0:STATE])
    c_pair = split(bc_ref[0, :, STATE:])
    inner = mm3(b_pair, c_pair, NT)
    reach = jnp.exp(before)
    weighted = jnp.zeros((T, T), F32)
    for j in range(PAIRS):
        at = cols(j)
        grad = grad_ref[0, :, at]
        x = x_ref[0, :, at]
        q = split(x * grad)
        q_high[:, at] = q[0]
        q_low[:, at] = q[1]
        fed = x * spread(step, j, left)
        high, low = split(grad)
        rhs = two_heads(high, low, left)
        decays = []
        logs = two_columns(log, j)
        for k in range(2):
            gap = log_turned[2 * j + k : 2 * j + k + 1, :] - logs[k]
            decays.append(jnp.exp(jnp.where(later, gap, MASKED)))
        both = jnp.where(left, *logs)
        mixing = split(jnp.concatenate([inner * decays[0], inner * decays[1]], axis=1))
        wide = mm(mixing[0], rhs)
        out = wide[:, :LANES] + (wide[:, LANES:] + mm(mixing[1], rhs[:, :LANES]))
        short = fed.astype(BF16)
        zero = jnp.zeros_like(short)
        stacked = jnp.concatenate(
            [jnp.where(left, short, zero), jnp.where(left, zero, short)], axis=0
        )
        dots = mm(stacked, high, NT)
        weighted = weighted + (decays[0] * dots[:T] + decays[1] * dots[T:])
        adj = split(adj_ref[0, 0, :, at])
        reached = jnp.exp(spread(end, j, left[0:1]) - both)
        xadj_ref[0, :, at] = out + reached * mm3(b_pair, adj)
        fed_s[:, at] = (fed * reached).astype(BF16)
        adj_s[:, at] = adj[0]
        entering = enter_ref[0, 0, :, at] + spread(reach, j, left[0:1]) * start_ref[0, :, at]
        states_s[0:STATE, at], states_s[STATE:, at] = split(entering)
        grads_s[0:T, at], grads_s[T:, at] = split(grad * jnp.exp(both))
    b_total = mm(fed_s[...], adj_s[...], NT)
    c_parts = mm(grads_s[...], states_s[...], NT)
    c_total = c_parts[:T, :STATE] + (c_parts[:T, STATE:] + c_parts[T:, :STATE])
    skip_ref[0] = mm(q_high[...], sel_ref[...]) + mm(q_low[...], sel_ref[...])
    bc_grad_ref[0, :, 0:STATE] = b_total + mm(weighted.astype(BF16), c_pair[0])
    bc_grad_ref[0, :, STATE:] = c_total + mm(weighted.T.astype(BF16), b_pair[0])


def finish_kernel(
    x_ref, bc_ref, log_ref, step_ref, aux_ref, total_ref, grad_ref, xadj_ref, bc_grad_ref, lg_ref,
    skip_ref, end_ref, start_ref, final_ref, conv_ref, prev_ref, halo_ref, dt_ref, taps_ref, heads_ref,
    rows_ref, sel_ref,
    out_ref, head_ref, last_ref, sums_ref, head_sums_ref,
    window, pre_s, last_s, q_high, q_low, carry,
):
    slices = CONV_CH // LANES
    s, c = pl.program_id(0), pl.program_id(1)
    first = c == pl.num_programs(1) - 1

    @pl.when(c == 0)
    def _():
        pre_s[:, T : T + 8, :] = jnp.zeros((slices, 8, LANES), F32)
        passed = jnp.exp(total_ref[0])
        tail = jnp.zeros((8, LANES), F32)
        for j in range(PAIRS):
            at = cols(j)
            decay = spread(passed[0:1, :], j, left_half(1))
            leaving = decay * start_ref[0, :, at] + final_ref[0, :, at]
            high, low = split(fold(end_ref[0, :, at] * leaving))
            tail = tail + (mm(high, sel_ref[at, :]) + mm(low, sel_ref[at, :]))
        carry[...] = jnp.broadcast_to(jnp.sum(tail, axis=0, keepdims=True), (8, LANES))

    @pl.when((s == 0) & (c == 0))
    def _():
        sums_ref[...] = jnp.zeros_like(sums_ref)
        head_sums_ref[...] = jnp.zeros_like(head_sums_ref)

    @pl.when(first)
    def _():
        for j in range(slices):
            window[j, 8:16, :] = halo_ref[0, :, cols(j)].astype(F32)

    @pl.when(jnp.logical_not(first))
    def _():
        for j in range(slices):
            window[j, 8:16, :] = prev_ref[0, :, cols(j)].astype(F32)[8:16, :]

    log = log_ref[0]
    step = step_ref[0]
    before = aux_ref[0, 0, 0:1, :]
    end = aux_ref[0, 0, 1:2, :]
    left = left_half(T)
    remain = jnp.exp((total_ref[0, 0:1, :] - before - end) + (end - log))
    b_pair = split(bc_ref[0, :, 0:STATE])
    b_total = bc_grad_ref[0, :, 0:STATE]

    def through(j, act_grad):
        at = cols(j)
        window[j, 16 : 16 + T, :] = conv_ref[0, :, cols(j)].astype(F32)
        pre, before_rows = convolve(window, taps_ref, j, 16 - (CONV - 1))
        sig = sigmoid(pre)
        pre_grad = act_grad * sig * (1.0 + pre * (1.0 - sig))
        pre_s[j, 0:T, :] = pre_grad
        for tap in range(CONV):
            rows = slice(8 * tap, 8 * tap + 8)
            sums_ref[rows, at] = sums_ref[rows, at] + fold(pre_grad * before_rows[tap])
        sums_ref[32:40, at] = sums_ref[32:40, at] + fold(pre_grad)
        into = pre_grad * taps_ref[CONV - 1 : CONV, cols(j)]
        for tap in range(CONV - 1):
            ahead = CONV - 1 - tap
            into = into + pre_s[j, ahead : ahead + T, :] * taps_ref[tap : tap + 1, cols(j)]
        out_ref[0, :, at] = into.astype(BF16)
        last_s[:, at] = into[T - 8 :, :]
        pre_s[j, T : T + 8, :] = pre_grad[0:8, :]

    for j in range(PAIRS):
        at = cols(j)
        x = x_ref[0, :, at]
        stepped = pick(step, j, left)
        left_over = pick(remain, j, left)
        end_pair = split(end_ref[0, :, at])
        xadj = xadj_ref[0, :, at] + left_over * mm3(b_pair, end_pair)
        b_total = b_total + mm((x * stepped * left_over).astype(BF16), end_pair[0], NT)
        q = split(x * xadj)
        q_high[:, at] = q[0]
        q_low[:, at] = q[1]
        through(j, stepped * xadj + rows_ref[1:2, at] * grad_ref[0, :, at])
    through(PAIRS, b_total)
    through(PAIRS + 1, bc_grad_ref[0, :, STATE:])

    direct = mm(q_high[...], sel_ref[...]) + mm(q_low[...], sel_ref[...])
    skipped = skip_ref[0]
    log_grad = lg_ref[0] - heads_ref[2:3, :] * skipped - step * direct
    log_grad = running(log_grad, True) + carry[0:1, :]
    carry[0:1, :] = log_grad[0:1, :]
    rate = heads_ref[1:2, :]
    step_grad = direct + log_grad * rate
    step_pre_grad = step_grad * sigmoid(dt_ref[0] + heads_ref[0:1, :])
    out_ref[0, :, CONV_CH:] = step_pre_grad.astype(BF16)
    head_sums_ref[0:8, :] = head_sums_ref[0:8, :] + fold(log_grad * step * rate)
    head_sums_ref[8:16, :] = head_sums_ref[8:16, :] + fold(step_pre_grad)
    head_sums_ref[16:24, :] = head_sums_ref[16:24, :] + fold(skipped)

    @pl.when(c == 0)
    def _():
        last_ref[0] = last_s[...]

    @pl.when(first)
    def _():
        for j in range(slices):
            head_ref[0, :, cols(j)] = pre_s[j, 0:8, :]


def input_kernel(
    proj_ref, gate_ref, front_ref, w_gate_ref, hidden_ref, cot_ref, gain_ref, *refs
):
    out_ref, sums_ref = refs[-2:]
    @pl.when(pl.program_id(0) == 0)
    def _():
        sums_ref[...] = jnp.zeros_like(sums_ref)

    x = hidden_ref[...].astype(F32)
    inv = lax.rsqrt(jnp.mean(x * x, axis=-1, keepdims=True) + EPSILON)
    unit = x * inv
    grad = mm(proj_ref[...], front_ref[...], NT) + mm(gate_ref[...], w_gate_ref[...], NT)
    sums_ref[...] = sums_ref[...] + fold(grad * unit)
    scaled = grad * gain_ref[0:1, :]
    mean = jnp.mean(scaled * unit, axis=-1, keepdims=True)
    out_ref[...] = cot_ref[...].astype(F32) + inv * (scaled - unit * mean)


def call(kernel, grid, ins, outs, scratch, flops, moved, aliases=None):
    return pl.pallas_call(
        kernel,
        input_output_aliases=aliases or {},
        grid=grid,
        in_specs=ins,
        out_specs=[spec for spec, _ in outs],
        out_shape=[shape for _, shape in outs],
        scratch_shapes=scratch,
        compiler_params=pltpu.CompilerParams(
            dimension_semantics=("arbitrary",) * len(grid), vmem_limit_bytes=56 * 2**20
        ),
        cost_estimate=pl.CostEstimate(flops=flops, bytes_accessed=moved, transcendentals=0),
    )


def flip(value, axis, bit):
    count = lax.axis_size(axis)
    return lax.ppermute(value, axis, [(i, i ^ bit) for i in range(count)])


def shifted(value, axis, steps):
    count = lax.axis_size(axis)
    initial, last = (max(0, -steps), min(count, count - steps))
    return lax.ppermute(value, axis, [(source, source + steps) for source in range(initial, last)])


def bits_of(axes):
    names = []
    for axis in axes:
        bit = lax.axis_size(axis) // 2
        while bit:
            names.append((axis, bit))
            bit //= 2
    return names


def my_bit(name):
    return (lax.axis_index(name[0]) // name[1]) % 2


def total_sum(value, sent):
    value = after(value, *sent[:1])
    value = sum((flip(value, "dp", hop) for hop in range(1, lax.axis_size("dp"))), value)
    value = after(value, *sent[1:2])
    hops = range(1, lax.axis_size("seq") // 2)
    value = sum((flip(value, "seq", 2 * hop) for hop in hops), value)
    return value + flip(value, "seq", 1)


class ScatterSum:
    def __init__(self, value, axes):
        self.names = bits_of(axes)
        core = self.names[-1]
        width = value.shape[-1]
        a = value.reshape((2,) * len(self.names) + (-1, width))
        d = len(self.names) - 1
        sent = lax.dynamic_index_in_dim(a, 1 - my_bit(core), d, False)
        sent, a = lax.optimization_barrier((sent, a))
        self.mine = lax.dynamic_index_in_dim(a, my_bit(core), d, False)
        self.arrived = flip(sent, *core)
        cut = width // LANES // 3 * LANES
        self.parts = [(0, cut), (cut, 2 * cut), (2 * cut, width)]

    def halves(self, a, d, name):
        b = my_bit(name)
        return (
            lax.dynamic_index_in_dim(a, b, d, False),
            lax.dynamic_index_in_dim(a, 1 - b, d, False),
        )

    def begin(self):
        rest = self.names[:-1]
        dp = [n for n in rest if n[0] == self.names[0][0]]
        seq = [n for n in rest if n[0] != self.names[0][0]]
        self.orders = [dp[::-1] + seq[::-1], dp + seq[::-1], seq[::-1] + dp]
        self.kept, self.got, sent = [], [], []
        for order, (begin, stop) in zip(self.orders, self.parts):
            a = self.mine[..., begin:stop] + self.arrived[..., begin:stop]
            mine, other = self.halves(a, rest.index(order[0]), order[0])
            self.kept.append(mine)
            sent.append(other)
        sent = lax.optimization_barrier(tuple(sent))
        self.got = [flip(other, *order[0]) for other, order in zip(sent, self.orders)]
        return sent

    def second(self, *beside):
        *got, beside = lax.optimization_barrier((*self.got, beside))
        self.live = []
        sent = []
        for k, order in enumerate(self.orders):
            live = [name for name in self.names[:-1] if name != order[0]]
            a = self.kept[k] + got[k]
            if len(order) > 1:
                d = live.index(order[1])
                self.kept[k], other = self.halves(a, d, order[1])
                live.pop(d)
                sent.append(other)
            self.live.append(live)
        sent = lax.optimization_barrier(tuple(sent))
        self.got = [flip(other, *order[1]) for other, order in zip(sent, self.orders)]
        return sent, beside

    def finish(self, *beside):
        *got, beside = lax.optimization_barrier((*self.got, beside))
        groups = []
        for order, live, kept, arrived in zip(self.orders, self.live, self.kept, got):
            if groups and groups[-1][0] == order[2:]:
                groups[-1][2].append(kept + arrived)
            else:
                groups.append((order[2:], live, [kept + arrived]))
        pieces, sent = [], []
        for k, (order, live, parts) in enumerate(groups):
            a = jnp.concatenate(parts, axis=-1) if len(parts) > 1 else parts[0]
            for name in order:
                d = live.index(name)
                mine, other = self.halves(a, d, name)
                if k == 0:
                    other = lax.optimization_barrier(other)
                    sent.append(other)
                a = mine + flip(other, *name)
                live.pop(d)
            pieces.append(a)
        return jnp.concatenate(pieces, axis=-1), sent, beside


def after(value, *others):
    return lax.optimization_barrier((value,) + others)[0]


def in_order(blocks, me):
    bit = 1
    while bit < len(blocks):
        swap = (me // bit) % 2 == 1
        blocks = [jnp.where(swap, blocks[i ^ bit], block) for i, block in enumerate(blocks)]
        bit *= 2
    return jnp.stack(blocks)


def gather(value):
    seq, dp = lax.axis_size("seq"), lax.axis_size("dp")
    me = lax.axis_index("seq")
    chips = [value] + [flip(value, "seq", 2 * hop) for hop in range(1, seq // 2)]
    held = in_order(chips, me // 2)
    held = in_order(
        [held] + [flip(held, "dp", hop) for hop in range(1, dp)], lax.axis_index("dp")
    )
    other = flip(held, "seq", 1)
    even = me % 2 == 0
    both = jnp.stack([jnp.where(even, held, other), jnp.where(even, other, held)], axis=2)
    return both.reshape(-1, value.shape[1])


def lanes_of(log_decay):
    return jnp.repeat(jnp.exp(log_decay[:, :HEADS]), HEADDIM, axis=1)[:, None, :]


class Entering:
    def __init__(self, state, logs, axis, reverse):
        self.axis = axis
        self.sign = -1 if reverse else 1
        self.state, self.logs = state, logs
        self.odd = lax.axis_index(axis) % 2
        self.late = self.odd == (0 if reverse else 1)
        self.partner = flip(state, axis, 1)
        self.partner_logs = flip(logs, axis, 1)
        self.chips = lax.axis_size(axis) // 2

    def half(self, value):
        return lax.dynamic_slice_in_dim(value, self.odd * (DI // 2), DI // 2, 2)

    def chip_total(self, *beside):
        self.partner, *beside = lax.optimization_barrier((self.partner,) + beside)
        here, there = self.half(self.state), self.half(self.partner)
        decay_here = self.half(lanes_of(self.logs))
        decay_there = self.half(lanes_of(self.partner_logs))
        total = jnp.where(self.late, decay_here * there + here, decay_there * here + there)
        self.total, self.decay = total, decay_here * decay_there
        self.got = shifted(total, self.axis, 2 * self.sign)
        return beside

    def first_hop(self, *beside):
        self.window, *beside = lax.optimization_barrier((self.got,) + beside)
        self.window_decay = shifted(self.decay, self.axis, 2 * self.sign)
        self.tail = self.decay * self.window + self.total
        self.tail_decay = self.decay * self.window_decay
        return beside

    def last_hops(self, *beside):
        hop = 2
        while hop < self.chips:
            got = shifted(self.tail, self.axis, 2 * self.sign * hop)
            if hop == 2:
                got, *beside = lax.optimization_barrier((got,) + beside)
            got_decay = shifted(self.tail_decay, self.axis, 2 * self.sign * hop)
            self.window = self.window_decay * got + self.window
            self.window_decay = self.window_decay * got_decay
            hop *= 2
            if hop < self.chips:
                self.tail = self.tail_decay * got + self.tail
                self.tail_decay = self.tail_decay * got_decay
        self.whole = flip(self.window, self.axis, 1)
        return beside

    def result(self, *beside):
        self.whole, *beside = lax.optimization_barrier((self.whole,) + beside)
        both = jnp.where(
            self.odd == 0,
            jnp.concatenate([self.window, self.whole], axis=2),
            jnp.concatenate([self.whole, self.window], axis=2),
        )
        state = jnp.where(self.late, lanes_of(self.partner_logs) * both + self.partner, both)
        return [state] + beside


def on_device(
    hidden_in,
    lengths,
    w_in,
    conv_w,
    conv_b,
    g_norm,
    g_gate,
    w_out,
    a_log,
    dt_bias,
    d_skip,
    out_cotangent,
):
    axes = ("dp", "seq")
    devices = lax.axis_size("dp") * lax.axis_size("seq")
    slots, tokens, _ = hidden_in.shape
    blocks = tokens // T
    rows = slots * tokens
    grid = (slots, blocks)
    share = D // devices

    small = jnp.concatenate(
        [conv_w.reshape(-1), conv_b, g_norm, g_gate], axis=0
    )
    per_row = -(-small.shape[0] // share)
    small = jnp.pad(small, (0, per_row * share - small.shape[0])).reshape(share, per_row)
    wide = CONV_CH + LANES
    front = jnp.pad(w_in[:, DI:], ((0, 0), (0, LANES - HEADS)))
    earlier = shifted(hidden_in[:, tokens - 8 :, :], "seq", 1)
    front_full = gather(jnp.concatenate([front, small], axis=1))
    extra = front_full[:, wide:].reshape(devices, -1)
    lane = CONV_CH // devices
    taps_full = jnp.moveaxis(extra[:, : CONV * lane].reshape(devices, CONV, lane), 0, 1)
    taps_full = taps_full.reshape(CONV, CONV_CH).astype(F32)
    at = CONV * lane
    bias_full = extra[:, at : at + lane].reshape(1, CONV_CH).astype(F32)
    at += lane
    norm_gain = extra[:, at : at + share].reshape(D).astype(F32)
    at += share
    gate_gain = extra[:, at : at + DI // devices].reshape(1, DI).astype(F32)
    back = jnp.concatenate([w_in[:, :DI], w_out.T], axis=1)
    back = lax.all_gather(back, axes, axis=0, tiled=True)

    taps_rows = jnp.concatenate([taps_full, bias_full, jnp.zeros((3, CONV_CH), F32)], axis=0)
    rate = -jnp.exp(a_log)
    heads_rows = jnp.pad(jnp.stack([dt_bias, rate, d_skip]), ((0, 5), (0, LANES - HEADS)))
    skip_row = jnp.repeat(d_skip, HEADDIM)[None]
    gain_rows = jnp.concatenate([gate_gain, skip_row, jnp.zeros((6, DI), F32)], axis=0)
    select = (
        jnp.arange(DI, dtype=jnp.int32)[:, None] // HEADDIM
        == jnp.arange(LANES, dtype=jnp.int32)[None]
    ).astype(BF16)

    place = lax.axis_index("seq") * tokens + jnp.arange(tokens, dtype=jnp.int32)
    keep = (place[None, :] < lengths[:, None]).astype(F32)
    residual = hidden_in.astype(F32)

    def tile(width, dtype=F32, flip_order=False, height=T):
        if flip_order:
            spec = pl.BlockSpec((1, height, width), lambda s, c: (s, blocks - 1 - c, 0))
        else:
            spec = pl.BlockSpec((1, height, width), lambda s, c: (s, c, 0))
        return spec, jax.ShapeDtypeStruct((slots, tokens, width), dtype)

    def per_block(height, width, flip_order=False):
        if flip_order:
            spec = pl.BlockSpec((1, 1, height, width), lambda s, c: (s, blocks - 1 - c, 0, 0))
        else:
            spec = pl.BlockSpec((1, 1, height, width), lambda s, c: (s, c, 0, 0))
        return spec, jax.ShapeDtypeStruct((slots, blocks, height, width), F32)

    def columns(width, whole, index):
        spec = pl.BlockSpec((1, T, width), lambda s, c: (s, blocks - 1 - c, index))
        return spec, jax.ShapeDtypeStruct((slots, tokens, whole), F32)

    def per_slot(height, width, dtype=F32):
        spec = pl.BlockSpec((1, height, width), lambda s, c: (s, 0, 0))
        return spec, jax.ShapeDtypeStruct((slots, height, width), dtype)

    def fixed(height, width):
        spec = pl.BlockSpec((height, width), lambda s, c: (0, 0))
        return spec, jax.ShapeDtypeStruct((height, width), F32)

    def specs(*pairs):
        return [spec for spec, _ in pairs]

    normed, conv_in, halo, step_raw, x, bc, log, step, aux, enter, final, total = call(
        states_kernel,
        grid,
        specs(
            tile(D), per_slot(8, D), fixed(D, wide), fixed(1, D), fixed(8, CONV_CH), fixed(8, LANES)
        ),
        [
            tile(D, BF16), tile(CONV_CH, BF16), per_slot(8, CONV_CH, BF16), tile(LANES), tile(DI),
            tile(2 * STATE), tile(LANES), tile(LANES), per_block(8, LANES), per_block(STATE, DI),
            per_slot(STATE, DI), per_slot(8, LANES),
        ],
        [
            pltpu.VMEM((CONV_CH // LANES, T + 8, LANES), F32), pltpu.VMEM((STATE, DI), F32),
            pltpu.VMEM((8, LANES), F32),
        ],
        6 * rows * STATE * DI + 2 * rows * D * wide,
        rows * (CONV_CH * 6 + DI * 4),
    )(hidden_in, earlier, front_full, norm_gain[None], taps_rows, heads_rows)
    normed = normed.reshape(rows, D)
    logs = total[:, 0, :]
    forward = Entering(final, logs, "seq", False)
    forward.chip_total()
    back = after(back, forward.total)
    w_gate, w_out_turned = lax.optimization_barrier((back[:, :DI], back[:, DI:]))
    gate_pre = jnp.dot(normed, w_gate, preferred_element_type=F32).reshape(slots, tokens, DI)
    cotangent = out_cotangent.astype(F32)
    branch_grad = (cotangent * keep[..., None]).astype(BF16).reshape(rows, D)
    norm_grad = jnp.dot(
        after(branch_grad, forward.total), w_out_turned, preferred_element_type=F32
    )
    normed_turned = after(normed, forward.total).T
    norm_grad, gate_pre, normed_turned = forward.first_hop(
        norm_grad.reshape(slots, tokens, DI), gate_pre, normed_turned
    )
    (local,) = call(
        local_kernel,
        grid,
        specs(
            tile(DI), tile(2 * STATE), tile(LANES), tile(LANES), per_block(STATE, DI), fixed(8, DI)
        ),
        [tile(DI)],
        [],
        12 * rows * T * DI,
        rows * (CONV_CH + 2 * DI) * 4,
    )(after(x, forward.tail), bc, log, step, enter, gain_rows)
    (local,) = forward.last_hops(local)
    (start,) = forward.result()

    gated_norm, mixed_grad, gate_grad, lg, adj_enter, adj_final, gate_sums = call(
        gate_kernel,
        grid,
        specs(
            columns(STATE, 2 * STATE, 1), tile(LANES, flip_order=True),
            per_block(8, LANES, True), tile(DI, flip_order=True), tile(DI, flip_order=True),
            tile(DI, flip_order=True), per_slot(STATE, DI), fixed(8, DI), fixed(DI, LANES),
        ),
        [
            tile(DI, BF16, True), tile(DI, F32, True), tile(DI, BF16, True),
            tile(LANES, F32, True), per_block(STATE, DI, True), per_slot(STATE, DI), fixed(8, DI),
        ],
        [
            pltpu.VMEM((T, DI), F32), pltpu.VMEM((T, DI), F32), pltpu.VMEM((STATE, DI), F32),
            pltpu.VMEM((T, DI), BF16), pltpu.VMEM((T, DI), BF16),
        ],
        12 * rows * STATE * DI,
        rows * (CONV_CH * 4 + DI * 24),
    )(bc, log, aux, local, gate_pre, norm_grad, start, gain_rows, select)
    gated_norm = gated_norm.reshape(rows, DI)
    gate_grad = gate_grad.reshape(rows, DI)
    backward = Entering(adj_final, logs, "seq", True)

    backward.chip_total()
    w_out_grad = lax.dot_general(
        branch_grad,
        after(gated_norm, backward.total),
        (((0,), (0,)), ((), ())),
        preferred_element_type=F32,
    )
    w_gate_grad = lax.dot_general(
        normed_turned, after(gate_grad, backward.total), NN, preferred_element_type=F32
    )
    branch = lax.dot_general(
        after(gated_norm, backward.total), w_out_turned, NT, preferred_element_type=F32
    )
    block_out = (residual + keep[..., None] * branch.reshape(slots, tokens, D)).astype(BF16)
    early = jnp.concatenate([w_gate_grad, w_out_grad], axis=1)
    early, block_out = backward.first_hop(early, block_out)
    early = lax.psum_scatter(early, axes, scatter_dimension=0, tiled=True)

    xadj, bc_grad, skipped = call(
        adjoint_kernel,
        grid,
        specs(
            tile(DI), tile(2 * STATE), tile(LANES), tile(LANES), per_block(8, LANES), tile(DI),
            per_block(STATE, DI), per_slot(STATE, DI), per_block(STATE, DI), fixed(DI, LANES),
        ),
        [tile(DI), tile(2 * STATE), tile(LANES)],
        [pltpu.VMEM((height, DI), BF16) for height in (T, T, T, STATE, 2 * T, 2 * STATE)],
        30 * rows * T * DI,
        rows * (CONV_CH + 4 * DI) * 4,
    )(
        x, bc, log, step, aux, after(mixed_grad, backward.tail), enter, start, adj_enter, select
    )
    (xadj,) = backward.last_hops(xadj)
    (end_adj,) = backward.result()

    prev = pl.BlockSpec(
        (1, 16, CONV_CH), lambda s, c: (s, jnp.maximum((blocks - 1 - c) * (T // 16) - 1, 0), 0)
    )
    def flipped(width, dtype=F32):
        return tile(width, dtype, True)

    slices = CONV_CH // LANES
    proj_grad, head_rows, last_rows, conv_sums, head_sums = call(
        finish_kernel,
        grid,
        specs(
            flipped(DI), flipped(2 * STATE), flipped(LANES), flipped(LANES),
            per_block(8, LANES, True), per_slot(8, LANES), flipped(DI), flipped(DI),
            flipped(2 * STATE), flipped(LANES), flipped(LANES), per_slot(STATE, DI),
            per_slot(STATE, DI), per_slot(STATE, DI), flipped(CONV_CH), (prev, None),
            per_slot(8, CONV_CH), flipped(LANES), fixed(8, CONV_CH), fixed(8, LANES), fixed(8, DI),
            fixed(DI, LANES),
        ),
        [
            flipped(wide, BF16), per_slot(8, CONV_CH), per_slot(8, CONV_CH), fixed(40, CONV_CH),
            fixed(24, LANES),
        ],
        [
            pltpu.VMEM((slices, T + 16, LANES), F32), pltpu.VMEM((slices, T + 8, LANES), F32),
            pltpu.VMEM((8, CONV_CH), F32), pltpu.VMEM((T, DI), BF16), pltpu.VMEM((T, DI), BF16),
            pltpu.VMEM((8, LANES), F32),
        ],
        12 * rows * STATE * DI,
        rows * (CONV_CH * 8 + DI * 8),
    )(
        x, bc, log, step, aux, total, mixed_grad, xadj, bc_grad, lg, skipped, end_adj, start,
        final, conv_in, conv_in, halo, step_raw, taps_rows, heads_rows, gain_rows, select,
    )

    ahead = shifted(head_rows, "seq", -1)
    ahead = jnp.concatenate([jnp.zeros((slots, 8, CONV_CH), F32), ahead], axis=1)
    for tap in range(CONV):
        begin = CONV - 1 - tap
        last_rows = last_rows + ahead[:, begin : begin + 8] * taps_full[tap]
    proj_grad = lax.dynamic_update_slice(
        proj_grad, last_rows.astype(BF16), (0, tokens - 8, 0)
    ).reshape(rows, wide)

    w_front_grad = jnp.dot(normed_turned, proj_grad, preferred_element_type=F32)
    scatter = ScatterSum(w_front_grad, axes)
    tall = min(2 * T, rows // 2)

    strips = rows // tall // 2

    def input_half(half, sent, *done):
        def strip(width, dtype=BF16):
            spec = pl.BlockSpec((tall, width), lambda r: (r + half * strips, 0))
            return spec, jax.ShapeDtypeStruct((rows, width), dtype)

        def whole(height, width):
            spec = pl.BlockSpec((height, width), lambda r: (0, 0))
            return spec, jax.ShapeDtypeStruct((height, width), F32)

        ins = [
            strip(wide), strip(DI), whole(D, wide), whole(D, DI), strip(D), strip(D), whole(1, D)
        ]
        return call(
            input_kernel,
            (strips,),
            specs(*ins) + [pl.BlockSpec(memory_space=pl.ANY)] * len(done),
            [strip(D, F32), whole(8, D)],
            [],
            rows * D * (wide + DI),
            (rows * (wide + DI) * 2 + rows * D * 8) // 2,
            {len(ins): 0} if done else None,
        )(
            after(proj_grad, *sent), gate_grad, front_full, w_gate, hidden_in.reshape(rows, D),
            out_cotangent.reshape(rows, D), norm_gain[None], *done,
        )

    input_grad, norm_sums = input_half(0, scatter.begin())
    sent, (input_grad, norm_sums, early) = scatter.second(input_grad, norm_sums, early)
    w_gate_owned, w_out_owned = early[:, :DI], early[:, DI:]
    input_grad, more_sums = input_half(1, sent, input_grad)
    front_owned, sent, (input_grad, norm_sums) = scatter.finish(input_grad, norm_sums + more_sums)
    input_grad = input_grad.reshape(slots, tokens, D)

    vectors = jnp.concatenate(
        [
            conv_sums.reshape(CONV + 1, 8, CONV_CH).sum(1).reshape(-1), norm_sums.sum(0),
            gate_sums.sum(0), head_sums.reshape(3, 8, LANES).sum(1).reshape(-1),
        ]
    )
    vectors = total_sum(vectors.reshape(-1, LANES), sent).reshape(-1)
    me = lax.axis_index("dp") * lax.axis_size("seq") + lax.axis_index("seq")

    def owned(begin, length):
        per = length // devices
        return lax.dynamic_slice_in_dim(vectors, begin + me * per, per)

    norm_at = (CONV + 1) * CONV_CH
    gate_at = norm_at + D
    heads_at = gate_at + DI
    return (
        block_out,
        input_grad,
        jnp.concatenate([w_gate_owned, front_owned[:, : CONV_CH + HEADS]], axis=1),
        jnp.stack([owned(k * CONV_CH, CONV_CH) for k in range(CONV)]),
        owned(CONV * CONV_CH, CONV_CH),
        owned(norm_at, D),
        owned(gate_at, DI),
        w_out_owned.T,
        vectors[heads_at : heads_at + HEADS],
        vectors[heads_at + LANES : heads_at + LANES + HEADS],
        vectors[heads_at + 2 * LANES : heads_at + 2 * LANES + HEADS],
    )


def solution(mesh):
    placed = (
        P("dp", "seq", None),
        P("dp"),
        P(("dp", "seq"), None),
        P(None, ("dp", "seq")),
        P(("dp", "seq")),
        P(("dp", "seq")),
        P(("dp", "seq")),
        P(None, ("dp", "seq")),
        P(),
        P(),
        P(),
        P("dp", "seq", None),
    )
    return jax.shard_map(
        on_device,
        mesh=mesh,
        in_specs=placed,
        out_specs=(
            P("dp", "seq", None),
            P("dp", "seq", None),
            P(("dp", "seq"), None),
            P(None, ("dp", "seq")),
            P(("dp", "seq")),
            P(("dp", "seq")),
            P(("dp", "seq")),
            P(None, ("dp", "seq")),
            P(),
            P(),
            P(),
        ),
        check_vma=False,
    )
```

```python
import functools

import jax
import jax.numpy as jnp
from jax import lax
from jax.experimental import pallas as pl
from jax.experimental.pallas import tpu as pltpu
from jax.sharding import PartitionSpec as P

D = 768
HEADS = 24
HEADDIM = 64
STATE = 128
CONV = 4
DI = 1536
CONV_CH = 1792
PROJ = 3352
T = 128
PAIRS = HEADS // 2
LANES = 128
EPSILON = 1e-05
MASKED = -1e30
F32 = jnp.float32
BF16 = jnp.bfloat16
NN = (((1,), (0,)), ((), ()))
NT = (((1,), (1,)), ((), ()))


def mm(a, b, dims=NN):
    return lax.dot_general(a, b, dims, preferred_element_type=F32)


def split(v):
    high = v.astype(BF16)
    return high, (v - high.astype(F32)).astype(BF16)


def mm3(a, b, dims=NN):
    return mm(a[0], b[0], dims) + (mm(a[0], b[1], dims) + mm(a[1], b[0], dims))


def left_half(rows):
    return lax.broadcasted_iota(jnp.int32, (rows, LANES), 1) < HEADDIM


def spread(values, pair, left):
    return jnp.where(
        left, values[:, 2 * pair : 2 * pair + 1], values[:, 2 * pair + 1 : 2 * pair + 2]
    )


def pick(values, pair, left):
    index = jnp.where(left, 2 * pair, 2 * pair + 1)
    return jnp.take_along_axis(values, index, axis=1, mode="promise_in_bounds")


def two_columns(values, pair):
    return [
        jnp.broadcast_to(values[:, head : head + 1], (values.shape[0], LANES))
        for head in (2 * pair, 2 * pair + 1)
    ]


def cols(j):
    return slice(j * LANES, (j + 1) * LANES)


def running(v, reverse):
    row = lax.broadcasted_iota(jnp.int32, v.shape, 0)
    hop = 1
    while hop < T:
        moved = pltpu.roll(v, T - hop if reverse else hop, 0)
        inside = row < T - hop if reverse else row >= hop
        v = v + jnp.where(inside, moved, 0.0)
        hop *= 2
    return v


def fold(v):
    return jnp.sum(v.reshape(v.shape[0] // 8, 8, v.shape[-1]), axis=0)


def two_heads(high, low, left):
    zero = jnp.zeros_like(high)
    top = jnp.concatenate([jnp.where(left, high, zero), jnp.where(left, low, zero)], axis=1)
    bottom = jnp.concatenate([jnp.where(left, zero, high), jnp.where(left, zero, low)], axis=1)
    return jnp.concatenate([top, bottom], axis=0)


def sigmoid(v):
    return 0.5 * jnp.tanh(0.5 * v) + 0.5


def convolve(window, taps_ref, j, first):
    at = cols(j)
    total = taps_ref[CONV : CONV + 1, at]
    rows = [window[j, first + tap : first + tap + T, :] for tap in range(CONV)]
    for tap in range(CONV):
        total = total + rows[tap] * taps_ref[tap : tap + 1, at]
    return total, rows


def states_kernel(
    hidden_ref, before_ref, front_ref, gain_ref, taps_ref, heads_ref,
    normed_ref, conv_ref, halo_ref, dt_ref, x_ref, bc_ref, log_ref, step_ref, aux_ref, enter_ref,
    final_ref, total_ref,
    window, state, before,
):
    c = pl.program_id(1)

    def norm(rows):
        rows = rows.astype(F32)
        inv = lax.rsqrt(jnp.mean(rows * rows, axis=-1, keepdims=True) + EPSILON)
        return (rows * inv * gain_ref[0:1, :]).astype(BF16)

    @pl.when(c == 0)
    def _():
        earlier = norm(before_ref[0])
        for j in range(CONV_CH // LANES):
            rows = mm(earlier, front_ref[:, cols(j)]).astype(BF16)
            halo_ref[0, :, cols(j)] = rows
            window[j, 0:8, :] = rows.astype(F32)
        state[...] = jnp.zeros_like(state)
        before[...] = jnp.zeros_like(before)

    normed = norm(hidden_ref[0])
    normed_ref[0] = normed
    for k in range(CONV_CH // LANES // 2):
        two = slice(2 * k * LANES, 2 * (k + 1) * LANES)
        rows = mm(normed, front_ref[:, two]).astype(BF16)
        conv_ref[0, :, two] = rows
        for j in (2 * k, 2 * k + 1):
            window[j, 8 : 8 + T, :] = rows[:, cols(j - 2 * k)].astype(F32)
            pre, _ = convolve(window, taps_ref, j, 8 - (CONV - 1))
            if j < PAIRS:
                x_ref[0, :, cols(j)] = pre * sigmoid(pre)
            else:
                bc_ref[0, :, cols(j - PAIRS)] = pre * sigmoid(pre)
            window[j, 0:8, :] = window[j, T : T + 8, :]

    dt = mm(normed, front_ref[:, CONV_CH : CONV_CH + LANES])
    dt_ref[0] = dt
    step = jax.nn.softplus(dt + heads_ref[0:1, :])
    log = running(step * heads_ref[1:2, :], False)
    end = log[T - 1 : T, :]
    step_ref[0] = step
    log_ref[0] = log
    weight = jnp.exp(end - log) * step
    decay = jnp.exp(end)
    left = left_half(T)
    aux_ref[0, 0] = jnp.concatenate([before[0:1, :], end, jnp.zeros((6, LANES), F32)], axis=0)
    before[0:1, :] = before[0:1, :] + end
    b_turned = split(bc_ref[0, :, 0:STATE].T)
    for j in range(PAIRS):
        prior = state[:, cols(j)]
        enter_ref[0, 0, :, cols(j)] = prior
        fed = split(x_ref[0, :, cols(j)] * spread(weight, j, left))
        state[:, cols(j)] = prior * spread(decay, j, left[0:1]) + mm3(b_turned, fed)

    @pl.when(c == pl.num_programs(1) - 1)
    def _():
        final_ref[0] = state[...]
        total_ref[0] = before[...]


def local_kernel(x_ref, bc_ref, log_ref, step_ref, enter_ref, rows_ref, out_ref):
    log = log_ref[0]
    log_turned = log.T
    step = step_ref[0]
    left = left_half(T)
    row = lax.broadcasted_iota(jnp.int32, (T, T), 0)
    col = lax.broadcasted_iota(jnp.int32, (T, T), 1)
    causal = row >= col
    b_pair = split(bc_ref[0, :, 0:STATE])
    c_pair = split(bc_ref[0, :, STATE:])
    inner = mm3(c_pair, b_pair, NT)
    for j in range(PAIRS):
        x = x_ref[0, :, cols(j)]
        fed = split(x * spread(step, j, left))
        rhs = two_heads(fed[0], fed[1], left)
        mats = []
        logs = two_columns(log, j)
        for k in range(2):
            gap = logs[k] - log_turned[2 * j + k : 2 * j + k + 1, :]
            mats.append(inner * jnp.exp(jnp.where(causal, gap, MASKED)))
        mixing = split(jnp.concatenate(mats, axis=1))
        wide = mm(mixing[0], rhs)
        out = wide[:, :LANES] + (wide[:, LANES:] + mm(mixing[1], rhs[:, :LANES]))
        crossed = mm3(c_pair, split(enter_ref[0, 0, :, cols(j)]))
        skipped = rows_ref[1:2, cols(j)] * x
        out_ref[0, :, cols(j)] = (out + skipped) + jnp.exp(jnp.where(left, *logs)) * crossed


def gate_kernel(
    c_ref, log_ref, aux_ref, local_ref, gate_ref, ng_ref, start_ref, rows_ref, sel_ref,
    normed_ref, mixed_grad_ref, gate_grad_ref, lg_ref, enter_ref, final_ref, sums_ref,
    mixed_s, gated_s, grown_s, adj, q_high, q_low,
):
    s, c = pl.program_id(0), pl.program_id(1)

    @pl.when(c == 0)
    def _():
        adj[...] = jnp.zeros_like(adj)

    @pl.when((s == 0) & (c == 0))
    def _():
        sums_ref[...] = jnp.zeros_like(sums_ref)

    log = log_ref[0]
    before = aux_ref[0, 0, 0:1, :]
    end = aux_ref[0, 0, 1:2, :]
    left = left_half(T)
    decay = jnp.exp(end)
    c_rows = c_ref[0]
    c_pair = split(c_rows)
    c_turned = split(c_rows.T)
    squares = jnp.zeros((T, LANES), F32)
    products = jnp.zeros((T, LANES), F32)
    for j in range(PAIRS):
        at = cols(j)
        crossed = mm3(c_pair, split(start_ref[0, :, at]))
        logs = pick(log, j, left)
        grown_s[:, at] = jnp.exp(logs)
        since = jnp.exp(spread(before, j, left[0:1]) + logs)
        mixed = local_ref[0, :, at] + since * crossed
        gate = gate_ref[0, :, at]
        gated = mixed * (gate * sigmoid(gate))
        mixed_s[:, at] = mixed
        gated_s[:, at] = gated
        squares = squares + gated * gated
        products = products + ng_ref[0, :, at] * rows_ref[0:1, at] * gated
    inv = lax.rsqrt(jnp.sum(squares, axis=-1, keepdims=True) / DI + EPSILON)
    mean = jnp.sum(products, axis=-1, keepdims=True) / DI
    pull = inv * inv * mean
    for j in range(PAIRS):
        at = cols(j)
        mixed = mixed_s[:, at]
        gated = gated_s[:, at]
        gate = gate_ref[0, :, at]
        gain = rows_ref[0:1, at]
        ng = ng_ref[0, :, at]
        sig = sigmoid(gate)
        unit = gated * inv
        normed_ref[0, :, at] = (unit * gain).astype(BF16)
        sums_ref[:, at] = sums_ref[:, at] + fold(ng * unit)
        gated_grad = inv * (ng * gain - gated * pull)
        mixed_grad = gated_grad * (gate * sig)
        mixed_grad_ref[0, :, at] = mixed_grad
        gate_grad_ref[0, :, at] = (
            gated_grad * mixed * sig * (1.0 + gate * (1.0 - sig))
        ).astype(BF16)
        q = split(mixed_grad * mixed)
        q_high[:, at] = q[0]
        q_low[:, at] = q[1]
        prior = adj[:, at]
        enter_ref[0, 0, :, at] = prior
        fed = split(mixed_grad * grown_s[:, at])
        adj[:, at] = prior * spread(decay, j, left[0:1]) + mm3(c_turned, fed)
    lg_ref[0] = mm(q_high[...], sel_ref[...]) + mm(q_low[...], sel_ref[...])

    @pl.when(c == pl.num_programs(1) - 1)
    def _():
        final_ref[0] = adj[...]


def adjoint_kernel(
    x_ref, bc_ref, log_ref, step_ref, aux_ref, grad_ref, enter_ref, start_ref, adj_ref, sel_ref,
    xadj_ref, bc_grad_ref, skip_ref,
    q_high, q_low, fed_s, adj_s, grads_s, states_s,
):
    log = log_ref[0]
    log_turned = log.T
    step = step_ref[0]
    before = aux_ref[0, 0, 0:1, :]
    end = aux_ref[0, 0, 1:2, :]
    left = left_half(T)
    row = lax.broadcasted_iota(jnp.int32, (T, T), 0)
    col = lax.broadcasted_iota(jnp.int32, (T, T), 1)
    later = col >= row
    b_pair = split(bc_ref[0, :, 0:STATE])
    c_pair = split(bc_ref[0, :, STATE:])
    inner = mm3(b_pair, c_pair, NT)
    reach = jnp.exp(before)
    weighted = jnp.zeros((T, T), F32)
    for j in range(PAIRS):
        at = cols(j)
        grad = grad_ref[0, :, at]
        x = x_ref[0, :, at]
        q = split(x * grad)
        q_high[:, at] = q[0]
        q_low[:, at] = q[1]
        fed = x * spread(step, j, left)
        high, low = split(grad)
        rhs = two_heads(high, low, left)
        decays = []
        logs = two_columns(log, j)
        for k in range(2):
            gap = log_turned[2 * j + k : 2 * j + k + 1, :] - logs[k]
            decays.append(jnp.exp(jnp.where(later, gap, MASKED)))
        both = jnp.where(left, *logs)
        mixing = split(jnp.concatenate([inner * decays[0], inner * decays[1]], axis=1))
        wide = mm(mixing[0], rhs)
        out = wide[:, :LANES] + (wide[:, LANES:] + mm(mixing[1], rhs[:, :LANES]))
        short = fed.astype(BF16)
        zero = jnp.zeros_like(short)
        stacked = jnp.concatenate(
            [jnp.where(left, short, zero), jnp.where(left, zero, short)], axis=0
        )
        dots = mm(stacked, high, NT)
        weighted = weighted + (decays[0] * dots[:T] + decays[1] * dots[T:])
        adj = split(adj_ref[0, 0, :, at])
        reached = jnp.exp(spread(end, j, left[0:1]) - both)
        xadj_ref[0, :, at] = out + reached * mm3(b_pair, adj)
        fed_s[:, at] = (fed * reached).astype(BF16)
        adj_s[:, at] = adj[0]
        entering = enter_ref[0, 0, :, at] + spread(reach, j, left[0:1]) * start_ref[0, :, at]
        states_s[0:STATE, at], states_s[STATE:, at] = split(entering)
        grads_s[0:T, at], grads_s[T:, at] = split(grad * jnp.exp(both))
    b_total = mm(fed_s[...], adj_s[...], NT)
    c_parts = mm(grads_s[...], states_s[...], NT)
    c_total = c_parts[:T, :STATE] + (c_parts[:T, STATE:] + c_parts[T:, :STATE])
    skip_ref[0] = mm(q_high[...], sel_ref[...]) + mm(q_low[...], sel_ref[...])
    bc_grad_ref[0, :, 0:STATE] = b_total + mm(weighted.astype(BF16), c_pair[0])
    bc_grad_ref[0, :, STATE:] = c_total + mm(weighted.T.astype(BF16), b_pair[0])


def finish_kernel(
    x_ref, bc_ref, log_ref, step_ref, aux_ref, total_ref, grad_ref, xadj_ref, bc_grad_ref, lg_ref,
    skip_ref, end_ref, start_ref, final_ref, conv_ref, prev_ref, halo_ref, dt_ref, taps_ref, heads_ref,
    rows_ref, sel_ref,
    out_ref, head_ref, last_ref, sums_ref, head_sums_ref,
    window, pre_s, last_s, q_high, q_low, carry,
):
    slices = CONV_CH // LANES
    s, c = pl.program_id(0), pl.program_id(1)
    first = c == pl.num_programs(1) - 1

    @pl.when(c == 0)
    def _():
        pre_s[:, T : T + 8, :] = jnp.zeros((slices, 8, LANES), F32)
        passed = jnp.exp(total_ref[0])
        tail = jnp.zeros((8, LANES), F32)
        for j in range(PAIRS):
            at = cols(j)
            decay = spread(passed[0:1, :], j, left_half(1))
            leaving = decay * start_ref[0, :, at] + final_ref[0, :, at]
            high, low = split(fold(end_ref[0, :, at] * leaving))
            tail = tail + (mm(high, sel_ref[at, :]) + mm(low, sel_ref[at, :]))
        carry[...] = jnp.broadcast_to(jnp.sum(tail, axis=0, keepdims=True), (8, LANES))

    @pl.when((s == 0) & (c == 0))
    def _():
        sums_ref[...] = jnp.zeros_like(sums_ref)
        head_sums_ref[...] = jnp.zeros_like(head_sums_ref)

    @pl.when(first)
    def _():
        for j in range(slices):
            window[j, 8:16, :] = halo_ref[0, :, cols(j)].astype(F32)

    @pl.when(jnp.logical_not(first))
    def _():
        for j in range(slices):
            window[j, 8:16, :] = prev_ref[0, :, cols(j)].astype(F32)[8:16, :]

    log = log_ref[0]
    step = step_ref[0]
    before = aux_ref[0, 0, 0:1, :]
    end = aux_ref[0, 0, 1:2, :]
    left = left_half(T)
    remain = jnp.exp((total_ref[0, 0:1, :] - before - end) + (end - log))
    b_pair = split(bc_ref[0, :, 0:STATE])
    b_total = bc_grad_ref[0, :, 0:STATE]

    def through(j, act_grad):
        at = cols(j)
        window[j, 16 : 16 + T, :] = conv_ref[0, :, cols(j)].astype(F32)
        pre, before_rows = convolve(window, taps_ref, j, 16 - (CONV - 1))
        sig = sigmoid(pre)
        pre_grad = act_grad * sig * (1.0 + pre * (1.0 - sig))
        pre_s[j, 0:T, :] = pre_grad
        for tap in range(CONV):
            rows = slice(8 * tap, 8 * tap + 8)
            sums_ref[rows, at] = sums_ref[rows, at] + fold(pre_grad * before_rows[tap])
        sums_ref[32:40, at] = sums_ref[32:40, at] + fold(pre_grad)
        into = pre_grad * taps_ref[CONV - 1 : CONV, cols(j)]
        for tap in range(CONV - 1):
            ahead = CONV - 1 - tap
            into = into + pre_s[j, ahead : ahead + T, :] * taps_ref[tap : tap + 1, cols(j)]
        out_ref[0, :, at] = into.astype(BF16)
        last_s[:, at] = into[T - 8 :, :]
        pre_s[j, T : T + 8, :] = pre_grad[0:8, :]

    for j in range(PAIRS):
        at = cols(j)
        x = x_ref[0, :, at]
        stepped = pick(step, j, left)
        left_over = pick(remain, j, left)
        end_pair = split(end_ref[0, :, at])
        xadj = xadj_ref[0, :, at] + left_over * mm3(b_pair, end_pair)
        b_total = b_total + mm((x * stepped * left_over).astype(BF16), end_pair[0], NT)
        q = split(x * xadj)
        q_high[:, at] = q[0]
        q_low[:, at] = q[1]
        through(j, stepped * xadj + rows_ref[1:2, at] * grad_ref[0, :, at])
    through(PAIRS, b_total)
    through(PAIRS + 1, bc_grad_ref[0, :, STATE:])

    direct = mm(q_high[...], sel_ref[...]) + mm(q_low[...], sel_ref[...])
    skipped = skip_ref[0]
    log_grad = lg_ref[0] - heads_ref[2:3, :] * skipped - step * direct
    log_grad = running(log_grad, True) + carry[0:1, :]
    carry[0:1, :] = log_grad[0:1, :]
    rate = heads_ref[1:2, :]
    step_grad = direct + log_grad * rate
    step_pre_grad = step_grad * sigmoid(dt_ref[0] + heads_ref[0:1, :])
    out_ref[0, :, CONV_CH:] = step_pre_grad.astype(BF16)
    head_sums_ref[0:8, :] = head_sums_ref[0:8, :] + fold(log_grad * step * rate)
    head_sums_ref[8:16, :] = head_sums_ref[8:16, :] + fold(step_pre_grad)
    head_sums_ref[16:24, :] = head_sums_ref[16:24, :] + fold(skipped)

    @pl.when(c == 0)
    def _():
        last_ref[0] = last_s[...]

    @pl.when(first)
    def _():
        for j in range(slices):
            head_ref[0, :, cols(j)] = pre_s[j, 0:8, :]


def input_kernel(
    proj_ref, gate_ref, front_ref, w_gate_ref, hidden_ref, cot_ref, gain_ref, *refs
):
    out_ref, sums_ref = refs[-2:]
    @pl.when(pl.program_id(0) == 0)
    def _():
        sums_ref[...] = jnp.zeros_like(sums_ref)

    x = hidden_ref[...].astype(F32)
    inv = lax.rsqrt(jnp.mean(x * x, axis=-1, keepdims=True) + EPSILON)
    unit = x * inv
    grad = mm(proj_ref[...], front_ref[...], NT) + mm(gate_ref[...], w_gate_ref[...], NT)
    sums_ref[...] = sums_ref[...] + fold(grad * unit)
    scaled = grad * gain_ref[0:1, :]
    mean = jnp.mean(scaled * unit, axis=-1, keepdims=True)
    out_ref[...] = cot_ref[...].astype(F32) + inv * (scaled - unit * mean)


def call(kernel, grid, ins, outs, scratch, flops, moved, aliases=None):
    return pl.pallas_call(
        kernel,
        input_output_aliases=aliases or {},
        grid=grid,
        in_specs=ins,
        out_specs=[spec for spec, _ in outs],
        out_shape=[shape for _, shape in outs],
        scratch_shapes=scratch,
        compiler_params=pltpu.CompilerParams(
            dimension_semantics=("arbitrary",) * len(grid), vmem_limit_bytes=56 * 2**20
        ),
        cost_estimate=pl.CostEstimate(flops=flops, bytes_accessed=moved, transcendentals=0),
    )


def flip(value, axis, bit):
    count = lax.axis_size(axis)
    return lax.ppermute(value, axis, [(i, i ^ bit) for i in range(count)])


def shifted(value, axis, steps):
    count = lax.axis_size(axis)
    initial, last = (max(0, -steps), min(count, count - steps))
    return lax.ppermute(value, axis, [(source, source + steps) for source in range(initial, last)])


def bits_of(axes):
    names = []
    for axis in axes:
        bit = lax.axis_size(axis) // 2
        while bit:
            names.append((axis, bit))
            bit //= 2
    return names


def my_bit(name):
    return (lax.axis_index(name[0]) // name[1]) % 2


def total_sum(value, sent):
    value = after(value, *sent[:1])
    value = sum((flip(value, "dp", hop) for hop in range(1, lax.axis_size("dp"))), value)
    value = after(value, *sent[1:2])
    hops = range(1, lax.axis_size("seq") // 2)
    value = sum((flip(value, "seq", 2 * hop) for hop in hops), value)
    return value + flip(value, "seq", 1)


class ScatterSum:
    def __init__(self, value, axes):
        self.names = bits_of(axes)
        core = self.names[-1]
        width = value.shape[-1]
        a = value.reshape((2,) * len(self.names) + (-1, width))
        d = len(self.names) - 1
        sent = lax.dynamic_index_in_dim(a, 1 - my_bit(core), d, False)
        sent, a = lax.optimization_barrier((sent, a))
        self.mine = lax.dynamic_index_in_dim(a, my_bit(core), d, False)
        self.arrived = flip(sent, *core)
        cut = width // LANES // 3 * LANES
        self.parts = [(0, cut), (cut, 2 * cut), (2 * cut, width)]

    def halves(self, a, d, name):
        b = my_bit(name)
        return (
            lax.dynamic_index_in_dim(a, b, d, False),
            lax.dynamic_index_in_dim(a, 1 - b, d, False),
        )

    def begin(self):
        rest = self.names[:-1]
        dp = [n for n in rest if n[0] == self.names[0][0]]
        seq = [n for n in rest if n[0] != self.names[0][0]]
        self.orders = [dp[::-1] + seq[::-1], dp + seq[::-1], seq[::-1] + dp]
        self.kept, self.got, sent = [], [], []
        for order, (begin, stop) in zip(self.orders, self.parts):
            a = self.mine[..., begin:stop] + self.arrived[..., begin:stop]
            mine, other = self.halves(a, rest.index(order[0]), order[0])
            self.kept.append(mine)
            sent.append(other)
        sent = lax.optimization_barrier(tuple(sent))
        self.got = [flip(other, *order[0]) for other, order in zip(sent, self.orders)]
        return sent

    def second(self, *beside):
        *got, beside = lax.optimization_barrier((*self.got, beside))
        self.live = []
        sent = []
        for k, order in enumerate(self.orders):
            live = [name for name in self.names[:-1] if name != order[0]]
            a = self.kept[k] + got[k]
            if len(order) > 1:
                d = live.index(order[1])
                self.kept[k], other = self.halves(a, d, order[1])
                live.pop(d)
                sent.append(other)
            self.live.append(live)
        sent = lax.optimization_barrier(tuple(sent))
        self.got = [flip(other, *order[1]) for other, order in zip(sent, self.orders)]
        return sent, beside

    def finish(self, *beside):
        *got, beside = lax.optimization_barrier((*self.got, beside))
        groups = []
        for order, live, kept, arrived in zip(self.orders, self.live, self.kept, got):
            if groups and groups[-1][0] == order[2:]:
                groups[-1][2].append(kept + arrived)
            else:
                groups.append((order[2:], live, [kept + arrived]))
        pieces, sent = [], []
        for k, (order, live, parts) in enumerate(groups):
            a = jnp.concatenate(parts, axis=-1) if len(parts) > 1 else parts[0]
            for name in order:
                d = live.index(name)
                mine, other = self.halves(a, d, name)
                if k == 0:
                    other = lax.optimization_barrier(other)
                    sent.append(other)
                a = mine + flip(other, *name)
                live.pop(d)
            pieces.append(a)
        return jnp.concatenate(pieces, axis=-1), sent, beside


def after(value, *others):
    return lax.optimization_barrier((value,) + others)[0]


def in_order(blocks, me):
    bit = 1
    while bit < len(blocks):
        swap = (me // bit) % 2 == 1
        blocks = [jnp.where(swap, blocks[i ^ bit], block) for i, block in enumerate(blocks)]
        bit *= 2
    return jnp.stack(blocks)


def gather(value):
    seq, dp = lax.axis_size("seq"), lax.axis_size("dp")
    me = lax.axis_index("seq")
    chips = [value] + [flip(value, "seq", 2 * hop) for hop in range(1, seq // 2)]
    held = in_order(chips, me // 2)
    held = in_order(
        [held] + [flip(held, "dp", hop) for hop in range(1, dp)], lax.axis_index("dp")
    )
    other = flip(held, "seq", 1)
    even = me % 2 == 0
    both = jnp.stack([jnp.where(even, held, other), jnp.where(even, other, held)], axis=2)
    return both.reshape(-1, value.shape[1])


def lanes_of(log_decay):
    return jnp.repeat(jnp.exp(log_decay[:, :HEADS]), HEADDIM, axis=1)[:, None, :]


class Entering:
    def __init__(self, state, logs, axis, reverse):
        self.axis = axis
        self.sign = -1 if reverse else 1
        self.state, self.logs = state, logs
        self.odd = lax.axis_index(axis) % 2
        self.late = self.odd == (0 if reverse else 1)
        self.partner = flip(state, axis, 1)
        self.partner_logs = flip(logs, axis, 1)
        self.chips = lax.axis_size(axis) // 2

    def half(self, value):
        return lax.dynamic_slice_in_dim(value, self.odd * (DI // 2), DI // 2, 2)

    def chip_total(self, *beside):
        self.partner, *beside = lax.optimization_barrier((self.partner,) + beside)
        here, there = self.half(self.state), self.half(self.partner)
        decay_here = self.half(lanes_of(self.logs))
        decay_there = self.half(lanes_of(self.partner_logs))
        total = jnp.where(self.late, decay_here * there + here, decay_there * here + there)
        self.total, self.decay = total, decay_here * decay_there
        self.got = shifted(total, self.axis, 2 * self.sign)
        return beside

    def first_hop(self, *beside):
        self.window, *beside = lax.optimization_barrier((self.got,) + beside)
        self.window_decay = shifted(self.decay, self.axis, 2 * self.sign)
        self.tail = self.decay * self.window + self.total
        self.tail_decay = self.decay * self.window_decay
        return beside

    def last_hops(self, *beside):
        hop = 2
        while hop < self.chips:
            got = shifted(self.tail, self.axis, 2 * self.sign * hop)
            if hop == 2:
                got, *beside = lax.optimization_barrier((got,) + beside)
            got_decay = shifted(self.tail_decay, self.axis, 2 * self.sign * hop)
            self.window = self.window_decay * got + self.window
            self.window_decay = self.window_decay * got_decay
            hop *= 2
            if hop < self.chips:
                self.tail = self.tail_decay * got + self.tail
                self.tail_decay = self.tail_decay * got_decay
        self.whole = flip(self.window, self.axis, 1)
        return beside

    def result(self, *beside):
        self.whole, *beside = lax.optimization_barrier((self.whole,) + beside)
        both = jnp.where(
            self.odd == 0,
            jnp.concatenate([self.window, self.whole], axis=2),
            jnp.concatenate([self.whole, self.window], axis=2),
        )
        state = jnp.where(self.late, lanes_of(self.partner_logs) * both + self.partner, both)
        return [state] + beside


def on_device(
    hidden_in,
    lengths,
    w_in,
    conv_w,
    conv_b,
    g_norm,
    g_gate,
    w_out,
    a_log,
    dt_bias,
    d_skip,
    out_cotangent,
):
    axes = ("dp", "seq")
    devices = lax.axis_size("dp") * lax.axis_size("seq")
    slots, tokens, _ = hidden_in.shape
    blocks = tokens // T
    rows = slots * tokens
    grid = (slots, blocks)
    share = D // devices

    small = jnp.concatenate(
        [conv_w.reshape(-1), conv_b, g_norm, g_gate], axis=0
    )
    per_row = -(-small.shape[0] // share)
    small = jnp.pad(small, (0, per_row * share - small.shape[0])).reshape(share, per_row)
    wide = CONV_CH + LANES
    front = jnp.pad(w_in[:, DI:], ((0, 0), (0, LANES - HEADS)))
    earlier = shifted(hidden_in[:, tokens - 8 :, :], "seq", 1)
    front_full = gather(jnp.concatenate([front, small], axis=1))
    extra = front_full[:, wide:].reshape(devices, -1)
    lane = CONV_CH // devices
    taps_full = jnp.moveaxis(extra[:, : CONV * lane].reshape(devices, CONV, lane), 0, 1)
    taps_full = taps_full.reshape(CONV, CONV_CH).astype(F32)
    at = CONV * lane
    bias_full = extra[:, at : at + lane].reshape(1, CONV_CH).astype(F32)
    at += lane
    norm_gain = extra[:, at : at + share].reshape(D).astype(F32)
    at += share
    gate_gain = extra[:, at : at + DI // devices].reshape(1, DI).astype(F32)
    back = jnp.concatenate([w_in[:, :DI], w_out.T], axis=1)
    back = lax.all_gather(back, axes, axis=0, tiled=True)

    taps_rows = jnp.concatenate([taps_full, bias_full, jnp.zeros((3, CONV_CH), F32)], axis=0)
    rate = -jnp.exp(a_log)
    heads_rows = jnp.pad(jnp.stack([dt_bias, rate, d_skip]), ((0, 5), (0, LANES - HEADS)))
    skip_row = jnp.repeat(d_skip, HEADDIM)[None]
    gain_rows = jnp.concatenate([gate_gain, skip_row, jnp.zeros((6, DI), F32)], axis=0)
    select = (
        jnp.arange(DI, dtype=jnp.int32)[:, None] // HEADDIM
        == jnp.arange(LANES, dtype=jnp.int32)[None]
    ).astype(BF16)

    place = lax.axis_index("seq") * tokens + jnp.arange(tokens, dtype=jnp.int32)
    keep = (place[None, :] < lengths[:, None]).astype(F32)
    residual = hidden_in.astype(F32)

    def tile(width, dtype=F32, flip_order=False, height=T):
        if flip_order:
            spec = pl.BlockSpec((1, height, width), lambda s, c: (s, blocks - 1 - c, 0))
        else:
            spec = pl.BlockSpec((1, height, width), lambda s, c: (s, c, 0))
        return spec, jax.ShapeDtypeStruct((slots, tokens, width), dtype)

    def per_block(height, width, flip_order=False):
        if flip_order:
            spec = pl.BlockSpec((1, 1, height, width), lambda s, c: (s, blocks - 1 - c, 0, 0))
        else:
            spec = pl.BlockSpec((1, 1, height, width), lambda s, c: (s, c, 0, 0))
        return spec, jax.ShapeDtypeStruct((slots, blocks, height, width), F32)

    def columns(width, whole, index):
        spec = pl.BlockSpec((1, T, width), lambda s, c: (s, blocks - 1 - c, index))
        return spec, jax.ShapeDtypeStruct((slots, tokens, whole), F32)

    def per_slot(height, width, dtype=F32):
        spec = pl.BlockSpec((1, height, width), lambda s, c: (s, 0, 0))
        return spec, jax.ShapeDtypeStruct((slots, height, width), dtype)

    def fixed(height, width):
        spec = pl.BlockSpec((height, width), lambda s, c: (0, 0))
        return spec, jax.ShapeDtypeStruct((height, width), F32)

    def specs(*pairs):
        return [spec for spec, _ in pairs]

    normed, conv_in, halo, step_raw, x, bc, log, step, aux, enter, final, total = call(
        states_kernel,
        grid,
        specs(
            tile(D), per_slot(8, D), fixed(D, wide), fixed(1, D), fixed(8, CONV_CH), fixed(8, LANES)
        ),
        [
            tile(D, BF16), tile(CONV_CH, BF16), per_slot(8, CONV_CH, BF16), tile(LANES), tile(DI),
            tile(2 * STATE), tile(LANES), tile(LANES), per_block(8, LANES), per_block(STATE, DI),
            per_slot(STATE, DI), per_slot(8, LANES),
        ],
        [
            pltpu.VMEM((CONV_CH // LANES, T + 8, LANES), F32), pltpu.VMEM((STATE, DI), F32),
            pltpu.VMEM((8, LANES), F32),
        ],
        6 * rows * STATE * DI + 2 * rows * D * wide,
        rows * (CONV_CH * 6 + DI * 4),
    )(hidden_in, earlier, front_full, norm_gain[None], taps_rows, heads_rows)
    normed = normed.reshape(rows, D)
    logs = total[:, 0, :]
    forward = Entering(final, logs, "seq", False)
    forward.chip_total()
    back = after(back, forward.total)
    w_gate, w_out_turned = lax.optimization_barrier((back[:, :DI], back[:, DI:]))
    gate_pre = jnp.dot(normed, w_gate, preferred_element_type=F32).reshape(slots, tokens, DI)
    cotangent = out_cotangent.astype(F32)
    branch_grad = (cotangent * keep[..., None]).astype(BF16).reshape(rows, D)
    norm_grad = jnp.dot(
        after(branch_grad, forward.total), w_out_turned, preferred_element_type=F32
    )
    normed_turned = after(normed, forward.total).T
    norm_grad, gate_pre, normed_turned = forward.first_hop(
        norm_grad.reshape(slots, tokens, DI), gate_pre, normed_turned
    )
    (local,) = call(
        local_kernel,
        grid,
        specs(
            tile(DI), tile(2 * STATE), tile(LANES), tile(LANES), per_block(STATE, DI), fixed(8, DI)
        ),
        [tile(DI)],
        [],
        12 * rows * T * DI,
        rows * (CONV_CH + 2 * DI) * 4,
    )(after(x, forward.tail), bc, log, step, enter, gain_rows)
    (local,) = forward.last_hops(local)
    (start,) = forward.result()

    gated_norm, mixed_grad, gate_grad, lg, adj_enter, adj_final, gate_sums = call(
        gate_kernel,
        grid,
        specs(
            columns(STATE, 2 * STATE, 1), tile(LANES, flip_order=True),
            per_block(8, LANES, True), tile(DI, flip_order=True), tile(DI, flip_order=True),
            tile(DI, flip_order=True), per_slot(STATE, DI), fixed(8, DI), fixed(DI, LANES),
        ),
        [
            tile(DI, BF16, True), tile(DI, F32, True), tile(DI, BF16, True),
            tile(LANES, F32, True), per_block(STATE, DI, True), per_slot(STATE, DI), fixed(8, DI),
        ],
        [
            pltpu.VMEM((T, DI), F32), pltpu.VMEM((T, DI), F32), pltpu.VMEM((T, DI), F32),
            pltpu.VMEM((STATE, DI), F32),
            pltpu.VMEM((T, DI), BF16), pltpu.VMEM((T, DI), BF16),
        ],
        12 * rows * STATE * DI,
        rows * (CONV_CH * 4 + DI * 24),
    )(bc, log, aux, local, gate_pre, norm_grad, start, gain_rows, select)
    gated_norm = gated_norm.reshape(rows, DI)
    gate_grad = gate_grad.reshape(rows, DI)
    backward = Entering(adj_final, logs, "seq", True)

    w_out_grad = lax.dot_general(
        branch_grad, gated_norm, (((0,), (0,)), ((), ())), preferred_element_type=F32
    )
    (w_out_grad,) = backward.chip_total(w_out_grad)
    w_gate_grad = lax.dot_general(
        normed_turned, after(gate_grad, backward.total), NN, preferred_element_type=F32
    )
    branch = lax.dot_general(
        after(gated_norm, backward.total), w_out_turned, NT, preferred_element_type=F32
    )
    block_out = (residual + keep[..., None] * branch.reshape(slots, tokens, D)).astype(BF16)
    early = jnp.concatenate([w_gate_grad, w_out_grad], axis=1)
    early, block_out = backward.first_hop(early, block_out)
    early = lax.psum_scatter(early, axes, scatter_dimension=0, tiled=True)

    xadj, bc_grad, skipped = call(
        adjoint_kernel,
        grid,
        specs(
            tile(DI), tile(2 * STATE), tile(LANES), tile(LANES), per_block(8, LANES), tile(DI),
            per_block(STATE, DI), per_slot(STATE, DI), per_block(STATE, DI), fixed(DI, LANES),
        ),
        [tile(DI), tile(2 * STATE), tile(LANES)],
        [pltpu.VMEM((height, DI), BF16) for height in (T, T, T, STATE, 2 * T, 2 * STATE)],
        30 * rows * T * DI,
        rows * (CONV_CH + 4 * DI) * 4,
    )(
        x, bc, log, step, aux, after(mixed_grad, backward.tail), enter, start, adj_enter, select
    )
    (xadj,) = backward.last_hops(xadj)
    (end_adj,) = backward.result()

    prev = pl.BlockSpec(
        (1, 16, CONV_CH), lambda s, c: (s, jnp.maximum((blocks - 1 - c) * (T // 16) - 1, 0), 0)
    )
    def flipped(width, dtype=F32):
        return tile(width, dtype, True)

    slices = CONV_CH // LANES
    proj_grad, head_rows, last_rows, conv_sums, head_sums = call(
        finish_kernel,
        grid,
        specs(
            flipped(DI), flipped(2 * STATE), flipped(LANES), flipped(LANES),
            per_block(8, LANES, True), per_slot(8, LANES), flipped(DI), flipped(DI),
            flipped(2 * STATE), flipped(LANES), flipped(LANES), per_slot(STATE, DI),
            per_slot(STATE, DI), per_slot(STATE, DI), flipped(CONV_CH), (prev, None),
            per_slot(8, CONV_CH), flipped(LANES), fixed(8, CONV_CH), fixed(8, LANES), fixed(8, DI),
            fixed(DI, LANES),
        ),
        [
            flipped(wide, BF16), per_slot(8, CONV_CH), per_slot(8, CONV_CH), fixed(40, CONV_CH),
            fixed(24, LANES),
        ],
        [
            pltpu.VMEM((slices, T + 16, LANES), F32), pltpu.VMEM((slices, T + 8, LANES), F32),
            pltpu.VMEM((8, CONV_CH), F32), pltpu.VMEM((T, DI), BF16), pltpu.VMEM((T, DI), BF16),
            pltpu.VMEM((8, LANES), F32),
        ],
        12 * rows * STATE * DI,
        rows * (CONV_CH * 8 + DI * 8),
    )(
        x, bc, log, step, aux, total, mixed_grad, xadj, bc_grad, lg, skipped, end_adj, start,
        final, conv_in, conv_in, halo, step_raw, taps_rows, heads_rows, gain_rows, select,
    )

    ahead = shifted(head_rows, "seq", -1)
    ahead = jnp.concatenate([jnp.zeros((slots, 8, CONV_CH), F32), ahead], axis=1)
    for tap in range(CONV):
        begin = CONV - 1 - tap
        last_rows = last_rows + ahead[:, begin : begin + 8] * taps_full[tap]
    proj_grad = lax.dynamic_update_slice(
        proj_grad, last_rows.astype(BF16), (0, tokens - 8, 0)
    ).reshape(rows, wide)

    w_front_grad = jnp.dot(normed_turned, proj_grad, preferred_element_type=F32)
    scatter = ScatterSum(w_front_grad, axes)
    tall = min(2 * T, rows // 2)

    strips = rows // tall // 2

    def input_half(half, sent, *done):
        def strip(width, dtype=BF16):
            spec = pl.BlockSpec((tall, width), lambda r: (r + half * strips, 0))
            return spec, jax.ShapeDtypeStruct((rows, width), dtype)

        def whole(height, width):
            spec = pl.BlockSpec((height, width), lambda r: (0, 0))
            return spec, jax.ShapeDtypeStruct((height, width), F32)

        ins = [
            strip(wide), strip(DI), whole(D, wide), whole(D, DI), strip(D), strip(D), whole(1, D)
        ]
        return call(
            input_kernel,
            (strips,),
            specs(*ins) + [pl.BlockSpec(memory_space=pl.ANY)] * len(done),
            [strip(D, F32), whole(8, D)],
            [],
            rows * D * (wide + DI),
            (rows * (wide + DI) * 2 + rows * D * 8) // 2,
            {len(ins): 0} if done else None,
        )(
            after(proj_grad, *sent), gate_grad, front_full, w_gate, hidden_in.reshape(rows, D),
            out_cotangent.reshape(rows, D), norm_gain[None], *done,
        )

    input_grad, norm_sums = input_half(0, scatter.begin())
    sent, (input_grad, norm_sums, early) = scatter.second(input_grad, norm_sums, early)
    w_gate_owned, w_out_owned = early[:, :DI], early[:, DI:]
    input_grad, more_sums = input_half(1, sent, input_grad)
    front_owned, sent, (input_grad, norm_sums) = scatter.finish(input_grad, norm_sums + more_sums)
    input_grad = input_grad.reshape(slots, tokens, D)

    vectors = jnp.concatenate(
        [
            conv_sums.reshape(CONV + 1, 8, CONV_CH).sum(1).reshape(-1), norm_sums.sum(0),
            gate_sums.sum(0), head_sums.reshape(3, 8, LANES).sum(1).reshape(-1),
        ]
    )
    vectors = total_sum(vectors.reshape(-1, LANES), sent).reshape(-1)
    me = lax.axis_index("dp") * lax.axis_size("seq") + lax.axis_index("seq")

    def owned(begin, length):
        per = length // devices
        return lax.dynamic_slice_in_dim(vectors, begin + me * per, per)

    norm_at = (CONV + 1) * CONV_CH
    gate_at = norm_at + D
    heads_at = gate_at + DI
    return (
        block_out,
        input_grad,
        jnp.concatenate([w_gate_owned, front_owned[:, : CONV_CH + HEADS]], axis=1),
        jnp.stack([owned(k * CONV_CH, CONV_CH) for k in range(CONV)]),
        owned(CONV * CONV_CH, CONV_CH),
        owned(norm_at, D),
        owned(gate_at, DI),
        w_out_owned.T,
        vectors[heads_at : heads_at + HEADS],
        vectors[heads_at + LANES : heads_at + LANES + HEADS],
        vectors[heads_at + 2 * LANES : heads_at + 2 * LANES + HEADS],
    )


def solution(mesh):
    placed = (
        P("dp", "seq", None),
        P("dp"),
        P(("dp", "seq"), None),
        P(None, ("dp", "seq")),
        P(("dp", "seq")),
        P(("dp", "seq")),
        P(("dp", "seq")),
        P(None, ("dp", "seq")),
        P(),
        P(),
        P(),
        P("dp", "seq", None),
    )
    return jax.shard_map(
        on_device,
        mesh=mesh,
        in_specs=placed,
        out_specs=(
            P("dp", "seq", None),
            P("dp", "seq", None),
            P(("dp", "seq"), None),
            P(None, ("dp", "seq")),
            P(("dp", "seq")),
            P(("dp", "seq")),
            P(("dp", "seq")),
            P(None, ("dp", "seq")),
            P(),
            P(),
            P(),
        ),
        check_vma=False,
    )
```
